32 devices in a mesh: dp: 8 (over z, x), tp: 4 (over y, core).
Axes of the slice: x: 2, y: 2, z: 4, core: 2. Of those that a mesh axis runs over, the one named last changes fastest.
Arguments:
- inputs: bfloat16 [4096, 768], P('dp'), may hold values from -6 to 6
- cotangent: bfloat16 [4096, 768], P('dp'), may hold values from -6 to 6
- seg_lengths: int32 [8, 4], P('dp'), may hold values from 1 to 256, 512 in all within a row
- bucket_ids: int32 [1023], replicated, may hold values from 0 to 31
- qkv_weight: float32 [3, 768, 768], P(None, 'dp', 'tp'), may hold values from -0.0625 to 0.0625
- qkv_first: float32 [3, 768, 768], P(None, 'dp', 'tp'), may hold values from -0.0009765625 to 0.0009765625
- qkv_second: float32 [3, 768, 768], P(None, 'dp', 'tp'), may hold values from 3.598771e-10 to 1.4280838e-09
- out_weight: float32 [768, 768], P('dp', 'tp'), may hold values from -3 to 3
- out_first: float32 [768, 768], P('dp', 'tp'), may hold values from -2.2888184e-05 to 2.2888184e-05
- out_second: float32 [768, 768], P('dp', 'tp'), may hold values from 1.8279472e-13 to 7.426035e-13
- ffn_in_weight: float32 [768, 3072], P('dp', 'tp'), may hold values from -0.21875 to 0.21875
- ffn_in_first: float32 [768, 3072], P('dp', 'tp'), may hold values from -0.00012207031 to 0.00012207031
- ffn_in_second: float32 [768, 3072], P('dp', 'tp'), may hold values from 6.854802e-12 to 2.7990442e-11
- ffn_down_weight: float32 [768, 3072], P('dp', 'tp'), may hold values from -0.109375 to 0.109375
- ffn_down_first: float32 [768, 3072], P('dp', 'tp'), may hold values from -0.00024414062 to 0.00024414062
- ffn_down_second: float32 [768, 3072], P('dp', 'tp'), may hold values from 2.8561674e-11 to 1.14246695e-10
- norm_gains: float32 [2, 768], replicated, may hold values from 0.5 to 1.5
- gains_first: float32 [2, 768], replicated, may hold values from -0.0004272461 to 0.0004272461
- gains_second: float32 [2, 768], replicated, may hold values from 6.854802e-11 to 2.7419209e-10
- bias_table: float32 [32, 12], P(None, 'tp'), may hold values from -4 to 4
- table_first: float32 [32, 12], P(None, 'tp'), may hold values from -0.00048828125 to 0.00048828125
- table_second: float32 [32, 12], P(None, 'tp'), may hold values from 7.997269e-11 to 3.3131542e-10
Outputs:
- block_out: bfloat16 [4096, 768], P(('dp', 'tp'))
- input_grad: float32 [4096, 768], P(('dp', 'tp'))
- grad_norm: float32 [], replicated
- qkv_new: float32 [3, 768, 768], P(None, 'dp', 'tp')
- qkv_first_new: float32 [3, 768, 768], P(None, 'dp', 'tp')
- qkv_second_new: float32 [3, 768, 768], P(None, 'dp', 'tp')
- qkv_low: bfloat16 [3, 768, 768], P(None, 'dp', 'tp')
- out_new: float32 [768, 768], P('dp', 'tp')
- out_first_new: float32 [768, 768], P('dp', 'tp')
- out_second_new: float32 [768, 768], P('dp', 'tp')
- out_low: bfloat16 [768, 768], P('dp', 'tp')
- ffn_in_new: float32 [768, 3072], P('dp', 'tp')
- ffn_in_first_new: float32 [768, 3072], P('dp', 'tp')
- ffn_in_second_new: float32 [768, 3072], P('dp', 'tp')
- ffn_in_low: bfloat16 [768, 3072], P('dp', 'tp')
- ffn_down_new: float32 [768, 3072], P('dp', 'tp')
- ffn_down_first_new: float32 [768, 3072], P('dp', 'tp')
- ffn_down_second_new: float32 [768, 3072], P('dp', 'tp')
- ffn_down_low: bfloat16 [768, 3072], P('dp', 'tp')
- gains_new: float32 [2, 768], replicated
- gains_first_new: float32 [2, 768], replicated
- gains_second_new: float32 [2, 768], replicated
- gains_grad: float32 [2, 768], replicated
- table_new: float32 [32, 12], P(None, 'tp')
- table_first_new: float32 [32, 12], P(None, 'tp')
- table_second_new: float32 [32, 12], P(None, 'tp')
The draws below stay inside these ranges and needn't reach their ends.
Inputs may be any that keep to these rules, and one draw needn't show every extreme that they name: `seg_lengths`: each packed row's 4 lengths sum to 512, and one of them is exactly 256.
All inputs are finite; a program needn't handle non-finite values.
Results may differ from the reference program's by a relative error of at most 0.014.
Values may be sent and summed in bfloat16 or wider, within the bound.
No kernel may reach another device: no remote copies, remote signals or barrier semaphores. Data moves between devices by JAX's collectives and lax.ppermute only.
A program may use at most 320 MiB of HBM per device.

```python
import math
import jax
import jax.numpy as jnp
import numpy as np
from jax import lax

D = 768
HEADS = 12
HDIM = 64
FF = 3072
BUCKETS = 32
LEN = 512
SEGS = 4
SEGMAX = 256
ROWS = 8
TOKENS = 4096


def plant(drawn, rng, least, top_value):
    extent = drawn.shape
    index_at = [jax.random.randint(jax.random.fold_in(rng, axis), (), 0, extent[axis]) for axis in range(len(extent))]
    drawn = drawn.at[tuple(index_at)].set(least)
    longest = extent.index(max(extent))
    index_at[longest] = (index_at[longest] + 1) % extent[longest]
    return drawn.at[tuple(index_at)].set(top_value)


def with_spikes(array, key, source, target, blocks, factor):
    owner, partner = [(jnp.arange(array.shape[axis_at]) // (array.shape[axis_at] // blocks)).reshape([-1 if axis == axis_at else 1 for axis in range(array.ndim)]) for axis_at in (source, target)]
    chosen = jax.random.permutation(key, blocks)[partner]
    strong = (owner == chosen) | (owner == (partner + blocks // 2) % blocks)
    return jnp.where(strong, factor * array, array)


def steps_of(rng, extent, shards, low, high):
    factor_of, own = 1.0, jax.random.fold_in(rng, 6)
    for axis_at, shards_of in shards:
        steps = jnp.exp(jax.random.uniform(jax.random.fold_in(own, axis_at), (shards_of,), jnp.float32, low / len(shards), high / len(shards)))
        factor_of = factor_of * jnp.repeat(steps, extent[axis_at] // shards_of).reshape([-1 if axis == axis_at else 1 for axis in range(len(extent))])
    return factor_of


def profile(number_of, total, limit, skew):
    weights = [(1 << 20) // math.isqrt(grade ** skew) + 1 for grade in range(2, number_of + 1)]
    surplus, holding = total - limit - (number_of - 1), [1] * (number_of - 1)
    while surplus > 0:
        movable = [i for i in range(number_of - 1) if holding[i] < limit]
        pool, remaining = sum([weights[i] for i in movable]), surplus
        for i in movable:
            addition = min(limit - holding[i], max(1, remaining * weights[i] // pool), surplus)
            holding[i] = holding[i] + addition
            surplus = surplus - addition
    return np.array([limit] + holding)


def uneven(rng, count, total, reach, lean):
    if count == 2:
        one = jax.random.randint(rng, (), max(1, total - reach), min(reach, total - 1) + 1)
        return jnp.stack([one, total - one])
    sizes = jnp.asarray(profile(count, total, reach, lean), jnp.int32)
    couples = (count - 1) // 2
    giver, taker = sizes[1:1 + 2 * couples:2], sizes[2:2 + 2 * couples:2]
    room = jnp.minimum(giver - 1, reach - taker)
    passed = jax.random.randint(jax.random.fold_in(rng, 1), (couples,), 0, 1 << 20) % (room + 1)
    sizes = sizes.at[1:1 + 2 * couples:2].set(giver - passed).at[2:2 + 2 * couples:2].set(taker + passed)
    return sizes[jax.random.permutation(jax.random.fold_in(rng, 2), count)]


def gaussian(own_key, dims, spread, reach, pieces=(), held_as=jnp.bfloat16):
    values = spread * jax.random.normal(own_key, dims, jnp.float32)
    if pieces:
        values = values * steps_of(own_key, dims, pieces, -0.22, 0.18)
    return jnp.clip(values, -reach, reach).astype(held_as)


def bell_draw_with(rng, extent, deviation, most, cuts, heavy, kind=jnp.bfloat16):
    drawn = deviation * jax.random.normal(rng, extent, jnp.float32)
    if cuts:
        drawn = drawn * steps_of(rng, extent, cuts, -0.22, 0.18)
    return jnp.clip(with_spikes(drawn, jax.random.fold_in(rng, 3), *heavy), -most, most).astype(kind)


def setup_inputs(seed: int = 0) -> dict:
    keys = jax.random.split(jax.random.key(seed), 23)
    return {
        "inputs": gaussian(keys[0], (TOKENS, D), 1.0, 6.0, ((0, 8),)),
        "cotangent": bell_draw_with(keys[1], (TOKENS, D), 1.0, 6.0, ((0, 8),), (0, 1, 8, 2.0)),
        "seg_lengths": jax.vmap(lambda own: uneven(own, SEGS, LEN, SEGMAX, 2))(jax.random.split(keys[2], ROWS)).reshape((ROWS, SEGS)).astype(jnp.int32),
        "bucket_ids": plant(jax.random.randint(keys[3], (2 * LEN - 1,), 0, BUCKETS), jax.random.fold_in(keys[3], 1), 0, BUCKETS - 1).astype(jnp.int32),
        "qkv_weight": gaussian(keys[4], (3, D, D), (12 * D) ** -0.5, 0.0625, ((1, 8), (2, 4)), jnp.float32),
        "qkv_first": gaussian(keys[5], (3, D, D), (0.28 / (27.2 * D * D + 0.62 * D * FF) ** 0.5), 0.0009765625, ((1, 8), (2, 4)), jnp.float32),
        "qkv_second": jnp.clip(jnp.exp(math.log(1.428083762355925e-09) - 1.3783262 * jax.random.uniform(keys[6], (3, D, D), jnp.float32) ** steps_of(keys[6], (3, D, D), ((1, 8), (2, 4)), -0.2, 0.2)), 3.5987710034213194e-10, 1.428083762355925e-09),
        "out_weight": gaussian(keys[7], (D, D), (max(D // 192, 1)) ** -0.5, 3.0, ((0, 8), (1, 4)), jnp.float32),
        "out_first": gaussian(keys[8], (D, D), (0.0063 / (27.2 * D * D + 0.62 * D * FF) ** 0.5), 2.288818359375e-05, ((0, 8), (1, 4)), jnp.float32),
        "out_second": jnp.clip(jnp.exp(math.log(7.426035155723432e-13) - 1.4017985 * jax.random.uniform(keys[9], (D, D), jnp.float32) ** steps_of(keys[9], (D, D), ((0, 8), (1, 4)), -0.2, 0.2)), 1.8279472445252576e-13, 7.426035155723432e-13),
        "ffn_in_weight": gaussian(keys[10], (D, FF), D ** -0.5, 0.21875, ((0, 8), (1, 4)), jnp.float32),
        "ffn_in_first": gaussian(keys[11], (D, FF), (0.039 / (27.2 * D * D + 0.62 * D * FF) ** 0.5), 0.00012207031, ((0, 8), (1, 4)), jnp.float32),
        "ffn_in_second": jnp.clip(jnp.exp(math.log(2.799044156176489e-11) - 1.40691367 * jax.random.uniform(keys[12], (D, FF), jnp.float32) ** steps_of(keys[12], (D, FF), ((0, 8), (1, 4)), -0.2, 0.2)), 6.854801882366646e-12, 2.799044156176489e-11),
        "ffn_down_weight": gaussian(keys[13], (D, FF), FF ** -0.5, 0.109375, ((0, 8), (1, 4)), jnp.float32),
        "ffn_down_first": gaussian(keys[14], (D, FF), (0.079 / (27.2 * D * D + 0.62 * D * FF) ** 0.5), 0.00024414062, ((0, 8), (1, 4)), jnp.float32),
        "ffn_down_second": jnp.clip(jnp.exp(math.log(1.1424669543735888e-10) - 1.3862944 * jax.random.uniform(keys[15], (D, FF), jnp.float32) ** steps_of(keys[15], (D, FF), ((0, 8), (1, 4)), -0.2, 0.2)), 2.856167385933972e-11, 1.1424669543735888e-10),
        "norm_gains": jnp.clip(1.0 + 0.1 * jax.random.normal(keys[16], (2, D), jnp.float32), 0.5, 1.5),
        "gains_first": gaussian(keys[17], (2, D), (0.12 / (27.2 * D * D + 0.62 * D * FF) ** 0.5), 0.0004272461, (), jnp.float32),
        "gains_second": jnp.clip(jnp.exp(jax.random.uniform(keys[18], (2, D), jnp.float32, math.log(6.854802142575167e-11), math.log(2.741920857030067e-10))), 6.854802142575167e-11, 2.741920857030067e-10),
        "bias_table": gaussian(keys[19], (BUCKETS, HEADS), 1.0, 4.0, ((1, 4),), jnp.float32),
        "table_first": gaussian(keys[20], (BUCKETS, HEADS), (0.133 / (27.2 * D * D + 0.62 * D * FF) ** 0.5), 0.00048828125, ((1, 4),), jnp.float32),
        "table_second": jnp.clip(jnp.exp(math.log(3.313154195438983e-10) - 1.4213857 * jax.random.uniform(keys[21], (BUCKETS, HEADS), jnp.float32) ** steps_of(keys[21], (BUCKETS, HEADS), ((1, 4),), -0.2, 0.2)), 7.997268819393e-11, 3.313154195438983e-10),
    }


eps_norm = 1e-06
clip_norm = 1.0
beta_one = 0.9
beta_two = 0.999
adam_eps = 1e-08
decay_rate = 0.01
adam_step = 10.0
mask_fill = -1000000000.0
rate_small = 0.02
rate_large = 0.5

@jax.custom_vjp
def low(v):
    return lax.optimization_barrier(v.astype(jnp.bfloat16)).astype(jnp.float32)

@jax.custom_vjp
def low_back(v):
    return v

def low_keep(v):
    return (low(v), None)

def low_pass(kept, grad):
    return (grad,)

def back_keep(v):
    return (v, None)

def back_low(kept, grad):
    return (low(grad),)
low.defvjp(low_keep, low_pass)
low_back.defvjp(back_keep, back_low)

def segment_ids(seg_lengths):
    ends = jnp.cumsum(seg_lengths, axis=1, dtype=jnp.int32)
    position = jnp.arange(LEN, dtype=jnp.int32)
    return lax.optimization_barrier(jnp.sum((position[None, :, None] >= ends[:, None, :-1]).astype(jnp.int32), axis=2))

def rms_norm(values, gain):
    scale = lax.rsqrt(lax.optimization_barrier(jnp.mean(values * values, axis=-1, keepdims=True)) + eps_norm)
    return values * scale * gain

def forward(params, inputs, segment, bucket_of):
    qkv_weight, out_weight, ffn_in_weight, ffn_down_weight, norm_gains, bias_table = params
    highest = lax.Precision.HIGHEST
    act_one = low(rms_norm(inputs, norm_gains[0]))
    projected = jnp.einsum('td,cde->cte', act_one, low(qkv_weight), precision=highest)
    projected = low(low_back(projected))
    group_size = math.gcd(ROWS, 8)
    grouped = projected.reshape(3, ROWS // group_size, group_size, LEN, HEADS, HDIM)
    seg_groups = segment.reshape(ROWS // group_size, group_size, LEN)
    bias_full = jnp.transpose(bias_table[bucket_of], (2, 0, 1))

    def attend(block_rows):
        query_rows, key_rows, value_rows, seg_rows = block_rows
        raw_scores = jnp.einsum('gihd,gjhd->ghij', query_rows, key_rows, precision=highest)
        logits = low_back(raw_scores) + bias_full[None]
        visible = seg_rows[:, None, :, None] == seg_rows[:, None, None, :]
        logits = jnp.where(visible, logits, mask_fill)
        attn_prob = low(jax.nn.softmax(logits, axis=-1))
        mixed_rows = jnp.einsum('ghij,gjhd->gihd', attn_prob, value_rows, precision=highest)
        return low(low_back(mixed_rows))
    mixed_all = lax.map(jax.checkpoint(attend), (grouped[0], grouped[1], grouped[2], seg_groups))
    mixed_all = mixed_all.reshape(TOKENS, D)
    attn_out = low_back(jnp.dot(mixed_all, low(out_weight).T, precision=highest, preferred_element_type=jnp.float32))
    resid_one = inputs + attn_out
    act_two = low(rms_norm(resid_one, norm_gains[1]))
    hidden_pre = low_back(jnp.dot(act_two, low(ffn_in_weight), precision=highest, preferred_element_type=jnp.float32))
    hidden_act = low(jax.nn.gelu(hidden_pre, approximate=True))
    ffn_out = low_back(jnp.dot(hidden_act, low(ffn_down_weight).T, precision=highest, preferred_element_type=jnp.float32))
    return resid_one + ffn_out

def adamw_update(weight, gradient, moment_one, moment_two, rate):
    one_new = beta_one * moment_one + (1.0 - beta_one) * gradient
    two_new = beta_two * moment_two + (1.0 - beta_two) * gradient * gradient
    one_hat = one_new / (1.0 - beta_one ** adam_step)
    two_hat = two_new / (1.0 - beta_two ** adam_step)
    weight_new = weight - rate * (one_hat / (jnp.sqrt(two_hat) + adam_eps) + decay_rate * weight)
    return (weight_new, one_new, two_new)

def reference(inputs, cotangent, seg_lengths, bucket_ids, qkv_weight, qkv_first, qkv_second, out_weight, out_first, out_second, ffn_in_weight, ffn_in_first, ffn_in_second, ffn_down_weight, ffn_down_first, ffn_down_second, norm_gains, gains_first, gains_second, bias_table, table_first, table_second):
    segment = segment_ids(seg_lengths)
    position = jnp.arange(LEN, dtype=jnp.int32)
    offsets = position[None, :] - position[:, None] + (LEN - 1)
    bucket_of = bucket_ids[offsets]
    params = (qkv_weight, out_weight, ffn_in_weight, ffn_down_weight, norm_gains, bias_table)

    def run(params_now, inputs_now):
        return forward(params_now, inputs_now, segment, bucket_of)
    block_f32, pullback = jax.vjp(run, params, inputs.astype(jnp.float32))
    grads, input_grad = pullback(cotangent.astype(jnp.float32))
    total_squares = sum((jnp.sum(gradient * gradient) for gradient in grads))
    grad_norm = jnp.sqrt(total_squares)
    factor = clip_norm / jnp.maximum(grad_norm, clip_norm)
    qkv_grad, out_grad, in_grad, down_grad, gains_raw, table_grad = [gradient * factor for gradient in grads]
    qkv_new, qkv_first_new, qkv_second_new = adamw_update(qkv_weight, qkv_grad, qkv_first, qkv_second, rate_small)
    out_new, out_first_new, out_second_new = adamw_update(out_weight, out_grad, out_first, out_second, rate_large)
    ffn_in_new, ffn_in_first_new, ffn_in_second_new = adamw_update(ffn_in_weight, in_grad, ffn_in_first, ffn_in_second, rate_small)
    ffn_down_new, ffn_down_first_new, ffn_down_second_new = adamw_update(ffn_down_weight, down_grad, ffn_down_first, ffn_down_second, rate_small)
    gains_new, gains_first_new, gains_second_new = adamw_update(norm_gains, gains_raw, gains_first, gains_second, rate_large)
    table_new, table_first_new, table_second_new = adamw_update(bias_table, table_grad, table_first, table_second, rate_large)
    return (block_f32.astype(jnp.bfloat16), input_grad, grad_norm, qkv_new, qkv_first_new, qkv_second_new, qkv_new.astype(jnp.bfloat16), out_new, out_first_new, out_second_new, out_new.astype(jnp.bfloat16), ffn_in_new, ffn_in_first_new, ffn_in_second_new, ffn_in_new.astype(jnp.bfloat16), ffn_down_new, ffn_down_first_new, ffn_down_second_new, ffn_down_new.astype(jnp.bfloat16), gains_new, gains_first_new, gains_second_new, gains_raw, table_new, table_first_new, table_second_new)
```

```python
import functools
import math

import jax
import jax.numpy as jnp
from jax import lax
from jax.experimental import pallas as pl
from jax.experimental.pallas import tpu as pltpu
from jax.sharding import PartitionSpec as P

HEADS = 12
HDIM = 64
BUCKETS = 32
LEN = 512
BLK = 128
WIN = LEN + BLK


eps_norm = 1e-06
clip_norm = 1.0
beta_one = 0.9
beta_two = 0.999
adam_eps = 1e-08
decay_rate = 0.01
adam_step = 10.0
mask_fill = -1000000000.0
rate_small = 0.02
rate_large = 0.5
gelu_coef = 0.044715
root_coef = math.sqrt(2.0 / math.pi)

f32 = jnp.float32
bf16 = jnp.bfloat16
sds = jax.ShapeDtypeStruct


def dot_nn(a, b):
    return lax.dot_general(a, b, (((1,), (0,)), ((), ())), preferred_element_type=f32)


def dot_nt(a, b):
    return lax.dot_general(a, b, (((1,), (1,)), ((), ())), preferred_element_type=f32)


def dot_tn(a, b):
    return lax.dot_general(a, b, (((0,), (0,)), ((), ())), preferred_element_type=f32)


def call(body, outs, args, name, flops=0, smem=(), scratch=(), limit=28):
    moved = sum(a.size * a.dtype.itemsize for a in (*args, *outs))
    return pl.pallas_call(
        body,
        out_shape=tuple(outs),
        in_specs=[
            pl.BlockSpec(memory_space=pltpu.SMEM if i in smem else pltpu.VMEM)
            for i in range(len(args))
        ],
        out_specs=tuple(pl.BlockSpec(memory_space=pltpu.VMEM) for _ in outs),
        scratch_shapes=list(scratch),
        compiler_params=pltpu.CompilerParams(vmem_limit_bytes=limit << 20),
        cost_estimate=pl.CostEstimate(flops=flops, bytes_accessed=moved, transcendentals=0),
        name=name,
    )(*args)


def assemble(into, blocks):
    if len(blocks) == 1:
        into[...] = blocks[0][...]
        return
    me = lax.axis_index("dp")
    rows = blocks[0].shape[0]
    for e, block in enumerate(blocks):
        start = pl.multiple_of((me ^ e) * rows, 32)
        into[pl.ds(start, rows), :] = block[...]


def spread(grad, outs):
    if len(outs) == 1:
        outs[0][...] = grad[...].astype(bf16)
        return
    me = lax.axis_index("dp")
    rows = outs[0].shape[1]
    for b, out in enumerate(outs):
        for k in range(out.shape[0]):
            start = pl.multiple_of((me ^ (2 * k + b)) * rows, 32)
            out[k] = grad[pl.ds(start, rows), :].astype(bf16)


def spread_shapes(dp, width, cols):
    if dp == 8:
        return [sds((dp // 2, width // dp, cols), bf16)] * 2
    return [sds((width, cols), bf16)]


def half_rows():
    core = lax.axis_index("tp") & 1
    for half in range(2):
        for at in range(2):
            start = pl.multiple_of(((core ^ half) + 2 * at) * BLK, BLK)
            yield half, at, pl.ds(start, BLK)


def pack_kernel(qkv, out, packed):
    for part in range(3):
        packed[:, part * 192 : part * 192 + 192] = qkv[part].astype(bf16)
    packed[:, 576:768] = out[...].astype(bf16)


def prep_kernel(seg, table, bucket, x, gains, act, act_t, bias):
    values = x[...].astype(f32)
    scale = lax.rsqrt(jnp.mean(values * values, axis=-1, keepdims=True) + eps_norm)
    low = (values * scale * gains[0:1, :]).astype(bf16)
    act[...] = low
    act_t[...] = low.T
    ends = [seg[0, 0]]
    for k in (1, 2):
        ends.append(ends[-1] + seg[0, k])

    def segment_of(position):
        return sum((position >= end).astype(jnp.int32) for end in ends)

    seg_cols = segment_of(lax.broadcasted_iota(jnp.int32, (1, LEN), 1))
    heads = bias.shape[0]
    lines = []
    for h in range(heads):
        line = jnp.zeros((1, 2 * LEN), f32)
        for b in range(BUCKETS):
            line = jnp.where(bucket[...] == b, table[b, h], line)
        lines.append(line)
    for r in range(LEN // BLK):
        seg_rows = segment_of(lax.broadcasted_iota(jnp.int32, (BLK, 1), 0) + r * BLK)
        visible = seg_rows == seg_cols
        low_at = LEN - BLK - r * BLK
        for h in range(heads):
            window = jnp.broadcast_to(lines[h][:, low_at : low_at + WIN], (BLK, WIN))
            turned = pltpu.roll(window, 1, 1, stride=1, stride_axis=0)
            bias[h, r * BLK : (r + 1) * BLK, :] = jnp.where(visible, turned[:, BLK:], mask_fill)


def attend_kernel(n_blocks, act, bias, *rest):
    blocks = rest[:n_blocks]
    weights, qkv, prob, mixed, keep, send = rest[n_blocks:]
    assemble(weights, blocks)
    width = qkv.shape[1] // 3
    qkv[...] = dot_nn(act[...], weights[:, : 3 * width]).astype(bf16)
    for h in range(bias.shape[0]):
        cols = slice(h * HDIM, (h + 1) * HDIM)
        query, key, value = (qkv[:, s * width + h * HDIM : s * width + (h + 1) * HDIM] for s in range(3))
        scores = dot_nt(query, key) + bias[h]
        top = jnp.max(scores, axis=-1, keepdims=True)
        exps = jnp.exp(scores - top)
        total = jnp.sum(exps, axis=-1, keepdims=True)
        low = (exps * (1.0 / total)).astype(bf16)
        prob[h] = low
        mixed[:, cols] = dot_nn(low, value).astype(bf16)
    out_cols = weights[:, 3 * width :]
    for half, at, rows in half_rows():
        to = send if half else keep
        to[at * BLK : (at + 1) * BLK, :] = dot_nt(mixed[rows, :], out_cols).astype(bf16)


def dhid_kernel(n_blocks, dy, *rest):
    blocks = rest[:n_blocks]
    weights, hidden_grad = rest[n_blocks:]
    assemble(weights, blocks)
    hidden_grad[...] = dot_nn(dy[...], weights[...])


def ffn_kernel(n_blocks, x, gains, hidden_grad, own_a, own_b, other_a, other_b, *rest):
    blocks = rest[:n_blocks]
    resid, act, hidden, pre_grad, keep, send, weights = rest[n_blocks:]
    assemble(weights, blocks)
    for half, at, rows in half_rows():
        here = slice(at * BLK, (at + 1) * BLK)
        part_a, part_b = ((own_a, own_b), (other_a, other_b))[half]
        values = x[rows, :].astype(f32) + (part_a[here, :].astype(f32) + part_b[here, :].astype(f32))
        resid[rows, :] = values
        scale = lax.rsqrt(jnp.mean(values * values, axis=-1, keepdims=True) + eps_norm)
        low = (values * scale * gains[1:2, :]).astype(bf16)
        act[rows, :] = low
        u = dot_nn(low, weights[...])
        square = u * u
        tanh_part = jnp.tanh(root_coef * (u + gelu_coef * square * u))
        hidden[rows, :] = (0.5 * u * (1.0 + tanh_part)).astype(bf16)
        inner = root_coef * (1.0 + 3.0 * gelu_coef * square)
        slope = 0.5 * (1.0 + tanh_part) + 0.5 * u * (1.0 - tanh_part * tanh_part) * inner
        du = (hidden_grad[rows, :] * slope).astype(bf16)
        pre_grad[rows, :] = du
        (send if half else keep)[here, :] = dot_nt(du, weights[...]).astype(bf16)


def weight_grad_kernel(left, right, *rest):
    outs, grad = rest[:-1], rest[-1]
    grad[...] = dot_tn(left[...], right[...])
    spread(grad, outs)


def ffn_out_kernel(hidden, weights, keep, send):
    for half, at, rows in half_rows():
        to = send if half else keep
        to[at * BLK : (at + 1) * BLK, :] = dot_nt(hidden[rows, :], weights[...]).astype(bf16)


def attend_back_kernel(
    n_outs, resid, dy, gains, own_a, own_b, other_a, other_b, weights, qkv, prob, mixed, act_t, *rest
):
    outs = rest[:n_outs]
    share_grad, gain_part, score_grad, proj_grad, resid_low, grad = rest[n_outs:]
    chip = lax.axis_index("tp") >> 1
    width = qkv.shape[1] // 3
    for half, at, rows in half_rows():
        here = slice(at * BLK, (at + 1) * BLK)
        part_a, part_b = ((own_a, own_b), (other_a, other_b))[half]
        act_grad = part_a[here, :].astype(f32) + part_b[here, :].astype(f32)
        values = resid[rows, :]
        scale = lax.rsqrt(jnp.mean(values * values, axis=-1, keepdims=True) + eps_norm)
        normed = values * scale
        normal_grad = act_grad * gains[1:2, :]
        mean_part = jnp.mean(normal_grad * normed, axis=-1, keepdims=True)
        total = dy[rows, :].astype(f32) + scale * (normal_grad - normed * mean_part)
        resid_low[rows, :] = total.astype(bf16)
        if half == 0:

            @pl.when(chip == at)
            def _():
                share_grad[...] = total
                gain_part[...] = jnp.sum(act_grad * normed, axis=0, keepdims=True)

    mix_grad = dot_nn(resid_low[...], weights[:, 3 * width :]).astype(bf16)
    for h in range(prob.shape[0]):
        query, key, value = (qkv[:, s * width + h * HDIM : s * width + (h + 1) * HDIM] for s in range(3))
        grad_rows = mix_grad[:, h * HDIM : (h + 1) * HDIM]
        prob_grad = dot_nt(grad_rows, value)
        prob_here = prob[h].astype(f32)
        row_dot = jnp.sum(prob_here * prob_grad, axis=-1, keepdims=True)
        low = (prob_here * (prob_grad - row_dot)).astype(bf16)
        score_grad[h] = low
        for s, part in enumerate((dot_nn(low, key), dot_tn(low, query), dot_tn(prob[h], grad_rows))):
            proj_grad[:, s * width + h * HDIM : s * width + (h + 1) * HDIM] = part.astype(bf16)
    grad[:, : 3 * width] = dot_nn(act_t[...], proj_grad[...])
    grad[:, 3 * width :] = dot_tn(resid_low[...], mixed[...])
    spread(grad, outs)


def tail_kernel(score_grad, proj_grad, weights, bucket, keep, send, table_part, diag):
    width = proj_grad.shape[1]
    for half, at, rows in half_rows():
        to = send if half else keep
        to[at * BLK : (at + 1) * BLK, :] = dot_nt(proj_grad[rows, :], weights[:, :width]).astype(bf16)
    row = lax.broadcasted_iota(jnp.int32, (BLK, BLK), 0)
    col = lax.broadcasted_iota(jnp.int32, (BLK, BLK), 1)
    flip = (row + col == BLK - 1).astype(f32).astype(bf16)
    onehot = lax.broadcasted_iota(jnp.int32, (BUCKETS, 2 * LEN), 0) == bucket[...]
    diag[...] = jnp.zeros_like(diag)
    for h in range(score_grad.shape[0]):
        for r in range(LEN // BLK):
            flipped = dot_nn(flip, score_grad[h, r * BLK : (r + 1) * BLK, :])
            wide = jnp.concatenate([flipped, jnp.zeros((BLK, BLK), f32)], axis=1)
            turned = pltpu.roll(wide, 0, 1, stride=1, stride_axis=0)
            low_at = LEN - BLK - r * BLK
            diag[h : h + 1, low_at : low_at + WIN] += jnp.sum(turned, axis=0, keepdims=True)
        table_part[:, h : h + 1] = jnp.sum(
            jnp.where(onehot, diag[h : h + 1, :], 0.0), axis=1, keepdims=True
        )


def core_add_kernel(keep, got, mine, theirs):
    chip = lax.axis_index("tp") >> 1
    for to, index in ((mine, chip), (theirs, 1 - chip)):
        rows = pl.ds(pl.multiple_of(index * BLK, BLK), BLK)
        to[...] = (keep[rows, :].astype(f32) + got[rows, :].astype(f32)).astype(bf16)


def share_ds():
    return pl.ds(pl.multiple_of(lax.axis_index("tp") * BLK, BLK), BLK)


def block_out_kernel(resid, mine, got, out):
    out[...] = (resid[share_ds(), :] + (mine[...].astype(f32) + got[...].astype(f32))).astype(bf16)


def input_grad_kernel(x, gains, share_grad, mine, got, out, gain_part):
    values = x[share_ds(), :].astype(f32)
    scale = lax.rsqrt(jnp.mean(values * values, axis=-1, keepdims=True) + eps_norm)
    normed = values * scale
    act_grad = mine[...].astype(f32) + got[...].astype(f32)
    normal_grad = act_grad * gains[0:1, :]
    mean_part = jnp.mean(normal_grad * normed, axis=-1, keepdims=True)
    out[...] = share_grad[...] + scale * (normal_grad - normed * mean_part)
    gain_part[...] = jnp.sum(act_grad * normed, axis=0, keepdims=True)


def pair_add_kernel(keep, got, *outs):
    for k, out in enumerate(outs):
        out[...] = (keep[k].astype(f32) + got[k].astype(f32)).astype(bf16)


def fold(values):
    rows, cols = values.shape
    squares = values * values
    lanes = sum(squares[:, c : c + BLK] for c in range(0, cols, BLK))
    return jnp.sum(lanes, axis=0, keepdims=True)


def sum_kernel(n_parts, *rest):
    parts, (grad, squares) = rest[:n_parts], rest[n_parts:]
    total = sum(part[...].astype(f32) for part in parts)
    grad[...] = total
    squares[...] = fold(total)


def last_sum_kernel(n_parts, *rest):
    parts, (extra_a, extra_b, grad, payload) = rest[:n_parts], rest[n_parts:]
    total = sum(part[...].astype(f32) for part in parts)
    grad[...] = total
    squares = fold(total) + extra_a[...] + extra_b[...]
    payload[...] = jnp.broadcast_to(squares[None] * 0.125, payload.shape)


def adamw(weight, gradient, moment_one, moment_two, rate):
    one_new = beta_one * moment_one + (1.0 - beta_one) * gradient
    two_new = beta_two * moment_two + (1.0 - beta_two) * gradient * gradient
    one_hat = one_new / (1.0 - beta_one**adam_step)
    two_hat = two_new / (1.0 - beta_two**adam_step)
    weight_new = weight - rate * (one_hat / (jnp.sqrt(two_hat) + adam_eps) + decay_rate * weight)
    return (weight_new, one_new, two_new)


def adam_kernel(*refs):
    (
        sums,
        gains_sum,
        table_whole,
        table_grad,
        grad_qkvo,
        grad_in,
        grad_down,
        *state,
    ) = refs[:25]
    outs = refs[25:]
    qkv, out, ffn_in, ffn_down, gains, table = (state[i : i + 3] for i in range(0, 18, 3))
    norm_ref, qkv_o, out_o, in_o, down_o, gains_o, gains_grad, table_o = (
        outs[0],
        outs[1:5],
        outs[5:9],
        outs[9:13],
        outs[13:17],
        outs[17:20],
        outs[20],
        outs[21:24],
    )
    squares = (
        jnp.sum(sums[...])
        + jnp.sum(gains_sum[...] * gains_sum[...])
        + jnp.sum(table_whole[...] * table_whole[...])
    )
    norm = jnp.sqrt(jnp.full((1, 1), squares, f32))
    norm_ref[...] = norm
    factor = clip_norm / jnp.maximum(norm, clip_norm)

    def update(state_refs, gradient, to, rate, at=...):
        new = adamw(state_refs[0][at], gradient * factor, state_refs[1][at], state_refs[2][at], rate)
        for ref, value in zip(to, new):
            ref[at] = value
        if len(to) == 4:
            to[3][at] = new[0].astype(bf16)

    width = qkv[0].shape[2]
    for part in range(3):
        update(qkv, grad_qkvo[:, part * width : (part + 1) * width], qkv_o, rate_small, part)
    update(out, grad_qkvo[:, 3 * width :], out_o, rate_large)
    update(ffn_in, grad_in[...], in_o, rate_small)
    update(ffn_down, grad_down[...], down_o, rate_small)
    update(gains, gains_sum[...], gains_o, rate_large)
    gains_grad[...] = gains_sum[...] * factor
    update(table, table_grad[...], table_o, rate_large)


def on_device(
    dp,
    inputs,
    cotangent,
    seg_lengths,
    bucket_ids,
    qkv_weight,
    qkv_first,
    qkv_second,
    out_weight,
    out_first,
    out_second,
    ffn_in_weight,
    ffn_in_first,
    ffn_in_second,
    ffn_down_weight,
    ffn_down_first,
    ffn_down_second,
    norm_gains,
    gains_first,
    gains_second,
    bias_table,
    table_first,
    table_second,
):
    tokens, model = inputs.shape
    rows, local = out_weight.shape
    hidden = ffn_in_weight.shape[1]
    heads_here = local // HDIM
    tp = lax.axis_size("tp")
    packed_cols = 4 * local
    direct = dp == 8

    def swap_dp(value, distance):
        return lax.ppermute(value, "dp", [(i, i ^ distance) for i in range(dp)])

    def swap_tp(value, distance):
        return lax.ppermute(value, "tp", [(i, i ^ distance) for i in range(tp)])

    def gather(block):
        if not direct:
            return [lax.all_gather(block, "dp", axis=0, tiled=True)]
        along = [block] + [swap_dp(block, 2 * k) for k in range(1, dp // 2)]
        return [b for own in along for b in (own, swap_dp(own, 1))]

    def scatter(parts):
        if not direct:
            return [lax.psum_scatter(parts[0].astype(f32), "dp", scatter_dimension=0, tiled=True)]
        keep, send = parts
        outs = [sds(keep.shape[1:], bf16)] * keep.shape[0]
        folded = call(pair_add_kernel, outs, (keep, swap_dp(send, 1)), "pair_add")
        return [folded[0]] + [swap_dp(folded[k], 2 * k) for k in range(1, len(folded))]

    def sum_halves(keep, send):
        first = keep + swap_tp(send, 1)
        other_first = swap_tp(first, 1)
        second = swap_tp(first, 2)
        return (first, second, other_first, swap_tp(second, 1))

    def share_sum(keep, send):
        outs = [sds((BLK, model), bf16)] * 2
        mine, theirs = call(core_add_kernel, outs, (keep, swap_tp(send, 1)), "core_add")
        return mine, swap_tp(theirs, 2)

    half_shape = [sds((tokens // 2, model), bf16)] * 2
    (packed,) = call(
        pack_kernel, [sds((rows, packed_cols), bf16)], (qkv_weight, out_weight), "pack"
    )
    qkvo_blocks = gather(packed)
    down_blocks = gather(ffn_down_weight.astype(bf16))
    in_blocks = gather(ffn_in_weight.astype(bf16))
    n_blocks = len(qkvo_blocks)

    bucket_row = jnp.pad(bucket_ids, (0, 1))[None, :]
    act_one, act_one_t, bias = call(
        prep_kernel,
        [
            sds((tokens, model), bf16),
            sds((model, tokens), bf16),
            sds((heads_here, LEN, LEN), f32),
        ],
        (seg_lengths, bias_table, bucket_row, inputs, norm_gains),
        "prep",
        flops=20 * tokens * model,
        smem=(0, 1),
    )
    weights_one, qkv, prob, mixed, attn_keep, attn_send = call(
        functools.partial(attend_kernel, n_blocks),
        [
            sds((model, packed_cols), bf16),
            sds((tokens, 3 * local), bf16),
            sds((heads_here, LEN, LEN), bf16),
            sds((tokens, local), bf16),
            *half_shape,
        ],
        (act_one, bias, *qkvo_blocks),
        "attend",
        flops=2 * tokens * model * packed_cols + 4 * tokens * LEN * local,
    )
    down_full, hidden_grad = call(
        functools.partial(dhid_kernel, n_blocks),
        [sds((model, hidden), bf16), sds((tokens, hidden), f32)],
        (cotangent, *down_blocks),
        "dhid",
        flops=2 * tokens * model * hidden,
    )
    attn_sums = sum_halves(attn_keep, attn_send)
    resid, act_two, hidden_act, pre_grad, back_keep, back_send = call(
        functools.partial(ffn_kernel, n_blocks),
        [
            sds((tokens, model), f32),
            sds((tokens, model), bf16),
            sds((tokens, hidden), bf16),
            sds((tokens, hidden), bf16),
            *half_shape,
        ],
        (inputs, norm_gains, hidden_grad, *attn_sums, *in_blocks),
        "ffn",
        flops=4 * tokens * model * hidden,
        scratch=[pltpu.VMEM((model, hidden), bf16)],
    )
    back_sums = sum_halves(back_keep, back_send)
    grad_scratch = [pltpu.VMEM((model, hidden), f32)]
    down_parts = call(
        weight_grad_kernel,
        spread_shapes(dp, model, hidden),
        (cotangent, hidden_act),
        "down_grad",
        flops=2 * tokens * model * hidden,
        scratch=grad_scratch,
    )
    in_parts = call(
        weight_grad_kernel,
        spread_shapes(dp, model, hidden),
        (act_two, pre_grad),
        "in_grad",
        flops=2 * tokens * model * hidden,
        scratch=grad_scratch,
    )
    ffn_halves = call(
        ffn_out_kernel,
        half_shape,
        (hidden_act, down_full),
        "ffn_out",
        flops=2 * tokens * model * hidden,
    )
    qkvo_shapes = spread_shapes(dp, model, packed_cols)
    *qkvo_parts, share_grad, gain_two_part, score_grad, proj_grad = call(
        functools.partial(attend_back_kernel, len(qkvo_shapes)),
        [
            *qkvo_shapes,
            sds((BLK, model), f32),
            sds((1, model), f32),
            sds((heads_here, LEN, LEN), bf16),
            sds((tokens, 3 * local), bf16),
        ],
        (
            resid,
            cotangent,
            norm_gains,
            *back_sums,
            weights_one,
            qkv,
            prob,
            mixed,
            act_one_t,
        ),
        "attend_back",
        flops=2 * tokens * model * (packed_cols + local) + 10 * tokens * LEN * local,
        scratch=[pltpu.VMEM((tokens, model), bf16), pltpu.VMEM((model, packed_cols), f32)],
        limit=40,
    )
    act_keep, act_send, table_part = call(
        tail_kernel,
        [*half_shape, sds((BUCKETS, heads_here), f32)],
        (score_grad, proj_grad, weights_one, bucket_row),
        "tail",
        flops=2 * tokens * model * 3 * local,
        scratch=[pltpu.VMEM((8, 2 * LEN), f32)],
    )
    (block_out,) = call(
        block_out_kernel,
        [sds((BLK, model), bf16)],
        (resid, *share_sum(*ffn_halves)),
        "block_out",
    )
    input_grad, gain_one_part = call(
        input_grad_kernel,
        [sds((BLK, model), f32), sds((1, model), f32)],
        (inputs, norm_gains, share_grad, *share_sum(act_keep, act_send)),
        "input_grad",
    )

    everyone = dp * tp
    table_spread = lax.dynamic_update_slice_in_dim(
        jnp.zeros((BUCKETS, HEADS), f32), table_part, lax.axis_index("tp") * heads_here, 1
    )
    small = jnp.concatenate(
        (gain_one_part, gain_two_part, table_spread.reshape(1, -1)), axis=1
    ).reshape(-1, BLK)
    small = jnp.pad(small, ((0, 16 - small.shape[0]), (0, 0)))
    gathered = lax.all_to_all(
        jnp.broadcast_to(small[None], (everyone, 16, BLK)), ("dp", "tp"), 0, 0
    )
    small_sum = jnp.sum(gathered, axis=0).reshape(-1)
    gains_sum = small_sum[: 2 * model].reshape(2, model)
    table_whole = small_sum[2 * model : 2 * model + BUCKETS * HEADS].reshape(BUCKETS, HEADS)
    table_grad = lax.dynamic_slice_in_dim(
        table_whole, lax.axis_index("tp") * heads_here, heads_here, 1
    )

    def summed(parts):
        return call(
            functools.partial(sum_kernel, len(parts)),
            [sds((rows, parts[0].shape[1]), f32), sds((1, BLK), f32)],
            parts,
            "sum_parts",
        )

    down_grad, down_squares = summed(scatter(down_parts))
    in_grad, in_squares = summed(scatter(in_parts))
    last_parts = scatter(qkvo_parts)
    qkvo_grad, payload = call(
        functools.partial(last_sum_kernel, len(last_parts)),
        [sds((rows, packed_cols), f32), sds((everyone, 8, BLK), f32)],
        (*last_parts, down_squares, in_squares),
        "last_sum",
    )
    squares = lax.all_to_all(payload, ("dp", "tp"), 0, 0)
    matrix = [sds((rows, hidden), f32)] * 3 + [sds((rows, hidden), bf16)]
    state = (
        qkv_weight,
        qkv_first,
        qkv_second,
        out_weight,
        out_first,
        out_second,
        ffn_in_weight,
        ffn_in_first,
        ffn_in_second,
        ffn_down_weight,
        ffn_down_first,
        ffn_down_second,
        norm_gains,
        gains_first,
        gains_second,
        bias_table,
        table_first,
        table_second,
    )
    norm, *updated = call(
        adam_kernel,
        [
            sds((1, 1), f32),
            *[sds(qkv_weight.shape, f32)] * 3,
            sds(qkv_weight.shape, bf16),
            *[sds(out_weight.shape, f32)] * 3,
            sds(out_weight.shape, bf16),
            *matrix,
            *matrix,
            *[sds(norm_gains.shape, f32)] * 4,
            *[sds(bias_table.shape, f32)] * 3,
        ],
        (
            squares,
            gains_sum,
            table_whole,
            table_grad,
            qkvo_grad,
            in_grad,
            down_grad,
            *state,
        ),
        "adam",
    )
    return (block_out, input_grad, norm.reshape(()), *updated)


def solution(mesh):
    row = P("dp", None)
    matrix = P("dp", "tp")
    stack = P(None, "dp", "tp")
    table = P(None, "tp")
    share = P(("dp", "tp"), None)
    in_specs = (
        *(row,) * 3,
        P(),
        *(stack,) * 3,
        *(matrix,) * 9,
        *(P(),) * 3,
        *(table,) * 3,
    )
    out_specs = (
        *(share,) * 2,
        P(),
        *(stack,) * 4,
        *(matrix,) * 12,
        *(P(),) * 4,
        *(table,) * 3,
    )
    return jax.shard_map(
        functools.partial(on_device, mesh.shape["dp"]),
        mesh=mesh,
        in_specs=in_specs,
        out_specs=out_specs,
        check_vma=False,
    )
```

```python
import functools
import math

import jax
import jax.numpy as jnp
from jax import lax
from jax.experimental import pallas as pl
from jax.experimental.pallas import tpu as pltpu
from jax.sharding import PartitionSpec as P

HEADS = 12
HDIM = 64
BUCKETS = 32
LEN = 512
BLK = 128
WIN = LEN + BLK
SMALL = 16


eps_norm = 1e-06
clip_norm = 1.0
beta_one = 0.9
beta_two = 0.999
adam_eps = 1e-08
decay_rate = 0.01
adam_step = 10.0
mask_fill = -1000000000.0
rate_small = 0.02
rate_large = 0.5
gelu_coef = 0.044715
root_coef = math.sqrt(2.0 / math.pi)

f32 = jnp.float32
bf16 = jnp.bfloat16
sds = jax.ShapeDtypeStruct


def dot_nn(a, b):
    return lax.dot_general(a, b, (((1,), (0,)), ((), ())), preferred_element_type=f32)


def dot_nt(a, b):
    return lax.dot_general(a, b, (((1,), (1,)), ((), ())), preferred_element_type=f32)


def dot_tn(a, b):
    return lax.dot_general(a, b, (((0,), (0,)), ((), ())), preferred_element_type=f32)


def after(value, *deps):
    return lax.optimization_barrier((value, *deps))[0]


def call(body, outs, args, name, hbm=(), scratch=(), limit=16, behind=()):
    spaces = [pl.ANY if i in hbm else pltpu.VMEM for i in range(len(args))]
    args = [after(args[0], *behind), *args[1:]] if behind else args
    args = [
        pltpu.with_memory_space_constraint(a, pltpu.HBM) if i in hbm else a for i, a in enumerate(args)
    ]
    return pl.pallas_call(
        body,
        out_shape=tuple(outs),
        in_specs=[pl.BlockSpec(memory_space=space) for space in spaces],
        out_specs=tuple(
            pl.BlockSpec(memory_space=pl.ANY if hasattr(o, "memory_space") else pltpu.VMEM) for o in outs
        ),
        scratch_shapes=list(scratch),
        compiler_params=pltpu.CompilerParams(vmem_limit_bytes=limit << 20),
        cost_estimate=pl.CostEstimate(flops=0, bytes_accessed=0, transcendentals=0),
        name=name,
    )(*args)


def to_hbm(staged, out, sem):
    copy = pltpu.make_async_copy(staged, out, sem)
    copy.start()
    copy.wait()


def assemble(into, blocks, start_col=0):
    cols = slice(start_col, start_col + into.shape[1])
    if len(blocks) == 1:
        into[...] = blocks[0][:, cols]
        return
    me = lax.axis_index("dp")
    rows = blocks[0].shape[0]
    for e, block in enumerate(blocks):
        start = pl.multiple_of((me ^ e) * rows, 32)
        into[pl.ds(start, rows), :] = block[:, cols]


def spread(grad, outs, order=(1, 2, 4)):
    if len(outs) == 1:
        outs[0][...] = grad[...].astype(bf16)
        return
    me = lax.axis_index("dp")
    rows = outs[0].shape[1]
    keep, high, low = outs
    for b in range(2):
        for k in range(4):
            out, at = ((low, high)[k >> 1], k & 1) if b else (keep, k)
            apart = b * order[0] ^ (k >> 1) * order[1] ^ (k & 1) * order[2]
            start = pl.multiple_of((me ^ apart) * rows, 32)
            out[at] = grad[pl.ds(start, rows), :].astype(bf16)


def spread_shapes(dp, width, cols):
    if dp == 8:
        return [sds((n, width // dp, cols), bf16) for n in (4, 2, 2)]
    return [sds((width, cols), bf16)]


def half_rows():
    core = lax.axis_index("tp") & 1
    for half in range(2):
        for at in range(2):
            start = pl.multiple_of(((core ^ half) + 2 * at) * BLK, BLK)
            yield half, at, pl.ds(start, BLK)


def pack_kernel(qkv, out, down, ffn_in, packed, packed_ffn, *scratch):
    *landed, sems = scratch
    copies = [
        pltpu.make_async_copy(source, to, sems.at[i])
        for i, (source, to) in enumerate(zip((qkv, out, down, ffn_in), landed))
    ]
    for copy in copies:
        copy.start()
    local = out.shape[1]
    copies[0].wait()
    copies[1].wait()
    for part in range(3):
        packed[:, part * local : (part + 1) * local] = landed[0][part].astype(bf16)
    packed[:, 3 * local :] = landed[1][...].astype(bf16)
    width = down.shape[1]
    for i in (2, 3):
        copies[i].wait()
        packed_ffn[:, (i - 2) * width : (i - 1) * width] = landed[i][...].astype(bf16)


def prep_kernel(
    seg_in, table_in, bucket_in, x_in, gains_in, dy_in, act, act_t, bias, bucket, x, gains, dy, seg, table, ids, sems
):
    sources = (x_in, gains_in, bucket_in, seg_in, table_in, dy_in)
    copies = [
        pltpu.make_async_copy(source, to, sems.at[i])
        for i, (source, to) in enumerate(zip(sources, (x, gains, ids, seg, table, dy)))
    ]
    for copy in copies:
        copy.start()
    copies[0].wait()
    copies[1].wait()
    values = x[...].astype(f32)
    scale = lax.rsqrt(jnp.mean(values * values, axis=-1, keepdims=True) + eps_norm)
    low = (values * scale * gains[0:1, :]).astype(bf16)
    act[...] = low
    act_t[...] = low.T
    for copy in copies[2:]:
        copy.wait()
    ends = [seg[0, 0]]
    for k in (1, 2):
        ends.append(ends[-1] + seg[0, k])

    def segment_of(position):
        return sum((position >= end).astype(jnp.int32) for end in ends)

    seg_cols = segment_of(lax.broadcasted_iota(jnp.int32, (1, LEN), 1))
    heads = bias.shape[0]
    bucket[...] = jnp.zeros_like(bucket)
    bucket[:, : 2 * LEN - 1] = ids[...]
    lines = []
    for h in range(heads):
        line = jnp.zeros((1, 2 * LEN), f32)
        for b in range(BUCKETS):
            line = jnp.where(bucket[...] == b, table[h, b], line)
        lines.append(line)
    for r in range(LEN // BLK):
        seg_rows = segment_of(lax.broadcasted_iota(jnp.int32, (BLK, 1), 0) + r * BLK)
        visible = seg_rows == seg_cols
        low_at = LEN - BLK - r * BLK
        for h in range(heads):
            window = jnp.broadcast_to(lines[h][:, low_at : low_at + WIN], (BLK, WIN))
            turned = pltpu.roll(window, 1, 1, stride=1, stride_axis=0)
            bias[h, r * BLK : (r + 1) * BLK, :] = jnp.where(visible, turned[:, BLK:], mask_fill)


def attend_kernel(n_blocks, act, bias, *rest):
    blocks = rest[:n_blocks]
    weights, qkv, prob, mixed, keep, send = rest[n_blocks:]
    assemble(weights, blocks)
    width = qkv.shape[1] // 3
    qkv[...] = dot_nn(act[...], weights[:, : 3 * width]).astype(bf16)
    for h in range(bias.shape[0]):
        cols = slice(h * HDIM, (h + 1) * HDIM)
        query, key, value = (qkv[:, s * width + h * HDIM : s * width + (h + 1) * HDIM] for s in range(3))
        scores = dot_nt(query, key) + bias[h]
        top = jnp.max(scores, axis=-1, keepdims=True)
        exps = jnp.exp(scores - top)
        total = jnp.sum(exps, axis=-1, keepdims=True)
        low = (exps * (1.0 / total)).astype(bf16)
        prob[h] = low
        mixed[:, cols] = dot_nn(low, value).astype(bf16)
    out_cols = weights[:, 3 * width :]
    for half, at, rows in half_rows():
        to = send if half else keep
        to[at * BLK : (at + 1) * BLK, :] = dot_nt(mixed[rows, :], out_cols).astype(bf16)


def ffn_kernel(n_blocks, x, gains, dy, own, other, *rest):
    blocks = rest[:n_blocks]
    resid, act, hidden, pre_grad, keep, send, down, weights, hidden_grad = rest[n_blocks:]
    assemble(down, blocks)
    assemble(weights, blocks, down.shape[1])
    hidden_grad[...] = dot_nn(dy[...], down[...])
    for half, at, rows in half_rows():
        here = slice(at * BLK, (at + 1) * BLK)
        values = x[rows, :].astype(f32) + (other if half else own)[here, :].astype(f32)
        resid[rows, :] = values
        scale = lax.rsqrt(jnp.mean(values * values, axis=-1, keepdims=True) + eps_norm)
        low = (values * scale * gains[1:2, :]).astype(bf16)
        act[rows, :] = low
        u = dot_nn(low, weights[...])
        square = u * u
        tanh_part = jnp.tanh(root_coef * (u + gelu_coef * square * u))
        hidden[rows, :] = (0.5 * u * (1.0 + tanh_part)).astype(bf16)
        inner = root_coef * (1.0 + 3.0 * gelu_coef * square)
        slope = 0.5 * (1.0 + tanh_part) + 0.5 * u * (1.0 - tanh_part * tanh_part) * inner
        du = (hidden_grad[rows, :] * slope).astype(bf16)
        pre_grad[rows, :] = du
        (send if half else keep)[here, :] = dot_nt(du, weights[...]).astype(bf16)


def weight_grad_kernel(order, left, right, *rest):
    outs, grad = rest[:-1], rest[-1]
    grad[...] = dot_tn(left[...], right[...])
    spread(grad, outs, order)


def ffn_out_kernel(hidden, weights, keep, send):
    for half, at, rows in half_rows():
        to = send if half else keep
        to[at * BLK : (at + 1) * BLK, :] = dot_nt(hidden[rows, :], weights[...]).astype(bf16)


def attend_back_kernel(
    n_outs, resid, dy, gains, own, other, weights, qkv, prob, mixed, act_t, *rest
):
    outs = rest[:n_outs]
    share_grad, gain_part, score_grad, proj_grad, resid_low, grad = rest[n_outs:]
    chip = lax.axis_index("tp") >> 1
    width = qkv.shape[1] // 3
    for half, at, rows in half_rows():
        here = slice(at * BLK, (at + 1) * BLK)
        act_grad = (other if half else own)[here, :].astype(f32)
        values = resid[rows, :]
        scale = lax.rsqrt(jnp.mean(values * values, axis=-1, keepdims=True) + eps_norm)
        normed = values * scale
        normal_grad = act_grad * gains[1:2, :]
        mean_part = jnp.mean(normal_grad * normed, axis=-1, keepdims=True)
        total = dy[rows, :].astype(f32) + scale * (normal_grad - normed * mean_part)
        resid_low[rows, :] = total.astype(bf16)
        if half == 0:

            @pl.when(chip == at)
            def _():
                share_grad[...] = total
                gain_part[...] = jnp.sum(act_grad * normed, axis=0, keepdims=True)

    mix_grad = dot_nn(resid_low[...], weights[:, 3 * width :]).astype(bf16)
    for h in range(prob.shape[0]):
        query, key, value = (qkv[:, s * width + h * HDIM : s * width + (h + 1) * HDIM] for s in range(3))
        grad_rows = mix_grad[:, h * HDIM : (h + 1) * HDIM]
        prob_grad = dot_nt(grad_rows, value)
        prob_here = prob[h].astype(f32)
        row_dot = jnp.sum(prob_here * prob_grad, axis=-1, keepdims=True)
        low = (prob_here * (prob_grad - row_dot)).astype(bf16)
        score_grad[h] = low
        for s, part in enumerate((dot_nn(low, key), dot_tn(low, query), dot_tn(prob[h], grad_rows))):
            proj_grad[:, s * width + h * HDIM : s * width + (h + 1) * HDIM] = part.astype(bf16)
    grad[:, : 3 * width] = dot_nn(act_t[...], proj_grad[...])
    grad[:, 3 * width :] = dot_tn(resid_low[...], mixed[...])
    spread(grad, outs)


def tail_kernel(score_grad, proj_grad, weights, bucket, x, gain_two, *rest):
    *high, keep, send, small, diag = rest
    width = proj_grad.shape[1]
    gain_one = jnp.zeros(gain_two.shape, f32)
    for half, at, rows in half_rows():
        to = send if half else keep
        act_grad = dot_nt(proj_grad[rows, :], weights[:, :width])
        to[at * BLK : (at + 1) * BLK, :] = act_grad.astype(bf16)
        values = x[rows, :].astype(f32)
        scale = lax.rsqrt(jnp.mean(values * values, axis=-1, keepdims=True) + eps_norm)
        gain_one = gain_one + jnp.sum(act_grad * (values * scale), axis=0, keepdims=True)
    row = lax.broadcasted_iota(jnp.int32, (BLK, BLK), 0)
    col = lax.broadcasted_iota(jnp.int32, (BLK, BLK), 1)
    flip = (row + col == BLK - 1).astype(f32).astype(bf16)
    onehot = (lax.broadcasted_iota(jnp.int32, (BUCKETS, 2 * LEN), 0) == bucket[...]).astype(f32)
    diag[...] = jnp.zeros_like(diag)
    heads = score_grad.shape[0]
    for h in range(heads):
        for r in range(LEN // BLK):
            flipped = dot_nn(flip, score_grad[h, r * BLK : (r + 1) * BLK, :])
            wide = jnp.concatenate([flipped, jnp.zeros((BLK, BLK), f32)], axis=1)
            turned = pltpu.roll(wide, 0, 1, stride=1, stride_axis=0)
            low_at = LEN - BLK - r * BLK
            diag[h : h + 1, low_at : low_at + WIN] += jnp.sum(turned, axis=0, keepdims=True)
    by_bucket = lax.dot_general(
        diag[...],
        onehot,
        (((1,), (1,)), ((), ())),
        precision=lax.Precision.HIGHEST,
        preferred_element_type=f32,
    )
    first = lax.axis_index("tp") * heads
    cells = [
        sum(jnp.where(first + h == head, by_bucket[h : h + 1, :], 0.0) for h in range(heads))
        for head in range(HEADS)
    ]
    cells.append(jnp.zeros((1, gain_one.shape[1] - HEADS * BUCKETS), f32))
    lines = (gain_one, gain_two[...], jnp.concatenate(cells, axis=1))
    whole = jnp.concatenate((*lines, jnp.zeros((SMALL - 3, gain_one.shape[1]), f32)), axis=0)
    if high:
        rows = high[0].shape[1]
        small[:rows, :] = high[0][0]
        small[rows : 2 * rows, :] = high[0][1]
        small[2 * rows :, :] = whole.astype(bf16)
    else:
        small[...] = whole


def core_add_kernel(keep, got, mine, theirs):
    chip = lax.axis_index("tp") >> 1
    for to, index in ((mine, chip), (theirs, 1 - chip)):
        rows = pl.ds(pl.multiple_of(index * BLK, BLK), BLK)
        to[...] = (keep[rows, :].astype(f32) + got[rows, :].astype(f32)).astype(bf16)


def share_ds():
    return pl.ds(pl.multiple_of(lax.axis_index("tp") * BLK, BLK), BLK)


def block_out_kernel(resid, mine, got, out):
    out[...] = (resid[share_ds(), :] + (mine[...].astype(f32) + got[...].astype(f32))).astype(bf16)


def input_grad_kernel(x, gains, share_grad, mine, got, out):
    values = x[share_ds(), :].astype(f32)
    scale = lax.rsqrt(jnp.mean(values * values, axis=-1, keepdims=True) + eps_norm)
    normed = values * scale
    normal_grad = (mine[...].astype(f32) + got[...].astype(f32)) * gains[0:1, :]
    mean_part = jnp.mean(normal_grad * normed, axis=-1, keepdims=True)
    out[...] = share_grad[...] + scale * (normal_grad - normed * mean_part)


def add_kernel(one, two, out):
    out[...] = (one[...].astype(f32) + two[...].astype(f32)).astype(bf16)


def high_add_kernel(keep, got, theirs):
    for k in range(2):
        theirs[k] = (keep[k + 2].astype(f32) + got[k].astype(f32)).astype(bf16)


def last_high_kernel(keep, sent, got, out, out_small):
    rows = keep.shape[1]
    out[...] = (keep[2].astype(f32) + got[:rows, :].astype(f32)).astype(bf16)
    out_small[:rows, :] = (keep[3].astype(f32) + got[rows : 2 * rows, :].astype(f32)).astype(bf16)
    small = slice(2 * rows, None)
    out_small[rows:, :] = (sent[small, :].astype(f32) + got[small, :].astype(f32)).astype(bf16)


def last_late_kernel(keep, got_low, sent, got, out):
    rows = keep.shape[1]
    block = keep[1].astype(f32) + got_low[1].astype(f32) + got[:rows, :].astype(f32)
    out[:rows, :] = block.astype(bf16)
    out[rows:, :] = (sent[rows:, :].astype(f32) + got[rows:, :].astype(f32)).astype(bf16)


def late_add_kernel(keep, got_low, got, mine, theirs):
    for k, to in enumerate((mine, theirs)):
        to[...] = (keep[k].astype(f32) + got_low[k].astype(f32) + got[k].astype(f32)).astype(bf16)


def fold(values):
    rows, cols = values.shape
    squares = values * values
    lanes = sum(squares[:, c : c + BLK] for c in range(0, cols, BLK))
    return jnp.sum(lanes, axis=0, keepdims=True)


def sum_kernel(n_parts, *rest):
    parts, (grad, squares) = rest[:n_parts], rest[n_parts:]
    total = sum(part[...].astype(f32) for part in parts)
    grad[...] = total
    squares[...] = fold(total)


def last_sum_kernel(direct, extra_a, extra_b, *rest):
    *parts, grad, out, payload, lines, sem = rest
    if direct:
        keep, got_low, got_block, sent, got = parts
        rows = keep.shape[1]
        total = keep[0].astype(f32) + got_low[0].astype(f32)
        total = total + (got_block[...].astype(f32) + got[:rows, :].astype(f32))
        small = sent[rows:, :].astype(f32) + got[rows:, :].astype(f32)
    else:
        total, small = (part[...] for part in parts)
    grad[...] = total
    per_row = total.shape[1] // BLK
    lines[...] = jnp.zeros_like(lines)
    for line in range(SMALL):
        row, at = divmod(line, per_row)
        lines[line : line + 1, :] = small[row : row + 1, at * BLK : (at + 1) * BLK]
    me = lax.axis_index("dp")
    start = pl.multiple_of(jnp.minimum(2 * me, SMALL), 2)
    squares = fold(total) + extra_a[...] + extra_b[...]
    told = jnp.concatenate((squares, lines[pl.ds(start, 2), :], jnp.zeros((5, BLK), f32)), axis=0)
    payload[...] = jnp.broadcast_to(told[None], payload.shape)
    to_hbm(payload, out, sem)


def adamw(weight, gradient, moment_one, moment_two, rate):
    one_new = beta_one * moment_one + (1.0 - beta_one) * gradient
    two_new = beta_two * moment_two + (1.0 - beta_two) * gradient * gradient
    one_hat = one_new / (1.0 - beta_one**adam_step)
    two_hat = two_new / (1.0 - beta_two**adam_step)
    weight_new = weight - rate * (one_hat / (jnp.sqrt(two_hat) + adam_eps) + decay_rate * weight)
    return (weight_new, one_new, two_new)


def adam_kernel(*refs):
    told, grad_qkvo, grad_in, grad_down, *state = refs[:22]
    outs = refs[22:46]
    *landed, gains_sum, table_grad, sems = refs[46:]
    copies = [pltpu.make_async_copy(state[i], landed[i], sems.at[i]) for i in range(12)]
    for copy in copies:
        copy.start()
    qkv, out, ffn_in, ffn_down = (landed[i : i + 3] for i in range(0, 12, 3))
    gains, table = state[12:15], state[15:18]
    norm_ref, qkv_o, out_o, in_o, down_o, gains_o, gains_grad, table_o = (
        outs[0],
        outs[1:5],
        outs[5:9],
        outs[9:13],
        outs[13:17],
        outs[17:20],
        outs[20],
        outs[21:24],
    )
    tp = lax.axis_size("tp")
    squares = told[0, 0:1, :]
    for i in range(1, told.shape[0]):
        squares = squares + told[i, 0:1, :]
    model = gains_sum.shape[1]
    per_row = model // BLK
    per_line = BLK // BUCKETS
    first = lax.axis_index("tp") * table_grad.shape[0]
    for line in range(2 * per_row + HEADS // per_line):
        index, at = divmod(line, 2)
        value = told[index * tp, at + 1 : at + 2, :]
        for i in range(1, tp):
            value = value + told[index * tp + i, at + 1 : at + 2, :]
        squares = squares + value * value
        row, at = divmod(line, per_row)
        if row < 2:
            gains_sum[row : row + 1, at * BLK : (at + 1) * BLK] = value
            continue
        for i in range(per_line):
            head = at * per_line + i
            cell = value[:, i * BUCKETS : (i + 1) * BUCKETS]
            for h in range(table_grad.shape[0]):

                @pl.when(first + h == head)
                def _():
                    table_grad[h : h + 1, :] = cell

    norm = jnp.sqrt(jnp.sum(squares, axis=1, keepdims=True))
    norm_ref[...] = norm
    factor = clip_norm / jnp.maximum(norm, clip_norm)

    def update(state_refs, gradient, to, rate, at=...):
        new = adamw(state_refs[0][at], gradient * factor, state_refs[1][at], state_refs[2][at], rate)
        for ref, value in zip(to, new):
            ref[at] = value
        if len(to) == 4:
            to[3][at] = new[0].astype(bf16)

    update(gains, gains_sum[...], gains_o, rate_large)
    gains_grad[...] = gains_sum[...] * factor
    update(table, table_grad[...], table_o, rate_large)
    width = qkv[0].shape[2]
    for copy in copies[:3]:
        copy.wait()
    for part in range(3):
        update(qkv, grad_qkvo[:, part * width : (part + 1) * width], qkv_o, rate_small, part)
    for copy in copies[3:6]:
        copy.wait()
    update(out, grad_qkvo[:, 3 * width :], out_o, rate_large)
    for copy in copies[6:9]:
        copy.wait()
    update(ffn_in, grad_in[...], in_o, rate_small)
    for copy in copies[9:]:
        copy.wait()
    update(ffn_down, grad_down[...], down_o, rate_small)


def on_device(
    dp,
    inputs,
    cotangent,
    seg_lengths,
    bucket_ids,
    qkv_weight,
    qkv_first,
    qkv_second,
    out_weight,
    out_first,
    out_second,
    ffn_in_weight,
    ffn_in_first,
    ffn_in_second,
    ffn_down_weight,
    ffn_down_first,
    ffn_down_second,
    norm_gains,
    gains_first,
    gains_second,
    bias_table,
    table_first,
    table_second,
):
    tokens, model = inputs.shape
    rows, local = out_weight.shape
    hidden = ffn_in_weight.shape[1]
    heads_here = local // HDIM
    tp = lax.axis_size("tp")
    packed_cols = 4 * local
    direct = dp == 8

    def swap_dp(value, distance):
        return lax.ppermute(value, "dp", [(i, i ^ distance) for i in range(dp)])

    def swap_tp(value, distance):
        return lax.ppermute(value, "tp", [(i, i ^ distance) for i in range(tp)])

    def add(one, two, behind=()):
        (out,) = call(add_kernel, [sds(one.shape, bf16)], (one, two), "add", limit=4, behind=behind)
        return out

    def high_add(keep, got, behind):
        (out,) = call(
            high_add_kernel,
            [sds((2, *keep.shape[1:]), bf16)],
            (keep, got),
            "high_add",
            limit=4,
            behind=behind,
        )
        return out

    def late_add(keep, got_low, got, behind):
        return call(
            late_add_kernel,
            [sds(keep.shape[1:], bf16)] * 2,
            (keep, got_low, got),
            "late_add",
            limit=4,
            behind=behind,
        )

    half_shape = [sds((tokens // 2, model), bf16)] * 2
    matrices = (qkv_weight, out_weight, ffn_down_weight, ffn_in_weight)
    packed, packed_ffn = call(
        pack_kernel,
        [sds((rows, packed_cols), bf16), sds((rows, 2 * hidden), bf16)],
        matrices,
        "pack",
        hbm=(0, 1, 2, 3),
        scratch=[*(pltpu.VMEM(m.shape, f32) for m in matrices), pltpu.SemaphoreType.DMA((4,))],
    )
    ids = bucket_ids[None, :]
    act_one, act_one_t, bias, bucket_row, inputs, norm_gains_here, cotangent = call(
        prep_kernel,
        [
            sds((tokens, model), bf16),
            sds((model, tokens), bf16),
            sds((heads_here, LEN, LEN), f32),
            sds((1, 2 * LEN), jnp.int32),
            sds(inputs.shape, bf16),
            sds(norm_gains.shape, f32),
            sds(inputs.shape, bf16),
        ],
        (seg_lengths, bias_table.T, ids, inputs, norm_gains, cotangent),
        "prep",
        hbm=range(6),
        scratch=[
            pltpu.SMEM(seg_lengths.shape, jnp.int32),
            pltpu.SMEM((heads_here, BUCKETS), f32),
            pltpu.VMEM(ids.shape, jnp.int32),
            pltpu.SemaphoreType.DMA((6,)),
        ],
    )
    if direct:
        one, two, own = swap_dp(packed, 2), swap_dp(packed, 4), swap_dp(packed, 1)
        ffn_own = swap_dp(packed_ffn, 1)
        one_across = swap_dp(after(one, act_one, ffn_own), 1)
        three = swap_dp(after(two, one, own), 2)
        ffn_two = swap_dp(after(packed_ffn, two, one), 4)
        two_across = swap_dp(two, 1)
        ffn_one = swap_dp(after(packed_ffn, two, one), 2)
        three_across = swap_dp(after(three, one_across), 1)
        qkvo_blocks = [packed, own, one, one_across, two, two_across, three, three_across]
        ffn_three = swap_dp(ffn_two, 2)
        ffn_blocks = [packed_ffn, ffn_own]
        for block in (ffn_one, ffn_two, ffn_three):
            ffn_blocks += [block, swap_dp(block, 1)]
        bias = after(bias, ffn_one, ffn_two)
        ffn_early = (ffn_blocks[3], ffn_blocks[5], ffn_three)
    else:
        qkvo_blocks = [lax.all_gather(packed, "dp", axis=0, tiled=True)]
        ffn_blocks = ffn_early = [lax.all_gather(packed_ffn, "dp", axis=0, tiled=True)]
    n_blocks = len(qkvo_blocks)

    weights_one, qkv, prob, mixed, attn_keep, attn_send = call(
        functools.partial(attend_kernel, n_blocks),
        [
            sds((model, packed_cols), bf16),
            sds((tokens, 3 * local), bf16),
            sds((heads_here, LEN, LEN), bf16),
            sds((tokens, local), bf16),
            *half_shape,
        ],
        (act_one, bias, *qkvo_blocks),
        "attend",
    )
    attn_first = add(attn_keep, swap_tp(attn_send, 1))
    attn_sum = add(attn_first, swap_tp(attn_first, 2), ffn_early)
    resid, act_two, hidden_act, pre_grad, back_keep, back_send, down_full = call(
        functools.partial(ffn_kernel, n_blocks),
        [
            sds((tokens, model), f32),
            sds((tokens, model), bf16),
            sds((tokens, hidden), bf16),
            sds((tokens, hidden), bf16),
            *half_shape,
            sds((model, hidden), bf16),
        ],
        (inputs, norm_gains_here, cotangent, attn_sum, swap_tp(attn_sum, 1), *ffn_blocks),
        "ffn",
        scratch=[pltpu.VMEM((model, hidden), bf16), pltpu.VMEM((tokens, hidden), f32)],
    )
    back_first = add(back_keep, swap_tp(back_send, 1))
    back_got = swap_tp(back_first, 2)
    down_order, in_order = (1, 2, 4), (2, 4, 1)
    grad_scratch = [pltpu.VMEM((model, hidden), f32)]
    down_parts = call(
        functools.partial(weight_grad_kernel, down_order),
        spread_shapes(dp, model, hidden),
        (cotangent, after(hidden_act, back_first)),
        "down_grad",
        scratch=grad_scratch,
    )
    in_parts = call(
        functools.partial(weight_grad_kernel, in_order),
        spread_shapes(dp, model, hidden),
        (act_two, after(pre_grad, down_parts[0])),
        "in_grad",
        scratch=grad_scratch,
    )
    if direct:
        down_keep, down_high, down_low = down_parts
        in_keep, in_high, in_low = in_parts
        down_got, in_got = swap_dp(down_high, down_order[0]), swap_dp(in_high, in_order[0])
        back_sum = add(back_first, back_got, (down_got, in_got))
        down_one = high_add(down_keep, down_got, (back_sum,))
        in_one = high_add(in_keep, in_got, (down_one,))
        back_behind = (in_one,)
    else:
        back_sum = add(back_first, back_got, in_parts)
        back_behind = (back_sum,)
    qkvo_shapes = spread_shapes(dp, model, packed_cols)
    *qkvo_parts, share_grad, gain_two_part, score_grad, proj_grad = call(
        functools.partial(attend_back_kernel, len(qkvo_shapes)),
        [
            *qkvo_shapes,
            sds((BLK, model), f32),
            sds((1, model), f32),
            sds((heads_here, LEN, LEN), bf16),
            sds((tokens, 3 * local), bf16),
        ],
        (
            resid,
            cotangent,
            norm_gains_here,
            back_sum,
            swap_tp(back_sum, 1),
            weights_one,
            qkv,
            prob,
            mixed,
            act_one_t,
        ),
        "attend_back",
        scratch=[pltpu.VMEM((tokens, model), bf16), pltpu.VMEM((model, packed_cols), f32)],
        behind=back_behind,
    )
    everyone = dp * tp
    share_shape = [sds((BLK, model), bf16)] * 2
    small_rows = 2 * rows + SMALL if direct else SMALL
    act_keep, act_send, small = call(
        tail_kernel,
        [*half_shape, sds((small_rows, model), bf16 if direct else f32)],
        (score_grad, proj_grad, weights_one, bucket_row, inputs, gain_two_part, *qkvo_parts[1:2]),
        "tail",
        scratch=[pltpu.VMEM((8, 2 * LEN), f32)],
    )
    if direct:
        keep, _, send_low = qkvo_parts
        single = sds((rows, packed_cols), bf16)
        longer = sds((rows + SMALL, packed_cols), bf16)
        got_high, got_low = swap_dp(small, 1), swap_dp(send_low, 1)
        down_two = late_add(
            down_keep, swap_dp(down_low, down_order[0]), swap_dp(down_one, down_order[1]), (act_keep,)
        )
        high, high_small = call(
            last_high_kernel, [single, longer], (keep, small, got_high), "last_high", behind=down_two
        )
        got_block, got_small = swap_dp(high, 2), swap_dp(high_small, 2)
        in_two = late_add(in_keep, swap_dp(in_low, in_order[0]), swap_dp(in_one, in_order[1]), (high,))
        ffn_behind = in_two
    else:
        ffn_behind = (small,)
    ffn_keep, ffn_send = call(
        ffn_out_kernel, half_shape, (hidden_act, down_full), "ffn_out", behind=ffn_behind
    )
    if direct:
        (late,) = call(
            last_late_kernel, [longer], (keep, got_low, high_small, got_small), "last_late", behind=(ffn_keep,)
        )
        last_parts = (keep, got_low, got_block, late, swap_dp(late, 4))
        down_sums = (down_two[0], swap_dp(down_two[1], down_order[2]))
        in_sums = (in_two[0], swap_dp(in_two[1], in_order[2]))
        share_behind = (late,)
    else:
        qkvo_sums, down_sums, in_sums = (
            (lax.psum_scatter(p[0].astype(f32), "dp", scatter_dimension=0, tiled=True),)
            for p in (qkvo_parts, down_parts, in_parts)
        )
        last_parts = (*qkvo_sums, lax.psum(small, "dp"))
        share_behind = (ffn_keep,)
    ffn_mine, ffn_theirs = call(
        core_add_kernel, share_shape, (ffn_keep, swap_tp(ffn_send, 1)), "core_add", behind=share_behind
    )
    act_mine, act_theirs = call(
        core_add_kernel, share_shape, (act_keep, swap_tp(act_send, 1)), "core_add", behind=(ffn_mine,)
    )

    def summed(parts, behind):
        return call(
            functools.partial(sum_kernel, len(parts)),
            [sds((rows, parts[0].shape[1]), f32), sds((1, BLK), f32)],
            parts,
            "sum_parts",
            behind=behind,
        )

    down_grad, down_squares = summed(down_sums, (act_mine,))
    (block_out,) = call(
        block_out_kernel,
        [sds((BLK, model), bf16)],
        (resid, ffn_mine, swap_tp(ffn_theirs, 2)),
        "block_out",
        behind=(down_grad,),
    )
    (input_grad,) = call(
        input_grad_kernel,
        [sds((BLK, model), f32)],
        (inputs, norm_gains_here, share_grad, act_mine, swap_tp(act_theirs, 2)),
        "input_grad",
        behind=(block_out,),
    )
    in_grad, in_squares = summed(in_sums, (input_grad,))
    qkvo_grad, payload = call(
        functools.partial(last_sum_kernel, direct),
        [sds((rows, packed_cols), f32), pltpu.HBM((everyone, 8, BLK), f32)],
        (down_squares, in_squares, *last_parts),
        "last_sum",
        scratch=[
            pltpu.VMEM((everyone, 8, BLK), f32),
            pltpu.VMEM((SMALL + 8, BLK), f32),
            pltpu.SemaphoreType.DMA,
        ],
        behind=(in_grad,),
    )
    told = lax.all_to_all(payload, ("dp", "tp"), 0, 0)
    matrix = [sds((rows, hidden), f32)] * 3 + [sds((rows, hidden), bf16)]
    state = (
        qkv_weight,
        qkv_first,
        qkv_second,
        out_weight,
        out_first,
        out_second,
        ffn_in_weight,
        ffn_in_first,
        ffn_in_second,
        ffn_down_weight,
        ffn_down_first,
        ffn_down_second,
        norm_gains,
        gains_first,
        gains_second,
        bias_table.T,
        table_first.T,
        table_second.T,
    )
    norm, *updated = call(
        adam_kernel,
        [
            sds((1, 1), f32),
            *[sds(qkv_weight.shape, f32)] * 3,
            sds(qkv_weight.shape, bf16),
            *[sds(out_weight.shape, f32)] * 3,
            sds(out_weight.shape, bf16),
            *matrix,
            *matrix,
            *[sds(norm_gains.shape, f32)] * 4,
            *[sds((heads_here, BUCKETS), f32)] * 3,
        ],
        (
            told,
            qkvo_grad,
            in_grad,
            down_grad,
            *state,
        ),
        "adam",
        hbm=range(4, 16),
        scratch=[
            *(pltpu.VMEM(m.shape, f32) for m in state[:12]),
            pltpu.VMEM(norm_gains.shape, f32),
            pltpu.VMEM((heads_here, BUCKETS), f32),
            pltpu.SemaphoreType.DMA((12,)),
        ],
    )
    return (block_out, input_grad, norm.reshape(()), *updated[:-3], *(t.T for t in updated[-3:]))


def solution(mesh):
    row = P("dp", None)
    matrix = P("dp", "tp")
    stack = P(None, "dp", "tp")
    table = P(None, "tp")
    share = P(("dp", "tp"), None)
    in_specs = (
        *(row,) * 3,
        P(),
        *(stack,) * 3,
        *(matrix,) * 9,
        *(P(),) * 3,
        *(table,) * 3,
    )
    out_specs = (
        *(share,) * 2,
        P(),
        *(stack,) * 4,
        *(matrix,) * 12,
        *(P(),) * 4,
        *(table,) * 3,
    )
    return jax.shard_map(
        functools.partial(on_device, mesh.shape["dp"]),
        mesh=mesh,
        in_specs=in_specs,
        out_specs=out_specs,
        check_vma=False,
    )
```

```python
import functools
import math

import jax
import jax.numpy as jnp
from jax import lax
from jax.experimental import pallas as pl
from jax.experimental.pallas import tpu as pltpu
from jax.sharding import PartitionSpec as P

HEADS = 12
HDIM = 64
BUCKETS = 32
LEN = 512
BLK = 128
WIN = LEN + BLK
SMALL = 16


eps_norm = 1e-06
clip_norm = 1.0
beta_one = 0.9
beta_two = 0.999
adam_eps = 1e-08
decay_rate = 0.01
adam_step = 10.0
mask_fill = -1000000000.0
rate_small = 0.02
rate_large = 0.5
gelu_coef = 0.044715
root_coef = math.sqrt(2.0 / math.pi)

f32 = jnp.float32
bf16 = jnp.bfloat16
sds = jax.ShapeDtypeStruct


def dot_nn(a, b):
    return lax.dot_general(a, b, (((1,), (0,)), ((), ())), preferred_element_type=f32)


def dot_nt(a, b):
    return lax.dot_general(a, b, (((1,), (1,)), ((), ())), preferred_element_type=f32)


def dot_tn(a, b):
    return lax.dot_general(a, b, (((0,), (0,)), ((), ())), preferred_element_type=f32)


def after(value, *deps):
    return lax.optimization_barrier((value, *deps))[0]


def call(body, outs, args, name, hbm=(), scratch=(), limit=16, behind=()):
    spaces = [pl.ANY if i in hbm else pltpu.VMEM for i in range(len(args))]
    args = [after(args[0], *behind), *args[1:]] if behind else args
    args = [
        pltpu.with_memory_space_constraint(a, pltpu.HBM) if i in hbm else a for i, a in enumerate(args)
    ]
    return pl.pallas_call(
        body,
        out_shape=tuple(outs),
        in_specs=[pl.BlockSpec(memory_space=space) for space in spaces],
        out_specs=tuple(
            pl.BlockSpec(memory_space=pl.ANY if hasattr(o, "memory_space") else pltpu.VMEM) for o in outs
        ),
        scratch_shapes=list(scratch),
        compiler_params=pltpu.CompilerParams(vmem_limit_bytes=limit << 20),
        cost_estimate=pl.CostEstimate(flops=0, bytes_accessed=0, transcendentals=0),
        name=name,
    )(*args)


def to_hbm(staged, out, sem):
    copy = pltpu.make_async_copy(staged, out, sem)
    copy.start()
    copy.wait()


def assemble(into, blocks, start_col=0):
    cols = slice(start_col, start_col + into.shape[1])
    if len(blocks) == 1:
        into[...] = blocks[0][:, cols]
        return
    me = lax.axis_index("dp")
    rows = blocks[0].shape[0]
    for e, block in enumerate(blocks):
        start = pl.multiple_of((me ^ e) * rows, 32)
        into[pl.ds(start, rows), :] = block[:, cols]


def spread(grad, outs, order=(1, 2, 4)):
    if len(outs) == 1:
        outs[0][...] = grad[...].astype(bf16)
        return
    me = lax.axis_index("dp")
    rows = outs[0].shape[1]
    keep, *send = outs
    for b in range(2):
        for k in range(4):
            out, at = (keep, k) if b == 0 else (send[0], k) if len(send) == 1 else (send[1 - (k >> 1)], k & 1)
            apart = b * order[0] ^ (k >> 1) * order[1] ^ (k & 1) * order[2]
            start = pl.multiple_of((me ^ apart) * rows, 32)
            block = grad[pl.ds(start, rows), :].astype(bf16)
            if len(out.shape) == 2:
                out[at * rows : (at + 1) * rows, :] = block
            else:
                out[at] = block


def spread_shapes(dp, width, cols, lengths):
    if dp == 8:
        return [sds((n, width // dp, cols), bf16) for n in lengths]
    return [sds((width, cols), bf16)]


def half_rows():
    core = lax.axis_index("tp") & 1
    for half in range(2):
        for at in range(2):
            start = pl.multiple_of(((core ^ half) + 2 * at) * BLK, BLK)
            yield half, at, pl.ds(start, BLK)


def pack_kernel(qkv, out, down, ffn_in, packed, packed_ffn, *scratch):
    *landed, sems = scratch
    copies = [
        pltpu.make_async_copy(source, to, sems.at[i])
        for i, (source, to) in enumerate(zip((qkv, out, down, ffn_in), landed))
    ]
    for copy in copies:
        copy.start()
    local = out.shape[1]
    copies[0].wait()
    copies[1].wait()
    for part in range(3):
        packed[:, part * local : (part + 1) * local] = landed[0][part].astype(bf16)
    packed[:, 3 * local :] = landed[1][...].astype(bf16)
    width = down.shape[1]
    for i in (2, 3):
        copies[i].wait()
        packed_ffn[:, (i - 2) * width : (i - 1) * width] = landed[i][...].astype(bf16)


def prep_kernel(
    seg_in, table_in, bucket_in, x_in, gains_in, dy_in, act, act_t, bias, bucket, x, gains, dy, seg, table, ids, sems
):
    sources = (x_in, gains_in, bucket_in, seg_in, table_in, dy_in)
    copies = [
        pltpu.make_async_copy(source, to, sems.at[i])
        for i, (source, to) in enumerate(zip(sources, (x, gains, ids, seg, table, dy)))
    ]
    for copy in copies:
        copy.start()
    copies[0].wait()
    copies[1].wait()
    values = x[...].astype(f32)
    scale = lax.rsqrt(jnp.mean(values * values, axis=-1, keepdims=True) + eps_norm)
    low = (values * scale * gains[0:1, :]).astype(bf16)
    act[...] = low
    act_t[...] = low.T
    for copy in copies[2:]:
        copy.wait()
    ends = [seg[0, 0]]
    for k in (1, 2):
        ends.append(ends[-1] + seg[0, k])

    def segment_of(position):
        return sum((position >= end).astype(jnp.int32) for end in ends)

    seg_cols = segment_of(lax.broadcasted_iota(jnp.int32, (1, LEN), 1))
    heads = bias.shape[0]
    bucket[...] = jnp.zeros_like(bucket)
    bucket[:, : 2 * LEN - 1] = ids[...]
    lines = []
    for h in range(heads):
        line = jnp.zeros((1, 2 * LEN), f32)
        for b in range(BUCKETS):
            line = jnp.where(bucket[...] == b, table[h, b], line)
        lines.append(line)
    for r in range(LEN // BLK):
        seg_rows = segment_of(lax.broadcasted_iota(jnp.int32, (BLK, 1), 0) + r * BLK)
        visible = seg_rows == seg_cols
        low_at = LEN - BLK - r * BLK
        for h in range(heads):
            window = jnp.broadcast_to(lines[h][:, low_at : low_at + WIN], (BLK, WIN))
            turned = pltpu.roll(window, 1, 1, stride=1, stride_axis=0)
            bias[h, r * BLK : (r + 1) * BLK, :] = jnp.where(visible, turned[:, BLK:], mask_fill)


def attend_kernel(n_blocks, act, bias, *rest):
    blocks = rest[:n_blocks]
    weights, qkv, prob, mixed, keep, send = rest[n_blocks:]
    assemble(weights, blocks)
    width = qkv.shape[1] // 3
    qkv[...] = dot_nn(act[...], weights[:, : 3 * width]).astype(bf16)
    for h in range(bias.shape[0]):
        cols = slice(h * HDIM, (h + 1) * HDIM)
        query, key, value = (qkv[:, s * width + h * HDIM : s * width + (h + 1) * HDIM] for s in range(3))
        scores = dot_nt(query, key) + bias[h]
        top = jnp.max(scores, axis=-1, keepdims=True)
        exps = jnp.exp(scores - top)
        total = jnp.sum(exps, axis=-1, keepdims=True)
        low = (exps * (1.0 / total)).astype(bf16)
        prob[h] = low
        mixed[:, cols] = dot_nn(low, value).astype(bf16)
    out_cols = weights[:, 3 * width :]
    for half, at, rows in half_rows():
        to = send if half else keep
        to[at * BLK : (at + 1) * BLK, :] = dot_nt(mixed[rows, :], out_cols).astype(bf16)


def ffn_kernel(n_blocks, x, gains, dy, own_a, own_b, other_a, other_b, *rest):
    blocks = rest[:n_blocks]
    resid, act, hidden, pre_grad, keep, send, down, weights, hidden_grad = rest[n_blocks:]
    assemble(down, blocks)
    assemble(weights, blocks, down.shape[1])
    hidden_grad[...] = dot_nn(dy[...], down[...])
    for half, at, rows in half_rows():
        here = slice(at * BLK, (at + 1) * BLK)
        attn = ((own_a, own_b), (other_a, other_b))[half][at]
        values = x[rows, :].astype(f32) + attn[...].astype(f32)
        resid[rows, :] = values
        scale = lax.rsqrt(jnp.mean(values * values, axis=-1, keepdims=True) + eps_norm)
        low = (values * scale * gains[1:2, :]).astype(bf16)
        act[rows, :] = low
        u = dot_nn(low, weights[...])
        square = u * u
        tanh_part = jnp.tanh(root_coef * (u + gelu_coef * square * u))
        hidden[rows, :] = (0.5 * u * (1.0 + tanh_part)).astype(bf16)
        inner = root_coef * (1.0 + 3.0 * gelu_coef * square)
        slope = 0.5 * (1.0 + tanh_part) + 0.5 * u * (1.0 - tanh_part * tanh_part) * inner
        du = (hidden_grad[rows, :] * slope).astype(bf16)
        pre_grad[rows, :] = du
        (send if half else keep)[here, :] = dot_nt(du, weights[...]).astype(bf16)


def row_products(weights, grad):
    products = weights.astype(f32) * grad
    width = grad.shape[1]
    folded = sum(products[:, c : c + BLK] for c in range(0, width - BLK + 1, BLK))
    if width % BLK:
        rest = products[:, width - width % BLK :]
        wide = jnp.zeros((grad.shape[0], BLK - width % BLK), f32)
        folded = folded + jnp.concatenate([rest, wide], axis=1)
    return jnp.sum(folded.T, axis=0, keepdims=True)


def down_grad_kernel(order, left, right, *rest):
    outs, grad = rest[:-1], rest[-1]
    grad[...] = dot_tn(left[...], right[...])
    spread(grad, outs, order)


def in_grad_kernel(order, left, right, weights, gains, *rest):
    *outs, gain_part, grad = rest
    grad[...] = dot_tn(left[...], right[...])
    spread(grad, outs, order)
    gain_part[...] = row_products(weights[...], grad[...]) / gains[1:2, :]


def attend_back_kernel(
    n_outs, resid, dy, gains, own, other, weights, qkv, prob, mixed, act_t, bucket, gain_two, *rest
):
    outs = rest[:n_outs]
    share_grad, small, proj_grad, resid_low, grad, diag = rest[n_outs:]
    chip = lax.axis_index("tp") >> 1
    width = qkv.shape[1] // 3
    for half, at, rows in half_rows():
        here = slice(at * BLK, (at + 1) * BLK)
        act_grad = (other if half else own)[here, :].astype(f32)
        values = resid[rows, :]
        scale = lax.rsqrt(jnp.mean(values * values, axis=-1, keepdims=True) + eps_norm)
        normed = values * scale
        normal_grad = act_grad * gains[1:2, :]
        mean_part = jnp.mean(normal_grad * normed, axis=-1, keepdims=True)
        total = dy[rows, :].astype(f32) + scale * (normal_grad - normed * mean_part)
        resid_low[rows, :] = total.astype(bf16)
        if half == 0:

            @pl.when(chip == at)
            def _():
                share_grad[...] = total

    mix_grad = dot_nn(resid_low[...], weights[:, 3 * width :]).astype(bf16)
    heads = prob.shape[0]
    row = lax.broadcasted_iota(jnp.int32, (BLK, BLK), 0)
    col = lax.broadcasted_iota(jnp.int32, (BLK, BLK), 1)
    flip = (row + col == BLK - 1).astype(f32).astype(bf16)
    diag[...] = jnp.zeros_like(diag)
    for h in range(heads):
        query, key, value = (qkv[:, s * width + h * HDIM : s * width + (h + 1) * HDIM] for s in range(3))
        grad_rows = mix_grad[:, h * HDIM : (h + 1) * HDIM]
        prob_grad = dot_nt(grad_rows, value)
        prob_here = prob[h].astype(f32)
        row_dot = jnp.sum(prob_here * prob_grad, axis=-1, keepdims=True)
        low = (prob_here * (prob_grad - row_dot)).astype(bf16)
        for r in range(LEN // BLK):
            flipped = dot_nn(flip, low[r * BLK : (r + 1) * BLK, :])
            wide = jnp.concatenate([flipped, jnp.zeros((BLK, BLK), f32)], axis=1)
            turned = pltpu.roll(wide, 0, 1, stride=1, stride_axis=0)
            low_at = LEN - BLK - r * BLK
            diag[h : h + 1, low_at : low_at + WIN] += jnp.sum(turned, axis=0, keepdims=True)
        for s, part in enumerate((dot_nn(low, key), dot_tn(low, query), dot_tn(prob[h], grad_rows))):
            proj_grad[:, s * width + h * HDIM : s * width + (h + 1) * HDIM] = part.astype(bf16)
    grad[:, : 3 * width] = dot_nn(act_t[...], proj_grad[...])
    grad[:, 3 * width :] = dot_tn(resid_low[...], mixed[...])
    onehot = (lax.broadcasted_iota(jnp.int32, (BUCKETS, 2 * LEN), 0) == bucket[...]).astype(f32)
    by_bucket = lax.dot_general(
        diag[...],
        onehot,
        (((1,), (1,)), ((), ())),
        precision=lax.Precision.HIGHEST,
        preferred_element_type=f32,
    )
    first = lax.axis_index("tp") * heads
    cells = [
        sum(jnp.where(first + h == head, by_bucket[h : h + 1, :], 0.0) for h in range(heads))
        for head in range(HEADS)
    ]
    model = gains.shape[1]
    cells.append(jnp.zeros((1, model - HEADS * BUCKETS), f32))
    gain_one = row_products(weights[:, : 3 * width], grad[:, : 3 * width]) / gains[0:1, :]
    lines = (gain_one, gain_two[...], jnp.concatenate(cells, axis=1), jnp.zeros((SMALL - 3, model), f32))
    whole = jnp.concatenate(lines, axis=0)
    if n_outs == 1:
        spread(grad, outs)
        small[...] = whole
        return
    keep, low = outs
    rows = keep.shape[1]
    spread(grad, (keep, small, low))
    small[2 * rows :, :] = whole.astype(bf16)


def ffn_out_kernel(hidden, down, keep, send):
    for half, at, rows in half_rows():
        to = send if half else keep
        to[at * BLK : (at + 1) * BLK, :] = dot_nt(hidden[rows, :], down[...]).astype(bf16)


def act_grad_kernel(proj_grad, weights, keep, *send):
    width = proj_grad.shape[1]
    for half, at, rows in half_rows():
        block = dot_nt(proj_grad[rows, :], weights[:, :width]).astype(bf16)
        if half:
            send[at][...] = block
        else:
            keep[at * BLK : (at + 1) * BLK, :] = block


def core_add_kernel(ffn_keep, ffn_got, act_keep, act_got_a, act_got_b, mine, theirs):
    chip = lax.axis_index("tp") >> 1
    for at in range(2):
        here = slice(at * BLK, (at + 1) * BLK)
        ffn = (ffn_keep[here, :].astype(f32) + ffn_got[here, :].astype(f32)).astype(bf16)
        got = (act_got_a, act_got_b)[at]
        act = (act_keep[here, :].astype(f32) + got[...].astype(f32)).astype(bf16)

        @pl.when(chip == at)
        def _():
            mine[:BLK, :] = ffn
            mine[BLK:, :] = act

        @pl.when(chip != at)
        def _():
            theirs[:BLK, :] = ffn
            theirs[BLK:, :] = act


def share_out_kernel(resid, x, gains, share_grad, mine, got, block_out, input_grad):
    share = pl.ds(pl.multiple_of(lax.axis_index("tp") * BLK, BLK), BLK)
    first, second = slice(0, BLK), slice(BLK, 2 * BLK)
    ffn = mine[first, :].astype(f32) + got[first, :].astype(f32)
    block_out[...] = (resid[share, :] + ffn).astype(bf16)
    values = x[share, :].astype(f32)
    scale = lax.rsqrt(jnp.mean(values * values, axis=-1, keepdims=True) + eps_norm)
    normed = values * scale
    normal_grad = (mine[second, :].astype(f32) + got[second, :].astype(f32)) * gains[0:1, :]
    mean_part = jnp.mean(normal_grad * normed, axis=-1, keepdims=True)
    input_grad[...] = share_grad[...] + scale * (normal_grad - normed * mean_part)


def add_kernel(one, two, out):
    out[...] = (one[...].astype(f32) + two[...].astype(f32)).astype(bf16)


def split_add_kernel(one, two, *outs):
    for i, out in enumerate(outs):
        rows = slice(i * BLK, (i + 1) * BLK)
        out[...] = (one[rows, :].astype(f32) + two[rows, :].astype(f32)).astype(bf16)


def pair_add_kernel(keep, got, mine, theirs):
    for k in range(4):
        to = theirs if k >= 2 else mine
        to[k % 2] = (keep[k].astype(f32) + got[k].astype(f32)).astype(bf16)


def next_add_kernel(keep, got, mine, theirs):
    for k, to in enumerate((mine, theirs)):
        to[...] = (keep[k].astype(f32) + got[k].astype(f32)).astype(bf16)


def last_high_kernel(keep, sent, got, out):
    rows = keep.shape[1]
    for k in range(2):
        here = slice(k * rows, (k + 1) * rows)
        out[here, :] = (keep[k + 2].astype(f32) + got[here, :].astype(f32)).astype(bf16)
    small = slice(2 * rows, None)
    out[small, :] = (sent[small, :].astype(f32) + got[small, :].astype(f32)).astype(bf16)


def last_late_kernel(keep, got_low, sent, got, mine, out):
    rows = keep.shape[1]
    first, second, small = slice(0, rows), slice(rows, 2 * rows), slice(2 * rows, None)
    mine[...] = keep[0].astype(f32) + got_low[0].astype(f32) + got[first, :].astype(f32)
    block = keep[1].astype(f32) + got_low[1].astype(f32) + got[second, :].astype(f32)
    out[:rows, :] = block.astype(bf16)
    out[rows:, :] = (sent[small, :].astype(f32) + got[small, :].astype(f32)).astype(bf16)


def fold(values):
    rows, cols = values.shape
    squares = values * values
    lanes = sum(squares[:, c : c + BLK] for c in range(0, cols, BLK))
    return jnp.sum(lanes, axis=0, keepdims=True)


def sum_kernel(n_parts, *rest):
    parts, (grad, squares) = rest[:n_parts], rest[n_parts:]
    total = sum(part[...].astype(f32) for part in parts)
    grad[...] = total
    squares[...] = fold(total)


def last_sum_kernel(direct, extra_a, extra_b, *rest):
    *parts, grad, out, payload, lines, sem = rest
    if direct:
        mine, sent, got = parts
        rows = mine.shape[0]
        total = mine[...] + got[:rows, :].astype(f32)
        small = sent[rows:, :].astype(f32) + got[rows:, :].astype(f32)
    else:
        total, small = (part[...] for part in parts)
    grad[...] = total
    per_row = total.shape[1] // BLK
    lines[...] = jnp.zeros_like(lines)
    for line in range(SMALL):
        row, at = divmod(line, per_row)
        lines[line : line + 1, :] = small[row : row + 1, at * BLK : (at + 1) * BLK]
    me = lax.axis_index("dp")
    start = pl.multiple_of(jnp.minimum(2 * me, SMALL), 2)
    squares = fold(total) + extra_a[...] + extra_b[...]
    two = lines[pl.ds(start, 2), :]
    told = jnp.concatenate((squares, two[0:1, :], two[1:2, :]), axis=1)
    payload[...] = jnp.broadcast_to(told[None], payload.shape)
    to_hbm(payload, out, sem)


def adamw(weight, gradient, moment_one, moment_two, rate):
    one_new = beta_one * moment_one + (1.0 - beta_one) * gradient
    two_new = beta_two * moment_two + (1.0 - beta_two) * gradient * gradient
    one_hat = one_new / (1.0 - beta_one**adam_step)
    two_hat = two_new / (1.0 - beta_two**adam_step)
    weight_new = weight - rate * (one_hat / (jnp.sqrt(two_hat) + adam_eps) + decay_rate * weight)
    return (weight_new, one_new, two_new)


def adam_kernel(*refs):
    told, grad_qkvo, grad_in, grad_down, *state_in = refs[:22]
    norm_ref, *matrices, gains_a, gains_b, gains_c, gains_grad, table_a, table_b, table_c = refs[22:46]
    state, staged = refs[46:64], refs[64:80]
    gains_sum, table_grad, sems_in, sems = refs[80:]
    fetches = [pltpu.make_async_copy(state_in[i], state[i], sems_in.at[i]) for i in range(18)]
    for i in (*range(6, 12), *range(6), *range(12, 18)):
        fetches[i].start()
    gains_o, table_o = (gains_a, gains_b, gains_c), (table_a, table_b, table_c)
    qkv, out, ffn_in, ffn_down, gains, table = (state[i : i + 3] for i in range(0, 18, 3))
    qkv_o, out_o, in_o, down_o = (staged[i : i + 4] for i in range(0, 16, 4))
    tp = lax.axis_size("tp")
    squares = told[0, :, :BLK]
    for i in range(1, told.shape[0]):
        squares = squares + told[i, :, :BLK]
    model = gains_sum.shape[1]
    per_row = model // BLK
    per_line = BLK // BUCKETS
    first = lax.axis_index("tp") * table_grad.shape[0]
    for line in range(2 * per_row + HEADS // per_line):
        index, at = divmod(line, 2)
        cols = slice((at + 1) * BLK, (at + 2) * BLK)
        value = told[index * tp, :, cols]
        for i in range(1, tp):
            value = value + told[index * tp + i, :, cols]
        squares = squares + value * value
        row, at = divmod(line, per_row)
        if row < 2:
            gains_sum[row : row + 1, at * BLK : (at + 1) * BLK] = value
            continue
        for i in range(per_line):
            head = at * per_line + i
            cell = value[:, i * BUCKETS : (i + 1) * BUCKETS]
            for h in range(table_grad.shape[0]):

                @pl.when(first + h == head)
                def _():
                    table_grad[h : h + 1, :] = cell

    norm = jnp.sqrt(jnp.sum(squares, axis=1, keepdims=True))
    norm_ref[...] = norm
    factor = clip_norm / jnp.maximum(norm, clip_norm)

    def update(state_refs, gradient, to, rate, at=...):
        new = adamw(state_refs[0][at], gradient * factor, state_refs[1][at], state_refs[2][at], rate)
        for ref, value in zip(to, new):
            ref[at] = value
        if len(to) == 4:
            to[3][at] = new[0].astype(bf16)

    copies = []

    def arrived(first):
        for i in range(first, first + 3):
            fetches[i].wait()

    def send(first):
        for i in range(first, first + 4):
            copies.append(pltpu.make_async_copy(staged[i], matrices[i], sems.at[i]))
            copies[-1].start()

    arrived(6)
    update(ffn_in, grad_in[...], in_o, rate_small)
    send(8)
    arrived(9)
    update(ffn_down, grad_down[...], down_o, rate_small)
    send(12)
    arrived(0)
    width = qkv[0].shape[2]
    for part in range(3):
        update(qkv, grad_qkvo[:, part * width : (part + 1) * width], qkv_o, rate_small, part)
    send(0)
    arrived(3)
    update(out, grad_qkvo[:, 3 * width :], out_o, rate_large)
    send(4)
    arrived(12)
    update(gains, gains_sum[...], gains_o, rate_large)
    gains_grad[...] = gains_sum[...] * factor
    arrived(15)
    update(table, table_grad[...], table_o, rate_large)
    for copy in copies:
        copy.wait()


def on_device(
    dp,
    inputs,
    cotangent,
    seg_lengths,
    bucket_ids,
    qkv_weight,
    qkv_first,
    qkv_second,
    out_weight,
    out_first,
    out_second,
    ffn_in_weight,
    ffn_in_first,
    ffn_in_second,
    ffn_down_weight,
    ffn_down_first,
    ffn_down_second,
    norm_gains,
    gains_first,
    gains_second,
    bias_table,
    table_first,
    table_second,
):
    tokens, model = inputs.shape
    rows, local = out_weight.shape
    hidden = ffn_in_weight.shape[1]
    heads_here = local // HDIM
    tp = lax.axis_size("tp")
    packed_cols = 4 * local
    direct = dp == 8

    def swap_dp(value, distance):
        return lax.ppermute(value, "dp", [(i, i ^ distance) for i in range(dp)])

    def swap_tp(value, distance):
        return lax.ppermute(value, "tp", [(i, i ^ distance) for i in range(tp)])

    def add(one, two, behind=()):
        (out,) = call(add_kernel, [sds(one.shape, bf16)], (one, two), "add", limit=4, behind=behind)
        return out

    def pair_add(keep, got, behind):
        outs = [sds((2, *keep.shape[1:]), bf16)] * 2
        return call(pair_add_kernel, outs, (keep, got), "pair_add", limit=4, behind=behind)

    def next_add(keep, got, behind):
        outs = [sds(keep.shape[1:], bf16)] * 2
        return call(next_add_kernel, outs, (keep, got), "next_add", limit=4, behind=behind)

    half_shape = [sds((tokens // 2, model), bf16)] * 2
    matrices = (qkv_weight, out_weight, ffn_down_weight, ffn_in_weight)
    packed, packed_ffn = call(
        pack_kernel,
        [sds((rows, packed_cols), bf16), sds((rows, 2 * hidden), bf16)],
        matrices,
        "pack",
        hbm=(0, 1, 2, 3),
        scratch=[*(pltpu.VMEM(m.shape, f32) for m in matrices), pltpu.SemaphoreType.DMA((4,))],
    )
    ids = bucket_ids[None, :]
    act_one, act_one_t, bias, bucket_row, inputs, norm_gains_here, cotangent = call(
        prep_kernel,
        [
            sds((tokens, model), bf16),
            sds((model, tokens), bf16),
            sds((heads_here, LEN, LEN), f32),
            sds((1, 2 * LEN), jnp.int32),
            sds(inputs.shape, bf16),
            sds(norm_gains.shape, f32),
            sds(inputs.shape, bf16),
        ],
        (seg_lengths, bias_table.T, ids, inputs, norm_gains, cotangent),
        "prep",
        hbm=range(6),
        scratch=[
            pltpu.SMEM(seg_lengths.shape, jnp.int32),
            pltpu.SMEM((heads_here, BUCKETS), f32),
            pltpu.VMEM(ids.shape, jnp.int32),
            pltpu.SemaphoreType.DMA((6,)),
        ],
    )
    if direct:
        one, two = swap_dp(packed, 2), swap_dp(packed, 4)
        own, ffn_own = swap_dp(after(packed, act_one), 1), swap_dp(after(packed_ffn, act_one), 1)
        one_across = swap_dp(one, 1)
        three = swap_dp(two, 2)
        ffn_two = swap_dp(after(packed_ffn, two), 4)
        two_across = swap_dp(two, 1)
        ffn_one = swap_dp(after(packed_ffn, three, own, one_across), 2)
        three_across = swap_dp(three, 1)
        qkvo_blocks = [packed, own, one, one_across, two, two_across, three, three_across]
        ffn_three = swap_dp(after(ffn_two, ffn_one), 2)
        ffn_blocks = [packed_ffn, ffn_own, ffn_one, swap_dp(after(ffn_own, ffn_three), 2)]
        for block in (ffn_two, ffn_three):
            ffn_blocks += [block, swap_dp(block, 1)]
        bias = after(bias, ffn_own, ffn_two)
        ffn_early = (ffn_blocks[5], ffn_three)
    else:
        qkvo_blocks = [lax.all_gather(packed, "dp", axis=0, tiled=True)]
        ffn_blocks = ffn_early = [lax.all_gather(packed_ffn, "dp", axis=0, tiled=True)]
    n_blocks = len(qkvo_blocks)

    weights_one, qkv, prob, mixed, attn_keep, attn_send = call(
        functools.partial(attend_kernel, n_blocks),
        [
            sds((model, packed_cols), bf16),
            sds((tokens, 3 * local), bf16),
            sds((heads_here, LEN, LEN), bf16),
            sds((tokens, local), bf16),
            *half_shape,
        ],
        (act_one, bias, *qkvo_blocks),
        "attend",
    )
    half_blocks = [sds((BLK, model), bf16)] * 2
    attn_first = call(
        split_add_kernel, half_blocks, (attn_keep, swap_tp(attn_send, 1)), "split_add", limit=4
    )
    attn_own = [add(first, swap_tp(first, 2), ffn_early) for first in attn_first]
    attn_sums = (*attn_own, *(swap_tp(own, 1) for own in attn_own))
    resid, act_two, hidden_act, pre_grad, back_keep, back_send, down_full, in_full = call(
        functools.partial(ffn_kernel, n_blocks),
        [
            sds((tokens, model), f32),
            sds((tokens, model), bf16),
            sds((tokens, hidden), bf16),
            sds((tokens, hidden), bf16),
            *half_shape,
            *[sds((model, hidden), bf16)] * 2,
        ],
        (inputs, norm_gains_here, cotangent, *attn_sums, *ffn_blocks),
        "ffn",
        scratch=[pltpu.VMEM((tokens, hidden), f32)],
    )
    back_first = add(back_keep, swap_tp(back_send, 1))
    back_got = swap_tp(back_first, 2)
    down_order, in_order = (1, 2, 4), (2, 4, 1)
    grad_scratch = [pltpu.VMEM((model, hidden), f32)]
    down_parts = call(
        functools.partial(down_grad_kernel, down_order),
        spread_shapes(dp, model, hidden, (4, 4)),
        (cotangent, after(hidden_act, back_first)),
        "down_grad",
        scratch=grad_scratch,
    )
    *in_parts, gain_two_part = call(
        functools.partial(in_grad_kernel, in_order),
        [*spread_shapes(dp, model, hidden, (4, 4)), sds((1, model), f32)],
        (act_two, after(pre_grad, down_parts[0]), in_full, norm_gains_here),
        "in_grad",
        scratch=grad_scratch,
    )
    ffn_keep, ffn_send = call(
        ffn_out_kernel, half_shape, (hidden_act, down_full), "ffn_out", behind=(gain_two_part,)
    )
    back_sum = add(back_first, back_got, (ffn_keep,))
    everyone = dp * tp
    qkvo_shapes = spread_shapes(dp, model, packed_cols, (4, 2))
    small_shape = sds((2 * rows + SMALL, model), bf16) if direct else sds((SMALL, model), f32)
    *qkvo_parts, share_grad, small, proj_grad = call(
        functools.partial(attend_back_kernel, len(qkvo_shapes)),
        [*qkvo_shapes, sds((BLK, model), f32), small_shape, sds((tokens, 3 * local), bf16)],
        (
            resid,
            cotangent,
            norm_gains_here,
            back_sum,
            swap_tp(back_sum, 1),
            weights_one,
            qkv,
            prob,
            mixed,
            act_one_t,
            bucket_row,
            gain_two_part,
        ),
        "attend_back",
        scratch=[
            pltpu.VMEM((tokens, model), bf16),
            pltpu.VMEM((model, packed_cols), f32),
            pltpu.VMEM((8, 2 * LEN), f32),
        ],
    )
    def summed(parts, behind):
        return call(
            functools.partial(sum_kernel, len(parts)),
            [sds((rows, parts[0].shape[1]), f32), sds((1, BLK), f32)],
            parts,
            "sum_parts",
            limit=4,
            behind=behind,
        )

    def act_shares(behind):
        keep, *send = call(
            act_grad_kernel,
            [half_shape[0], *half_blocks],
            (proj_grad, weights_one),
            "act_grad",
            behind=behind,
        )
        return keep, [swap_tp(part, 1) for part in send]

    def share_sums(keep, got, behind):
        outs = [sds((2 * BLK, model), bf16)] * 2
        args = (ffn_keep, swap_tp(ffn_send, 1), keep, *got)
        return call(core_add_kernel, outs, args, "core_add", limit=4, behind=behind)

    if direct:
        keep, send_low = qkvo_parts
        down_keep, down_send = down_parts
        in_keep, in_send = in_parts
        in_one = pair_add(in_keep, swap_dp(in_send, in_order[0]), (proj_grad,))
        down_one = pair_add(down_keep, swap_dp(down_send, down_order[0]), in_one)
        got_high = swap_dp(after(small, *down_one), 1)
        share_own, share_got = act_shares(down_one)
        (high,) = call(
            last_high_kernel, [small_shape], (keep, small, got_high), "last_high", limit=4, behind=(share_own,)
        )
        got_low = swap_dp(after(send_low, high), 1)
        mine, theirs = share_sums(share_own, share_got, (high,))
        down_two = next_add(down_one[0], swap_dp(down_one[1], down_order[1]), (mine,))
        in_two = next_add(in_one[0], swap_dp(in_one[1], in_order[1]), down_two)
        down_grad, down_squares = summed((down_two[0], swap_dp(down_two[1], down_order[2])), in_two)
        in_grad, in_squares = summed((in_two[0], swap_dp(in_two[1], in_order[2])), (down_grad,))
        last, late = call(
            last_late_kernel,
            [sds((rows, packed_cols), f32), sds((rows + SMALL, packed_cols), bf16)],
            (keep, got_low, high, swap_dp(high, 2)),
            "last_late",
            limit=4,
            behind=(in_grad,),
        )
        last_parts = (last, late, swap_dp(late, 4))
        share_behind = (late,)
    else:
        qkvo_sums, down_sums, in_sums = (
            (lax.psum_scatter(p[0].astype(f32), "dp", scatter_dimension=0, tiled=True),)
            for p in (qkvo_parts, down_parts, in_parts)
        )
        last_parts = (*qkvo_sums, lax.psum(small, "dp"))
        down_grad, down_squares = summed(down_sums, ())
        in_grad, in_squares = summed(in_sums, ())
        mine, theirs = share_sums(*act_shares(()), ())
        share_behind = ()
    block_out, input_grad = call(
        share_out_kernel,
        [sds((BLK, model), bf16), sds((BLK, model), f32)],
        (resid, inputs, norm_gains_here, share_grad, mine, swap_tp(theirs, 2)),
        "share_out",
        behind=share_behind,
    )
    qkvo_grad, payload = call(
        functools.partial(last_sum_kernel, direct),
        [sds((rows, packed_cols), f32), pltpu.HBM((everyone, 1, 3 * BLK), f32)],
        (down_squares, in_squares, *last_parts),
        "last_sum",
        scratch=[
            pltpu.VMEM((everyone, 1, 3 * BLK), f32),
            pltpu.VMEM((SMALL + 8, BLK), f32),
            pltpu.SemaphoreType.DMA,
        ],
        behind=(block_out,),
    )
    told = lax.all_to_all(payload, ("dp", "tp"), 0, 0)
    matrices = (
        qkv_weight,
        qkv_first,
        qkv_second,
        out_weight,
        out_first,
        out_second,
        ffn_in_weight,
        ffn_in_first,
        ffn_in_second,
        ffn_down_weight,
        ffn_down_first,
        ffn_down_second,
    )
    vectors = (norm_gains, gains_first, gains_second, bias_table.T, table_first.T, table_second.T)
    state = matrices + vectors
    shapes = [(m.shape, kind) for m in matrices[::3] for kind in (f32, f32, f32, bf16)]
    norm, *updated = call(
        adam_kernel,
        [
            sds((1, 1), f32),
            *(pltpu.HBM(shape, kind) for shape, kind in shapes),
            *[sds(norm_gains.shape, f32)] * 4,
            *[sds((heads_here, BUCKETS), f32)] * 3,
        ],
        (told, qkvo_grad, in_grad, down_grad, *state),
        "adam",
        hbm=range(4, 22),
        scratch=[
            *(pltpu.VMEM(m.shape, f32) for m in state),
            *(pltpu.VMEM(shape, kind) for shape, kind in shapes),
            pltpu.VMEM(norm_gains.shape, f32),
            pltpu.VMEM((heads_here, BUCKETS), f32),
            pltpu.SemaphoreType.DMA((18,)),
            pltpu.SemaphoreType.DMA((16,)),
        ],
    )
    return (block_out, input_grad, norm.reshape(()), *updated[:-3], *(t.T for t in updated[-3:]))


def solution(mesh):
    row = P("dp", None)
    matrix = P("dp", "tp")
    stack = P(None, "dp", "tp")
    table = P(None, "tp")
    share = P(("dp", "tp"), None)
    in_specs = (
        *(row,) * 3,
        P(),
        *(stack,) * 3,
        *(matrix,) * 9,
        *(P(),) * 3,
        *(table,) * 3,
    )
    out_specs = (
        *(share,) * 2,
        P(),
        *(stack,) * 4,
        *(matrix,) * 12,
        *(P(),) * 4,
        *(table,) * 3,
    )
    return jax.shard_map(
        functools.partial(on_device, mesh.shape["dp"]),
        mesh=mesh,
        in_specs=in_specs,
        out_specs=out_specs,
        check_vma=False,
    )
```

```python
import functools
import math

import jax
import jax.numpy as jnp
from jax import lax
from jax.experimental import pallas as pl
from jax.experimental.pallas import tpu as pltpu
from jax.sharding import PartitionSpec as P

HEADS = 12
HDIM = 64
BUCKETS = 32
LEN = 512
BLK = 128
WIN = LEN + BLK
SMALL = 8
LINES = 16


eps_norm = 1e-06
clip_norm = 1.0
beta_one = 0.9
beta_two = 0.999
adam_eps = 1e-08
decay_rate = 0.01
adam_step = 10.0
mask_fill = -1000000000.0
rate_small = 0.02
rate_large = 0.5
gelu_coef = 0.044715
root_coef = math.sqrt(2.0 / math.pi)

f32 = jnp.float32
bf16 = jnp.bfloat16
sds = jax.ShapeDtypeStruct


def dot_nn(a, b):
    return lax.dot_general(a, b, (((1,), (0,)), ((), ())), preferred_element_type=f32)


def dot_nt(a, b):
    return lax.dot_general(a, b, (((1,), (1,)), ((), ())), preferred_element_type=f32)


def dot_tn(a, b):
    return lax.dot_general(a, b, (((0,), (0,)), ((), ())), preferred_element_type=f32)


def after(value, *deps):
    return lax.optimization_barrier((value, *deps))[0]


def call(body, outs, args, name, hbm=(), scratch=(), limit=16, behind=()):
    spaces = [pl.ANY if i in hbm else pltpu.VMEM for i in range(len(args))]
    args = [after(args[0], *behind), *args[1:]] if behind else args
    args = [
        pltpu.with_memory_space_constraint(a, pltpu.HBM) if i in hbm else a for i, a in enumerate(args)
    ]
    return pl.pallas_call(
        body,
        out_shape=tuple(outs),
        in_specs=[pl.BlockSpec(memory_space=space) for space in spaces],
        out_specs=tuple(
            pl.BlockSpec(memory_space=pl.ANY if hasattr(o, "memory_space") else pltpu.VMEM) for o in outs
        ),
        scratch_shapes=list(scratch),
        compiler_params=pltpu.CompilerParams(vmem_limit_bytes=limit << 20),
        cost_estimate=pl.CostEstimate(flops=0, bytes_accessed=0, transcendentals=0),
        name=name,
    )(*args)


def to_hbm(staged, out, sem):
    copy = pltpu.make_async_copy(staged, out, sem)
    copy.start()
    copy.wait()


def assemble(into, blocks, start_col=0):
    cols = slice(start_col, start_col + into.shape[1])
    if len(blocks) == 1:
        into[...] = blocks[0][:, cols]
        return
    me = lax.axis_index("dp")
    rows = blocks[0].shape[0]
    for e, block in enumerate(blocks):
        start = pl.multiple_of((me ^ e) * rows, 32)
        into[pl.ds(start, rows), :] = block[:, cols]


def spread(grad, outs, order=(1, 2, 4)):
    if len(outs) == 1:
        outs[0][...] = grad[...].astype(bf16)
        return
    me = lax.axis_index("dp")
    rows = outs[0].shape[1]
    keep, *send = outs
    for b in range(2):
        for k in range(4):
            out, at = (keep, k) if b == 0 else (send[0], k) if len(send) == 1 else (send[1 - (k >> 1)], k & 1)
            apart = b * order[0] ^ (k >> 1) * order[1] ^ (k & 1) * order[2]
            start = pl.multiple_of((me ^ apart) * rows, 32)
            block = grad[pl.ds(start, rows), :].astype(bf16)
            if len(out.shape) == 2:
                out[at * rows : (at + 1) * rows, :] = block
            else:
                out[at] = block


def spread_shapes(dp, width, cols, lengths):
    if dp == 8:
        return [sds((n, width // dp, cols), bf16) for n in lengths]
    return [sds((width, cols), bf16)]


def half_rows():
    core = lax.axis_index("tp") & 1
    for half in range(2):
        for at in range(2):
            start = pl.multiple_of(((core ^ half) + 2 * at) * BLK, BLK)
            yield half, at, pl.ds(start, BLK)


def pack_kernel(qkv, out, down, ffn_in, packed, packed_ffn, *scratch):
    *landed, sems = scratch
    copies = [
        pltpu.make_async_copy(source, to, sems.at[i])
        for i, (source, to) in enumerate(zip((qkv, out, down, ffn_in), landed))
    ]
    for copy in copies:
        copy.start()
    local = out.shape[1]
    copies[0].wait()
    copies[1].wait()
    for part in range(3):
        packed[:, part * local : (part + 1) * local] = landed[0][part].astype(bf16)
    packed[:, 3 * local :] = landed[1][...].astype(bf16)
    width = down.shape[1]
    for i in (2, 3):
        copies[i].wait()
        packed_ffn[:, (i - 2) * width : (i - 1) * width] = landed[i][...].astype(bf16)


def prep_kernel(
    seg_in, table_in, bucket_in, x_in, gains_in, dy_in, act, act_t, bias, bucket, x, gains, dy, seg, table, ids, sems
):
    sources = (x_in, gains_in, bucket_in, seg_in, table_in, dy_in)
    copies = [
        pltpu.make_async_copy(source, to, sems.at[i])
        for i, (source, to) in enumerate(zip(sources, (x, gains, ids, seg, table, dy)))
    ]
    for copy in copies:
        copy.start()
    copies[0].wait()
    copies[1].wait()
    values = x[...].astype(f32)
    scale = lax.rsqrt(jnp.mean(values * values, axis=-1, keepdims=True) + eps_norm)
    low = (values * scale * gains[0:1, :]).astype(bf16)
    act[...] = low
    act_t[...] = low.T
    for copy in copies[2:]:
        copy.wait()
    ends = [seg[0, 0]]
    for k in (1, 2):
        ends.append(ends[-1] + seg[0, k])

    def segment_of(position):
        return sum((position >= end).astype(jnp.int32) for end in ends)

    seg_cols = segment_of(lax.broadcasted_iota(jnp.int32, (1, LEN), 1))
    heads = bias.shape[0]
    bucket[...] = jnp.zeros_like(bucket)
    bucket[:, : 2 * LEN - 1] = ids[...]
    lines = []
    for h in range(heads):
        line = jnp.zeros((1, 2 * LEN), f32)
        for b in range(BUCKETS):
            line = jnp.where(bucket[...] == b, table[h, b], line)
        lines.append(line)
    for r in range(LEN // BLK):
        seg_rows = segment_of(lax.broadcasted_iota(jnp.int32, (BLK, 1), 0) + r * BLK)
        visible = seg_rows == seg_cols
        low_at = LEN - BLK - r * BLK
        for h in range(heads):
            window = jnp.broadcast_to(lines[h][:, low_at : low_at + WIN], (BLK, WIN))
            turned = pltpu.roll(window, 1, 1, stride=1, stride_axis=0)
            bias[h, r * BLK : (r + 1) * BLK, :] = jnp.where(visible, turned[:, BLK:], mask_fill)


def attend_kernel(n_blocks, act, bias, *rest):
    blocks = rest[:n_blocks]
    weights, qkv, prob, mixed, keep, send = rest[n_blocks:]
    assemble(weights, blocks)
    width = qkv.shape[1] // 3
    qkv[...] = dot_nn(act[...], weights[:, : 3 * width]).astype(bf16)
    for h in range(bias.shape[0]):
        cols = slice(h * HDIM, (h + 1) * HDIM)
        query, key, value = (qkv[:, s * width + h * HDIM : s * width + (h + 1) * HDIM] for s in range(3))
        scores = dot_nt(query, key) + bias[h]
        top = jnp.max(scores, axis=-1, keepdims=True)
        exps = jnp.exp(scores - top)
        total = jnp.sum(exps, axis=-1, keepdims=True)
        low = (exps * (1.0 / total)).astype(bf16)
        prob[h] = low
        mixed[:, cols] = dot_nn(low, value).astype(bf16)
    out_cols = weights[:, 3 * width :]
    for half, at, rows in half_rows():
        to = send if half else keep
        to[at * BLK : (at + 1) * BLK, :] = dot_nt(mixed[rows, :], out_cols).astype(bf16)


def ffn_kernel(n_blocks, x, gains, dy, own_a, own_b, other_a, other_b, *rest):
    blocks = rest[:n_blocks]
    resid, act, hidden, pre_grad, keep, send, down, weights, hidden_grad = rest[n_blocks:]
    assemble(down, blocks)
    assemble(weights, blocks, down.shape[1])
    hidden_grad[...] = dot_nn(dy[...], down[...])
    for half, at, rows in half_rows():
        here = slice(at * BLK, (at + 1) * BLK)
        attn = ((own_a, own_b), (other_a, other_b))[half][at]
        values = x[rows, :].astype(f32) + attn[...].astype(f32)
        resid[rows, :] = values
        scale = lax.rsqrt(jnp.mean(values * values, axis=-1, keepdims=True) + eps_norm)
        low = (values * scale * gains[1:2, :]).astype(bf16)
        act[rows, :] = low
        u = dot_nn(low, weights[...])
        square = u * u
        tanh_part = jnp.tanh(root_coef * (u + gelu_coef * square * u))
        hidden[rows, :] = (0.5 * u * (1.0 + tanh_part)).astype(bf16)
        inner = root_coef * (1.0 + 3.0 * gelu_coef * square)
        slope = 0.5 * (1.0 + tanh_part) + 0.5 * u * (1.0 - tanh_part * tanh_part) * inner
        du = (hidden_grad[rows, :] * slope).astype(bf16)
        pre_grad[rows, :] = du
        (send if half else keep)[here, :] = dot_nt(du, weights[...]).astype(bf16)


def row_products(weights, grad):
    products = weights.astype(f32) * grad
    width = grad.shape[1]
    folded = sum(products[:, c : c + BLK] for c in range(0, width - BLK + 1, BLK))
    if width % BLK:
        rest = products[:, width - width % BLK :]
        wide = jnp.zeros((grad.shape[0], BLK - width % BLK), f32)
        folded = folded + jnp.concatenate([rest, wide], axis=1)
    return jnp.sum(folded.T, axis=0, keepdims=True)


def down_grad_kernel(order, left, right, *rest):
    outs, grad = rest[:-1], rest[-1]
    grad[...] = dot_tn(left[...], right[...])
    spread(grad, outs, order)


def in_grad_kernel(order, left, right, weights, gains, *rest):
    *outs, gain_part, grad = rest
    grad[...] = dot_tn(left[...], right[...])
    spread(grad, outs, order)
    gain_part[...] = row_products(weights[...], grad[...]) / gains[1:2, :]


def attend_back_kernel(
    n_outs, resid, dy, gains, own, other, weights, qkv, prob, mixed, act_t, bucket, gain_two, *rest
):
    outs = rest[:n_outs]
    share_grad, small, proj_grad, resid_low, grad, diag = rest[n_outs:]
    chip = lax.axis_index("tp") >> 1
    width = qkv.shape[1] // 3
    for half, at, rows in half_rows():
        here = slice(at * BLK, (at + 1) * BLK)
        act_grad = (other if half else own)[here, :].astype(f32)
        values = resid[rows, :]
        scale = lax.rsqrt(jnp.mean(values * values, axis=-1, keepdims=True) + eps_norm)
        normed = values * scale
        normal_grad = act_grad * gains[1:2, :]
        mean_part = jnp.mean(normal_grad * normed, axis=-1, keepdims=True)
        total = dy[rows, :].astype(f32) + scale * (normal_grad - normed * mean_part)
        resid_low[rows, :] = total.astype(bf16)
        if half == 0:

            @pl.when(chip == at)
            def _():
                share_grad[...] = total

    mix_grad = dot_nn(resid_low[...], weights[:, 3 * width :]).astype(bf16)
    heads = prob.shape[0]
    row = lax.broadcasted_iota(jnp.int32, (BLK, BLK), 0)
    col = lax.broadcasted_iota(jnp.int32, (BLK, BLK), 1)
    flip = (row + col == BLK - 1).astype(f32).astype(bf16)
    diag[...] = jnp.zeros_like(diag)
    for h in range(heads):
        query, key, value = (qkv[:, s * width + h * HDIM : s * width + (h + 1) * HDIM] for s in range(3))
        grad_rows = mix_grad[:, h * HDIM : (h + 1) * HDIM]
        prob_grad = dot_nt(grad_rows, value)
        prob_here = prob[h].astype(f32)
        row_dot = jnp.sum(prob_here * prob_grad, axis=-1, keepdims=True)
        low = (prob_here * (prob_grad - row_dot)).astype(bf16)
        for r in range(LEN // BLK):
            flipped = dot_nn(flip, low[r * BLK : (r + 1) * BLK, :])
            wide = jnp.concatenate([flipped, jnp.zeros((BLK, BLK), f32)], axis=1)
            turned = pltpu.roll(wide, 0, 1, stride=1, stride_axis=0)
            low_at = LEN - BLK - r * BLK
            diag[h : h + 1, low_at : low_at + WIN] += jnp.sum(turned, axis=0, keepdims=True)
        for s, part in enumerate((dot_nn(low, key), dot_tn(low, query), dot_tn(prob[h], grad_rows))):
            proj_grad[:, s * width + h * HDIM : s * width + (h + 1) * HDIM] = part.astype(bf16)
    grad[:, : 3 * width] = dot_nn(act_t[...], proj_grad[...])
    grad[:, 3 * width :] = dot_tn(resid_low[...], mixed[...])
    onehot = (lax.broadcasted_iota(jnp.int32, (BUCKETS, 2 * LEN), 0) == bucket[...]).astype(f32)
    by_bucket = lax.dot_general(
        diag[...],
        onehot,
        (((1,), (1,)), ((), ())),
        precision=lax.Precision.HIGHEST,
        preferred_element_type=f32,
    )
    first = lax.axis_index("tp") * heads
    cells = [
        sum(jnp.where(first + h == head, by_bucket[h : h + 1, :], 0.0) for h in range(heads))
        for head in range(HEADS)
    ]
    model = gains.shape[1]
    cells.append(jnp.zeros((1, model - HEADS * BUCKETS), f32))
    gain_one = row_products(weights[:, : 3 * width], grad[:, : 3 * width]) / gains[0:1, :]
    lines = (gain_one, gain_two[...], jnp.concatenate(cells, axis=1), jnp.zeros((SMALL - 3, model), f32))
    whole = jnp.concatenate(lines, axis=0)
    if n_outs == 1:
        spread(grad, outs)
        small[...] = whole
        return
    keep, low = outs
    rows = keep.shape[1]
    spread(grad, (keep, small, low))
    small[2 * rows :, :] = whole.astype(bf16)


def ffn_out_kernel(hidden, down, keep, send):
    for half, at, rows in half_rows():
        to = send if half else keep
        to[at * BLK : (at + 1) * BLK, :] = dot_nt(hidden[rows, :], down[...]).astype(bf16)


def act_grad_kernel(proj_grad, weights, keep, *send):
    width = proj_grad.shape[1]
    for half, at, rows in half_rows():
        block = dot_nt(proj_grad[rows, :], weights[:, :width]).astype(bf16)
        if half:
            send[at][...] = block
        else:
            keep[at * BLK : (at + 1) * BLK, :] = block


def core_add_kernel(ffn_keep, ffn_got, act_keep, act_got_a, act_got_b, mine, theirs):
    chip = lax.axis_index("tp") >> 1
    for at in range(2):
        here = slice(at * BLK, (at + 1) * BLK)
        ffn = (ffn_keep[here, :].astype(f32) + ffn_got[here, :].astype(f32)).astype(bf16)
        got = (act_got_a, act_got_b)[at]
        act = (act_keep[here, :].astype(f32) + got[...].astype(f32)).astype(bf16)

        @pl.when(chip == at)
        def _():
            mine[:BLK, :] = ffn
            mine[BLK:, :] = act

        @pl.when(chip != at)
        def _():
            theirs[:BLK, :] = ffn
            theirs[BLK:, :] = act


def share_out_kernel(resid, x, gains, share_grad, mine, got, block_out, input_grad):
    share = pl.ds(pl.multiple_of(lax.axis_index("tp") * BLK, BLK), BLK)
    first, second = slice(0, BLK), slice(BLK, 2 * BLK)
    ffn = mine[first, :].astype(f32) + got[first, :].astype(f32)
    block_out[...] = (resid[share, :] + ffn).astype(bf16)
    values = x[share, :].astype(f32)
    scale = lax.rsqrt(jnp.mean(values * values, axis=-1, keepdims=True) + eps_norm)
    normed = values * scale
    normal_grad = (mine[second, :].astype(f32) + got[second, :].astype(f32)) * gains[0:1, :]
    mean_part = jnp.mean(normal_grad * normed, axis=-1, keepdims=True)
    input_grad[...] = share_grad[...] + scale * (normal_grad - normed * mean_part)


def add_kernel(one, two, out):
    out[...] = (one[...].astype(f32) + two[...].astype(f32)).astype(bf16)


def split_add_kernel(one, two, *outs):
    for i, out in enumerate(outs):
        rows = slice(i * BLK, (i + 1) * BLK)
        out[...] = (one[rows, :].astype(f32) + two[rows, :].astype(f32)).astype(bf16)


def pair_add_kernel(keep, got, mine, theirs):
    for k in range(4):
        to = theirs if k >= 2 else mine
        to[k % 2] = (keep[k].astype(f32) + got[k].astype(f32)).astype(bf16)


def next_add_kernel(keep, got, mine, theirs):
    for k, to in enumerate((mine, theirs)):
        to[...] = (keep[k].astype(f32) + got[k].astype(f32)).astype(bf16)


def last_high_kernel(keep, sent, got, out):
    rows = keep.shape[1]
    for k in range(2):
        here = slice(k * rows, (k + 1) * rows)
        out[here, :] = (keep[k + 2].astype(f32) + got[here, :].astype(f32)).astype(bf16)
    small = slice(2 * rows, None)
    out[small, :] = (sent[small, :].astype(f32) + got[small, :].astype(f32)).astype(bf16)


def last_late_kernel(keep, got_low, sent, got, mine, out):
    rows = keep.shape[1]
    first, second, small = slice(0, rows), slice(rows, 2 * rows), slice(2 * rows, None)
    mine[...] = keep[0].astype(f32) + got_low[0].astype(f32) + got[first, :].astype(f32)
    block = keep[1].astype(f32) + got_low[1].astype(f32) + got[second, :].astype(f32)
    out[:rows, :] = block.astype(bf16)
    out[rows:, :] = (sent[small, :].astype(f32) + got[small, :].astype(f32)).astype(bf16)


def fold(values):
    rows, cols = values.shape
    squares = values * values
    lanes = sum(squares[:, c : c + BLK] for c in range(0, cols, BLK))
    return jnp.sum(lanes, axis=0, keepdims=True)


def sum_kernel(n_parts, *rest):
    parts, (grad, squares) = rest[:n_parts], rest[n_parts:]
    total = sum(part[...].astype(f32) for part in parts)
    grad[...] = total
    squares[...] = fold(total)


def last_sum_kernel(direct, extra_a, extra_b, *rest):
    *parts, grad, out, payload, lines, sem = rest
    if direct:
        mine, sent, got = parts
        rows = mine.shape[0]
        total = mine[...] + got[:rows, :].astype(f32)
        small = sent[rows:, :].astype(f32) + got[rows:, :].astype(f32)
    else:
        total, small = (part[...] for part in parts)
    grad[...] = total
    per_row = total.shape[1] // BLK
    lines[...] = jnp.zeros_like(lines)
    for line in range(LINES):
        row, at = divmod(line, per_row)
        lines[line : line + 1, :] = small[row : row + 1, at * BLK : (at + 1) * BLK]
    me = lax.axis_index("dp")
    start = pl.multiple_of(jnp.minimum(2 * me, LINES), 2)
    squares = fold(total) + extra_a[...] + extra_b[...]
    two = lines[pl.ds(start, 2), :]
    told = jnp.concatenate((squares, two[0:1, :], two[1:2, :]), axis=1)
    payload[...] = jnp.broadcast_to(told[None], payload.shape)
    to_hbm(payload, out, sem)


def adamw(weight, gradient, moment_one, moment_two, rate):
    one_new = beta_one * moment_one + (1.0 - beta_one) * gradient
    two_new = beta_two * moment_two + (1.0 - beta_two) * gradient * gradient
    root = math.sqrt(1.0 - beta_two**adam_step)
    scale = rate * root / (1.0 - beta_one**adam_step)
    step = scale * one_new / (jnp.sqrt(two_new) + adam_eps * root)
    return (weight * (1.0 - rate * decay_rate) - step, one_new, two_new)


def fetch_kernel(*refs):
    count = len(refs) // 2
    copies = [pltpu.make_async_copy(refs[i], refs[count + i], refs[-1].at[i]) for i in range(count)]
    for copy in copies:
        copy.start()
    for copy in copies:
        copy.wait()


def adam_kernel(*refs):
    told, grad_qkvo, grad_in, grad_down, *state = refs[:22]
    norm_ref, *matrices, gains_a, gains_b, gains_c, gains_grad, table_a, table_b, table_c = refs[22:46]
    gains_sum, table_grad = refs[46:]
    gains_o, table_o = (gains_a, gains_b, gains_c), (table_a, table_b, table_c)
    qkv, out, ffn_in, ffn_down, gains, table = (state[i : i + 3] for i in range(0, 18, 3))
    qkv_o, out_o, in_o, down_o = (matrices[i : i + 4] for i in range(0, 16, 4))
    tp = lax.axis_size("tp")
    squares = told[0, :, :BLK]
    for i in range(1, told.shape[0]):
        squares = squares + told[i, :, :BLK]
    model = gains_sum.shape[1]
    per_row = model // BLK
    per_line = BLK // BUCKETS
    first = lax.axis_index("tp") * table_grad.shape[0]
    for line in range(2 * per_row + HEADS // per_line):
        index, at = divmod(line, 2)
        cols = slice((at + 1) * BLK, (at + 2) * BLK)
        value = told[index * tp, :, cols]
        for i in range(1, tp):
            value = value + told[index * tp + i, :, cols]
        squares = squares + value * value
        row, at = divmod(line, per_row)
        if row < 2:
            gains_sum[row : row + 1, at * BLK : (at + 1) * BLK] = value
            continue
        for i in range(per_line):
            head = at * per_line + i
            cell = value[:, i * BUCKETS : (i + 1) * BUCKETS]
            for h in range(table_grad.shape[0]):

                @pl.when(first + h == head)
                def _():
                    table_grad[h : h + 1, :] = cell

    norm = jnp.sqrt(jnp.sum(squares, axis=1, keepdims=True))
    norm_ref[...] = norm
    factor = clip_norm / jnp.maximum(norm, clip_norm)

    def update(state_refs, gradient, to, rate, at=...):
        new = adamw(state_refs[0][at], gradient * factor, state_refs[1][at], state_refs[2][at], rate)
        for ref, value in zip(to, new):
            ref[at] = value
        if len(to) == 4:
            to[3][at] = new[0].astype(bf16)

    update(ffn_in, grad_in[...], in_o, rate_small)
    update(ffn_down, grad_down[...], down_o, rate_small)
    width = qkv[0].shape[2]
    for part in range(3):
        update(qkv, grad_qkvo[:, part * width : (part + 1) * width], qkv_o, rate_small, part)
    update(out, grad_qkvo[:, 3 * width :], out_o, rate_large)
    update(gains, gains_sum[...], gains_o, rate_large)
    gains_grad[...] = gains_sum[...] * factor
    update(table, table_grad[...], table_o, rate_large)


def on_device(
    dp,
    inputs,
    cotangent,
    seg_lengths,
    bucket_ids,
    qkv_weight,
    qkv_first,
    qkv_second,
    out_weight,
    out_first,
    out_second,
    ffn_in_weight,
    ffn_in_first,
    ffn_in_second,
    ffn_down_weight,
    ffn_down_first,
    ffn_down_second,
    norm_gains,
    gains_first,
    gains_second,
    bias_table,
    table_first,
    table_second,
):
    tokens, model = inputs.shape
    rows, local = out_weight.shape
    hidden = ffn_in_weight.shape[1]
    heads_here = local // HDIM
    tp = lax.axis_size("tp")
    packed_cols = 4 * local
    direct = dp == 8

    def swap_dp(value, distance):
        return lax.ppermute(value, "dp", [(i, i ^ distance) for i in range(dp)])

    def swap_tp(value, distance):
        return lax.ppermute(value, "tp", [(i, i ^ distance) for i in range(tp)])

    def add(one, two, behind=()):
        (out,) = call(add_kernel, [sds(one.shape, bf16)], (one, two), "add", limit=4, behind=behind)
        return out

    def pair_add(keep, got, behind):
        outs = [sds((2, *keep.shape[1:]), bf16)] * 2
        return call(pair_add_kernel, outs, (keep, got), "pair_add", limit=4, behind=behind)

    def next_add(keep, got, behind):
        outs = [sds(keep.shape[1:], bf16)] * 2
        return call(next_add_kernel, outs, (keep, got), "next_add", limit=4, behind=behind)

    half_shape = [sds((tokens // 2, model), bf16)] * 2
    matrices = (qkv_weight, out_weight, ffn_down_weight, ffn_in_weight)
    packed, packed_ffn = call(
        pack_kernel,
        [sds((rows, packed_cols), bf16), sds((rows, 2 * hidden), bf16)],
        matrices,
        "pack",
        hbm=(0, 1, 2, 3),
        scratch=[*(pltpu.VMEM(m.shape, f32) for m in matrices), pltpu.SemaphoreType.DMA((4,))],
    )
    ids = bucket_ids[None, :]
    act_one, act_one_t, bias, bucket_row, inputs, norm_gains_here, cotangent = call(
        prep_kernel,
        [
            sds((tokens, model), bf16),
            sds((model, tokens), bf16),
            sds((heads_here, LEN, LEN), f32),
            sds((1, 2 * LEN), jnp.int32),
            sds(inputs.shape, bf16),
            sds(norm_gains.shape, f32),
            sds(inputs.shape, bf16),
        ],
        (seg_lengths, bias_table.T, ids, inputs, norm_gains, cotangent),
        "prep",
        hbm=range(6),
        scratch=[
            pltpu.SMEM(seg_lengths.shape, jnp.int32),
            pltpu.SMEM((heads_here, BUCKETS), f32),
            pltpu.VMEM(ids.shape, jnp.int32),
            pltpu.SemaphoreType.DMA((6,)),
        ],
    )
    if direct:
        one, two = swap_dp(packed, 2), swap_dp(packed, 4)
        own, ffn_own = swap_dp(after(packed, act_one), 1), swap_dp(after(packed_ffn, act_one), 1)
        one_across = swap_dp(one, 1)
        three = swap_dp(two, 2)
        ffn_two = swap_dp(after(packed_ffn, two), 4)
        two_across = swap_dp(two, 1)
        ffn_one = swap_dp(after(packed_ffn, three, own, one_across), 2)
        three_across = swap_dp(three, 1)
        qkvo_blocks = [packed, own, one, one_across, two, two_across, three, three_across]
        ffn_three = swap_dp(after(ffn_two, ffn_one), 2)
        ffn_blocks = [packed_ffn, ffn_own, ffn_one, swap_dp(after(ffn_own, ffn_three), 2)]
        for block in (ffn_two, ffn_three):
            ffn_blocks += [block, swap_dp(block, 1)]
        bias = after(bias, ffn_own, ffn_two)
        ffn_early = (ffn_blocks[5], ffn_three)
    else:
        qkvo_blocks = [lax.all_gather(packed, "dp", axis=0, tiled=True)]
        ffn_blocks = ffn_early = [lax.all_gather(packed_ffn, "dp", axis=0, tiled=True)]
    n_blocks = len(qkvo_blocks)

    weights_one, qkv, prob, mixed, attn_keep, attn_send = call(
        functools.partial(attend_kernel, n_blocks),
        [
            sds((model, packed_cols), bf16),
            sds((tokens, 3 * local), bf16),
            sds((heads_here, LEN, LEN), bf16),
            sds((tokens, local), bf16),
            *half_shape,
        ],
        (act_one, bias, *qkvo_blocks),
        "attend",
    )
    half_blocks = [sds((BLK, model), bf16)] * 2
    attn_first = call(
        split_add_kernel, half_blocks, (attn_keep, swap_tp(attn_send, 1)), "split_add", limit=4
    )
    attn_own = [add(first, swap_tp(first, 2), ffn_early) for first in attn_first]
    attn_sums = (*attn_own, *(swap_tp(own, 1) for own in attn_own))
    resid, act_two, hidden_act, pre_grad, back_keep, back_send, down_full, in_full = call(
        functools.partial(ffn_kernel, n_blocks),
        [
            sds((tokens, model), f32),
            sds((tokens, model), bf16),
            sds((tokens, hidden), bf16),
            sds((tokens, hidden), bf16),
            *half_shape,
            *[sds((model, hidden), bf16)] * 2,
        ],
        (inputs, norm_gains_here, cotangent, *attn_sums, *ffn_blocks),
        "ffn",
        scratch=[pltpu.VMEM((tokens, hidden), f32)],
    )
    back_first = add(back_keep, swap_tp(back_send, 1))
    back_got = swap_tp(back_first, 2)
    down_order, in_order = (1, 2, 4), (2, 4, 1)
    grad_scratch = [pltpu.VMEM((model, hidden), f32)]
    down_parts = call(
        functools.partial(down_grad_kernel, down_order),
        spread_shapes(dp, model, hidden, (4, 4)),
        (cotangent, after(hidden_act, back_first)),
        "down_grad",
        scratch=grad_scratch,
    )
    *in_parts, gain_two_part = call(
        functools.partial(in_grad_kernel, in_order),
        [*spread_shapes(dp, model, hidden, (4, 4)), sds((1, model), f32)],
        (act_two, after(pre_grad, down_parts[0]), in_full, norm_gains_here),
        "in_grad",
        scratch=grad_scratch,
    )
    ffn_keep, ffn_send = call(
        ffn_out_kernel, half_shape, (hidden_act, down_full), "ffn_out", behind=(gain_two_part,)
    )
    back_sum = add(back_first, back_got, (ffn_keep,))
    everyone = dp * tp
    qkvo_shapes = spread_shapes(dp, model, packed_cols, (4, 2))
    small_shape = sds((2 * rows + SMALL, model), bf16) if direct else sds((SMALL, model), f32)
    *qkvo_parts, share_grad, small, proj_grad = call(
        functools.partial(attend_back_kernel, len(qkvo_shapes)),
        [*qkvo_shapes, sds((BLK, model), f32), small_shape, sds((tokens, 3 * local), bf16)],
        (
            resid,
            cotangent,
            norm_gains_here,
            back_sum,
            swap_tp(back_sum, 1),
            weights_one,
            qkv,
            prob,
            mixed,
            act_one_t,
            bucket_row,
            gain_two_part,
        ),
        "attend_back",
        scratch=[
            pltpu.VMEM((tokens, model), bf16),
            pltpu.VMEM((model, packed_cols), f32),
            pltpu.VMEM((8, 2 * LEN), f32),
        ],
    )
    def summed(parts, behind):
        return call(
            functools.partial(sum_kernel, len(parts)),
            [sds((rows, parts[0].shape[1]), f32), sds((1, BLK), f32)],
            parts,
            "sum_parts",
            limit=4,
            behind=behind,
        )

    def act_shares(behind):
        keep, *send = call(
            act_grad_kernel,
            [half_shape[0], *half_blocks],
            (proj_grad, weights_one),
            "act_grad",
            behind=behind,
        )
        return keep, [swap_tp(part, 1) for part in send]

    def share_sums(keep, got, behind):
        outs = [sds((2 * BLK, model), bf16)] * 2
        args = (ffn_keep, swap_tp(ffn_send, 1), keep, *got)
        return call(core_add_kernel, outs, args, "core_add", limit=4, behind=behind)

    if direct:
        keep, send_low = qkvo_parts
        down_keep, down_send = down_parts
        in_keep, in_send = in_parts
        in_one = pair_add(in_keep, swap_dp(in_send, in_order[0]), (proj_grad,))
        down_one = pair_add(down_keep, swap_dp(down_send, down_order[0]), in_one)
        got_high = swap_dp(after(small, *down_one), 1)
        share_own, share_got = act_shares(down_one)
        (high,) = call(
            last_high_kernel, [small_shape], (keep, small, got_high), "last_high", limit=4, behind=(share_own,)
        )
        got_low = swap_dp(after(send_low, high), 1)
        mine, theirs = share_sums(share_own, share_got, (high,))
        down_two = next_add(down_one[0], swap_dp(down_one[1], down_order[1]), (mine,))
        in_two = next_add(in_one[0], swap_dp(in_one[1], in_order[1]), down_two)
        down_grad, down_squares = summed((down_two[0], swap_dp(down_two[1], down_order[2])), in_two)
        in_grad, in_squares = summed((in_two[0], swap_dp(in_two[1], in_order[2])), (down_grad,))
        last, late = call(
            last_late_kernel,
            [sds((rows, packed_cols), f32), sds((rows + SMALL, packed_cols), bf16)],
            (keep, got_low, high, swap_dp(high, 2)),
            "last_late",
            limit=4,
            behind=(in_grad,),
        )
        last_parts = (last, late, swap_dp(late, 4))
        share_behind = (late,)
    else:
        qkvo_sums, down_sums, in_sums = (
            (lax.psum_scatter(p[0].astype(f32), "dp", scatter_dimension=0, tiled=True),)
            for p in (qkvo_parts, down_parts, in_parts)
        )
        last_parts = (*qkvo_sums, lax.psum(small, "dp"))
        down_grad, down_squares = summed(down_sums, ())
        in_grad, in_squares = summed(in_sums, ())
        mine, theirs = share_sums(*act_shares(()), ())
        share_behind = ()
    block_out, input_grad = call(
        share_out_kernel,
        [sds((BLK, model), bf16), sds((BLK, model), f32)],
        (resid, inputs, norm_gains_here, share_grad, mine, swap_tp(theirs, 2)),
        "share_out",
        behind=share_behind,
    )
    matrices = (
        qkv_weight,
        qkv_first,
        qkv_second,
        out_weight,
        out_first,
        out_second,
        ffn_in_weight,
        ffn_in_first,
        ffn_in_second,
        ffn_down_weight,
        ffn_down_first,
        ffn_down_second,
    )
    vectors = (norm_gains, gains_first, gains_second, bias_table.T, table_first.T, table_second.T)
    state = matrices + vectors
    fetched = call(
        fetch_kernel,
        [sds(m.shape, f32) for m in state],
        state,
        "fetch",
        hbm=range(18),
        scratch=[pltpu.SemaphoreType.DMA((18,))],
        limit=4,
        behind=(block_out,),
    )
    qkvo_grad, payload = call(
        functools.partial(last_sum_kernel, direct),
        [sds((rows, packed_cols), f32), pltpu.HBM((everyone, 1, 3 * BLK), f32)],
        (down_squares, in_squares, *last_parts),
        "last_sum",
        scratch=[
            pltpu.VMEM((everyone, 1, 3 * BLK), f32),
            pltpu.VMEM((LINES + 8, BLK), f32),
            pltpu.SemaphoreType.DMA,
        ],
        behind=(fetched[0],),
    )
    told = lax.all_to_all(payload, ("dp", "tp"), 0, 0)
    shapes = [(m.shape, kind) for m in matrices[::3] for kind in (f32, f32, f32, bf16)]
    norm, *updated = call(
        adam_kernel,
        [
            sds((1, 1), f32),
            *(sds(shape, kind) for shape, kind in shapes),
            *[sds(norm_gains.shape, f32)] * 4,
            *[sds((heads_here, BUCKETS), f32)] * 3,
        ],
        (told, qkvo_grad, in_grad, down_grad, *fetched),
        "adam",
        scratch=[pltpu.VMEM(norm_gains.shape, f32), pltpu.VMEM((heads_here, BUCKETS), f32)],
    )
    return (block_out, input_grad, norm.reshape(()), *updated[:-3], *(t.T for t in updated[-3:]))


def solution(mesh):
    row = P("dp", None)
    matrix = P("dp", "tp")
    stack = P(None, "dp", "tp")
    table = P(None, "tp")
    share = P(("dp", "tp"), None)
    in_specs = (
        *(row,) * 3,
        P(),
        *(stack,) * 3,
        *(matrix,) * 9,
        *(P(),) * 3,
        *(table,) * 3,
    )
    out_specs = (
        *(share,) * 2,
        P(),
        *(stack,) * 4,
        *(matrix,) * 12,
        *(P(),) * 4,
        *(table,) * 3,
    )
    return jax.shard_map(
        functools.partial(on_device, mesh.shape["dp"]),
        mesh=mesh,
        in_specs=in_specs,
        out_specs=out_specs,
        check_vma=False,
    )
```

```python
import functools
import math

import jax
import jax.numpy as jnp
from jax import lax
from jax.experimental import pallas as pl
from jax.experimental.pallas import tpu as pltpu
from jax.sharding import PartitionSpec as P

HEADS = 12
HDIM = 64
BUCKETS = 32
LEN = 512
BLK = 128
WIN = LEN + BLK
SMALL = 8
LINES = 16


eps_norm = 1e-06
clip_norm = 1.0
beta_one = 0.9
beta_two = 0.999
adam_eps = 1e-08
decay_rate = 0.01
adam_step = 10.0
mask_fill = -1000000000.0
rate_small = 0.02
rate_large = 0.5
gelu_coef = 0.044715
root_coef = math.sqrt(2.0 / math.pi)

f32 = jnp.float32
bf16 = jnp.bfloat16
sds = jax.ShapeDtypeStruct


def dot_nn(a, b):
    return lax.dot_general(a, b, (((1,), (0,)), ((), ())), preferred_element_type=f32)


def dot_nt(a, b):
    return lax.dot_general(a, b, (((1,), (1,)), ((), ())), preferred_element_type=f32)


def dot_tn(a, b):
    return lax.dot_general(a, b, (((0,), (0,)), ((), ())), preferred_element_type=f32)


def after(value, *deps):
    return lax.optimization_barrier((value, *deps))[0]


def call(body, outs, args, name, hbm=(), scratch=(), limit=16, behind=()):
    spaces = [pl.ANY if i in hbm else pltpu.VMEM for i in range(len(args))]
    args = [after(args[0], *behind), *args[1:]] if behind else args
    args = [
        pltpu.with_memory_space_constraint(a, pltpu.HBM) if i in hbm else a for i, a in enumerate(args)
    ]
    return pl.pallas_call(
        body,
        out_shape=tuple(outs),
        in_specs=[pl.BlockSpec(memory_space=space) for space in spaces],
        out_specs=tuple(
            pl.BlockSpec(memory_space=pl.ANY if hasattr(o, "memory_space") else pltpu.VMEM) for o in outs
        ),
        scratch_shapes=list(scratch),
        compiler_params=pltpu.CompilerParams(vmem_limit_bytes=limit << 20),
        cost_estimate=pl.CostEstimate(flops=0, bytes_accessed=0, transcendentals=0),
        name=name,
    )(*args)


def to_hbm(staged, out, sem):
    copy = pltpu.make_async_copy(staged, out, sem)
    copy.start()
    copy.wait()


def assemble(into, blocks, start_col=0):
    cols = slice(start_col, start_col + into.shape[1])
    if len(blocks) == 1:
        into[...] = blocks[0][:, cols]
        return
    me = lax.axis_index("dp")
    rows = blocks[0].shape[0]
    for e, block in enumerate(blocks):
        start = pl.multiple_of((me ^ e) * rows, 32)
        into[pl.ds(start, rows), :] = block[:, cols]


def spread(grad, outs, order=(1, 2, 4)):
    if len(outs) == 1:
        outs[0][...] = grad[...].astype(bf16)
        return
    me = lax.axis_index("dp")
    rows = outs[0].shape[1]
    keep, *send = outs
    for b in range(2):
        for k in range(4):
            out, at = (keep, k) if b == 0 else (send[0], k) if len(send) == 1 else (send[1 - (k >> 1)], k & 1)
            apart = b * order[0] ^ (k >> 1) * order[1] ^ (k & 1) * order[2]
            start = pl.multiple_of((me ^ apart) * rows, 32)
            block = grad[pl.ds(start, rows), :].astype(bf16)
            if len(out.shape) == 2:
                out[at * rows : (at + 1) * rows, :] = block
            else:
                out[at] = block


def spread_shapes(dp, width, cols, lengths):
    if dp == 8:
        return [sds((n, width // dp, cols), bf16) for n in lengths]
    return [sds((width, cols), bf16)]


def half_rows():
    core = lax.axis_index("tp") & 1
    for half in range(2):
        for at in range(2):
            start = pl.multiple_of(((core ^ half) + 2 * at) * BLK, BLK)
            yield half, at, pl.ds(start, BLK)


def pack_kernel(qkv, out, down, ffn_in, packed, packed_ffn, *scratch):
    *landed, sems = scratch
    copies = [
        pltpu.make_async_copy(source, to, sems.at[i])
        for i, (source, to) in enumerate(zip((qkv, out, down, ffn_in), landed))
    ]
    for copy in copies:
        copy.start()
    local = out.shape[1]
    copies[0].wait()
    copies[1].wait()
    for part in range(3):
        packed[:, part * local : (part + 1) * local] = landed[0][part].astype(bf16)
    packed[:, 3 * local :] = landed[1][...].astype(bf16)
    width = down.shape[1]
    for i in (2, 3):
        copies[i].wait()
        packed_ffn[:, (i - 2) * width : (i - 1) * width] = landed[i][...].astype(bf16)


def prep_kernel(
    seg_in, table_in, bucket_in, x_in, gains_in, dy_in, act, act_t, bias, bucket, x, gains, dy, seg, table, ids, sems
):
    sources = (x_in, gains_in, bucket_in, seg_in, table_in, dy_in)
    copies = [
        pltpu.make_async_copy(source, to, sems.at[i])
        for i, (source, to) in enumerate(zip(sources, (x, gains, ids, seg, table, dy)))
    ]
    for copy in copies:
        copy.start()
    copies[0].wait()
    copies[1].wait()
    values = x[...].astype(f32)
    scale = lax.rsqrt(jnp.mean(values * values, axis=-1, keepdims=True) + eps_norm)
    low = (values * scale * gains[0:1, :]).astype(bf16)
    act[...] = low
    act_t[...] = low.T
    for copy in copies[2:]:
        copy.wait()
    ends = [seg[0, 0]]
    for k in (1, 2):
        ends.append(ends[-1] + seg[0, k])

    def segment_of(position):
        return sum((position >= end).astype(jnp.int32) for end in ends)

    seg_cols = segment_of(lax.broadcasted_iota(jnp.int32, (1, LEN), 1))
    heads = bias.shape[0]
    bucket[...] = jnp.zeros_like(bucket)
    bucket[:, : 2 * LEN - 1] = ids[...]
    lines = []
    for h in range(heads):
        line = jnp.zeros((1, 2 * LEN), f32)
        for b in range(BUCKETS):
            line = jnp.where(bucket[...] == b, table[h, b], line)
        lines.append(line)
    for r in range(LEN // BLK):
        seg_rows = segment_of(lax.broadcasted_iota(jnp.int32, (BLK, 1), 0) + r * BLK)
        visible = seg_rows == seg_cols
        low_at = LEN - BLK - r * BLK
        for h in range(heads):
            window = jnp.broadcast_to(lines[h][:, low_at : low_at + WIN], (BLK, WIN))
            turned = pltpu.roll(window, 1, 1, stride=1, stride_axis=0)
            bias[h, r * BLK : (r + 1) * BLK, :] = jnp.where(visible, turned[:, BLK:], mask_fill)


def attend_kernel(n_blocks, act, bias, *rest):
    blocks = rest[:n_blocks]
    weights, qkv, prob, mixed, keep, send = rest[n_blocks:]
    assemble(weights, blocks)
    width = qkv.shape[1] // 3
    qkv[...] = dot_nn(act[...], weights[:, : 3 * width]).astype(bf16)
    for h in range(bias.shape[0]):
        cols = slice(h * HDIM, (h + 1) * HDIM)
        query, key, value = (qkv[:, s * width + h * HDIM : s * width + (h + 1) * HDIM] for s in range(3))
        scores = dot_nt(query, key) + bias[h]
        top = jnp.max(scores, axis=-1, keepdims=True)
        exps = jnp.exp(scores - top)
        total = jnp.sum(exps, axis=-1, keepdims=True)
        low = (exps * (1.0 / total)).astype(bf16)
        prob[h] = low
        mixed[:, cols] = dot_nn(low, value).astype(bf16)
    out_cols = weights[:, 3 * width :]
    for half, at, rows in half_rows():
        to = send if half else keep
        to[at * BLK : (at + 1) * BLK, :] = dot_nt(mixed[rows, :], out_cols).astype(bf16)


def ffn_kernel(n_blocks, x, gains, dy, own_a, own_b, other_a, other_b, *rest):
    blocks = rest[:n_blocks]
    resid, act, hidden, pre_grad, keep, send, down, weights, hidden_grad = rest[n_blocks:]
    assemble(down, blocks)
    assemble(weights, blocks, down.shape[1])
    hidden_grad[...] = dot_nn(dy[...], down[...])
    for half, at, rows in half_rows():
        here = slice(at * BLK, (at + 1) * BLK)
        attn = ((own_a, own_b), (other_a, other_b))[half][at]
        values = x[rows, :].astype(f32) + attn[...].astype(f32)
        resid[rows, :] = values
        scale = lax.rsqrt(jnp.mean(values * values, axis=-1, keepdims=True) + eps_norm)
        low = (values * scale * gains[1:2, :]).astype(bf16)
        act[rows, :] = low
        u = dot_nn(low, weights[...])
        square = u * u
        tanh_part = jnp.tanh(root_coef * (u + gelu_coef * square * u))
        hidden[rows, :] = (0.5 * u * (1.0 + tanh_part)).astype(bf16)
        inner = root_coef * (1.0 + 3.0 * gelu_coef * square)
        slope = 0.5 * (1.0 + tanh_part) + 0.5 * u * (1.0 - tanh_part * tanh_part) * inner
        du = (hidden_grad[rows, :] * slope).astype(bf16)
        pre_grad[rows, :] = du
        (send if half else keep)[here, :] = dot_nt(du, weights[...]).astype(bf16)


def row_products(weights, grad):
    products = weights.astype(f32) * grad
    width = grad.shape[1]
    folded = sum(products[:, c : c + BLK] for c in range(0, width - BLK + 1, BLK))
    if width % BLK:
        rest = products[:, width - width % BLK :]
        wide = jnp.zeros((grad.shape[0], BLK - width % BLK), f32)
        folded = folded + jnp.concatenate([rest, wide], axis=1)
    return jnp.sum(folded.T, axis=0, keepdims=True)


def down_grad_kernel(order, left, right, *rest):
    outs, grad = rest[:-1], rest[-1]
    grad[...] = dot_tn(left[...], right[...])
    spread(grad, outs, order)


def in_grad_kernel(order, left, right, weights, gains, *rest):
    *outs, gain_part, grad = rest
    grad[...] = dot_tn(left[...], right[...])
    spread(grad, outs, order)
    gain_part[...] = row_products(weights[...], grad[...]) / gains[1:2, :]


def attend_back_kernel(
    n_outs, resid, dy, gains, own, other, weights, qkv, prob, mixed, act_t, bucket, gain_two, *rest
):
    outs = rest[:n_outs]
    share_grad, small, proj_grad, resid_low, grad, diag = rest[n_outs:]
    chip = lax.axis_index("tp") >> 1
    width = qkv.shape[1] // 3
    for half, at, rows in half_rows():
        here = slice(at * BLK, (at + 1) * BLK)
        act_grad = (other if half else own)[here, :].astype(f32)
        values = resid[rows, :]
        scale = lax.rsqrt(jnp.mean(values * values, axis=-1, keepdims=True) + eps_norm)
        normed = values * scale
        normal_grad = act_grad * gains[1:2, :]
        mean_part = jnp.mean(normal_grad * normed, axis=-1, keepdims=True)
        total = dy[rows, :].astype(f32) + scale * (normal_grad - normed * mean_part)
        resid_low[rows, :] = total.astype(bf16)
        if half == 0:

            @pl.when(chip == at)
            def _():
                share_grad[...] = total

    mix_grad = dot_nn(resid_low[...], weights[:, 3 * width :]).astype(bf16)
    heads = prob.shape[0]
    row = lax.broadcasted_iota(jnp.int32, (BLK, BLK), 0)
    col = lax.broadcasted_iota(jnp.int32, (BLK, BLK), 1)
    flip = (row + col == BLK - 1).astype(f32).astype(bf16)
    diag[...] = jnp.zeros_like(diag)
    for h in range(heads):
        query, key, value = (qkv[:, s * width + h * HDIM : s * width + (h + 1) * HDIM] for s in range(3))
        grad_rows = mix_grad[:, h * HDIM : (h + 1) * HDIM]
        prob_grad = dot_nt(grad_rows, value)
        prob_here = prob[h].astype(f32)
        row_dot = jnp.sum(prob_here * prob_grad, axis=-1, keepdims=True)
        low = (prob_here * (prob_grad - row_dot)).astype(bf16)
        for r in range(LEN // BLK):
            flipped = dot_nn(flip, low[r * BLK : (r + 1) * BLK, :])
            wide = jnp.concatenate([flipped, jnp.zeros((BLK, BLK), f32)], axis=1)
            turned = pltpu.roll(wide, 0, 1, stride=1, stride_axis=0)
            low_at = LEN - BLK - r * BLK
            diag[h : h + 1, low_at : low_at + WIN] += jnp.sum(turned, axis=0, keepdims=True)
        for s, part in enumerate((dot_nn(low, key), dot_tn(low, query), dot_tn(prob[h], grad_rows))):
            proj_grad[:, s * width + h * HDIM : s * width + (h + 1) * HDIM] = part.astype(bf16)
    grad[:, : 3 * width] = dot_nn(act_t[...], proj_grad[...])
    grad[:, 3 * width :] = dot_tn(resid_low[...], mixed[...])
    onehot = (lax.broadcasted_iota(jnp.int32, (BUCKETS, 2 * LEN), 0) == bucket[...]).astype(f32)
    by_bucket = lax.dot_general(
        diag[...],
        onehot,
        (((1,), (1,)), ((), ())),
        precision=lax.Precision.HIGHEST,
        preferred_element_type=f32,
    )
    first = lax.axis_index("tp") * heads
    cells = [
        sum(jnp.where(first + h == head, by_bucket[h : h + 1, :], 0.0) for h in range(heads))
        for head in range(HEADS)
    ]
    model = gains.shape[1]
    cells.append(jnp.zeros((1, model - HEADS * BUCKETS), f32))
    gain_one = row_products(weights[:, : 3 * width], grad[:, : 3 * width]) / gains[0:1, :]
    lines = (gain_one, gain_two[...], jnp.concatenate(cells, axis=1), jnp.zeros((SMALL - 3, model), f32))
    whole = jnp.concatenate(lines, axis=0)
    if n_outs == 1:
        spread(grad, outs)
        small[...] = whole
        return
    keep, low = outs
    rows = keep.shape[1]
    spread(grad, (keep, small, low))
    small[2 * rows :, :] = whole.astype(bf16)


def ffn_out_kernel(hidden, down, keep, *send):
    for half, at, rows in half_rows():
        block = dot_nt(hidden[rows, :], down[...]).astype(bf16)
        if half:
            send[at][...] = block
        else:
            keep[at * BLK : (at + 1) * BLK, :] = block


def act_grad_kernel(proj_grad, weights, keep, *send):
    width = proj_grad.shape[1]
    for half, at, rows in half_rows():
        block = dot_nt(proj_grad[rows, :], weights[:, :width]).astype(bf16)
        if half:
            send[at][...] = block
        else:
            keep[at * BLK : (at + 1) * BLK, :] = block


def core_add_kernel(*refs):
    *before, keep, got_a, got_b, mine, theirs = refs
    chip = lax.axis_index("tp") >> 1
    first = mine.shape[0] - BLK
    for to, block in zip((mine, theirs), before):
        to[:BLK, :] = block[...]
    for at, got in enumerate((got_a, got_b)):
        here = slice(at * BLK, (at + 1) * BLK)
        value = (keep[here, :].astype(f32) + got[...].astype(f32)).astype(bf16)

        @pl.when(chip == at)
        def _():
            mine[first:, :] = value

        @pl.when(chip != at)
        def _():
            theirs[first:, :] = value


def share_out_kernel(resid, x, gains, share_grad, mine, got, block_out, input_grad):
    share = pl.ds(pl.multiple_of(lax.axis_index("tp") * BLK, BLK), BLK)
    first, second = slice(0, BLK), slice(BLK, 2 * BLK)
    ffn = mine[first, :].astype(f32) + got[first, :].astype(f32)
    block_out[...] = (resid[share, :] + ffn).astype(bf16)
    values = x[share, :].astype(f32)
    scale = lax.rsqrt(jnp.mean(values * values, axis=-1, keepdims=True) + eps_norm)
    normed = values * scale
    normal_grad = (mine[second, :].astype(f32) + got[second, :].astype(f32)) * gains[0:1, :]
    mean_part = jnp.mean(normal_grad * normed, axis=-1, keepdims=True)
    input_grad[...] = share_grad[...] + scale * (normal_grad - normed * mean_part)


def add_kernel(one, two, out):
    out[...] = (one[...].astype(f32) + two[...].astype(f32)).astype(bf16)


def split_add_kernel(one, two, *outs):
    for i, out in enumerate(outs):
        rows = slice(i * BLK, (i + 1) * BLK)
        out[...] = (one[rows, :].astype(f32) + two[rows, :].astype(f32)).astype(bf16)


def pair_add_kernel(keep, got, mine, theirs):
    for k in range(4):
        to = theirs if k >= 2 else mine
        to[k % 2] = (keep[k].astype(f32) + got[k].astype(f32)).astype(bf16)


def next_add_kernel(keep, got, mine, theirs):
    for k, to in enumerate((mine, theirs)):
        to[...] = (keep[k].astype(f32) + got[k].astype(f32)).astype(bf16)


def last_high_kernel(keep, sent, got, out):
    rows = keep.shape[1]
    for k in range(2):
        here = slice(k * rows, (k + 1) * rows)
        out[here, :] = (keep[k + 2].astype(f32) + got[here, :].astype(f32)).astype(bf16)
    small = slice(2 * rows, None)
    out[small, :] = (sent[small, :].astype(f32) + got[small, :].astype(f32)).astype(bf16)


def last_late_kernel(keep, got_low, sent, got, mine, out):
    rows = keep.shape[1]
    first, second, small = slice(0, rows), slice(rows, 2 * rows), slice(2 * rows, None)
    mine[...] = keep[0].astype(f32) + got_low[0].astype(f32) + got[first, :].astype(f32)
    block = keep[1].astype(f32) + got_low[1].astype(f32) + got[second, :].astype(f32)
    out[:rows, :] = block.astype(bf16)
    out[rows:, :] = (sent[small, :].astype(f32) + got[small, :].astype(f32)).astype(bf16)


def fold(values):
    rows, cols = values.shape
    squares = values * values
    lanes = sum(squares[:, c : c + BLK] for c in range(0, cols, BLK))
    return jnp.sum(lanes, axis=0, keepdims=True)


def sum_kernel(n_parts, *rest):
    parts, (grad, squares) = rest[:n_parts], rest[n_parts:]
    total = sum(part[...].astype(f32) for part in parts)
    grad[...] = total
    squares[...] = fold(total)


def last_sum_kernel(direct, extra_a, extra_b, *rest):
    *parts, grad, out, payload, lines, sem = rest
    if direct:
        mine, sent, got = parts
        rows = mine.shape[0]
        total = mine[...] + got[:rows, :].astype(f32)
        small = sent[rows:, :].astype(f32) + got[rows:, :].astype(f32)
    else:
        total, small = (part[...] for part in parts)
    grad[...] = total
    per_row = total.shape[1] // BLK
    lines[...] = jnp.zeros_like(lines)
    for line in range(LINES):
        row, at = divmod(line, per_row)
        lines[line : line + 1, :] = small[row : row + 1, at * BLK : (at + 1) * BLK]
    me = lax.axis_index("dp")
    start = pl.multiple_of(jnp.minimum(2 * me, LINES), 2)
    squares = fold(total) + extra_a[...] + extra_b[...]
    two = lines[pl.ds(start, 2), :]
    told = jnp.concatenate((squares, two[0:1, :], two[1:2, :]), axis=1)
    payload[...] = jnp.broadcast_to(told[None], payload.shape)
    to_hbm(payload, out, sem)


def adamw(weight, gradient, moment_one, moment_two, rate):
    one_new = beta_one * moment_one + (1.0 - beta_one) * gradient
    two_new = beta_two * moment_two + (1.0 - beta_two) * gradient * gradient
    root = math.sqrt(1.0 - beta_two**adam_step)
    scale = rate * root / (1.0 - beta_one**adam_step)
    step = scale * one_new / (jnp.sqrt(two_new) + adam_eps * root)
    return (weight * (1.0 - rate * decay_rate) - step, one_new, two_new)


def fetch_kernel(*refs):
    count = len(refs) // 2
    copies = [pltpu.make_async_copy(refs[i], refs[count + i], refs[-1].at[i]) for i in range(count)]
    for copy in copies:
        copy.start()
    for copy in copies:
        copy.wait()


def adam_kernel(*refs):
    told, grad_qkvo, grad_in, grad_down, *state = refs[:22]
    norm_ref, *matrices, gains_a, gains_b, gains_c, gains_grad, table_a, table_b, table_c = refs[22:46]
    gains_sum, table_grad = refs[46:]
    gains_o, table_o = (gains_a, gains_b, gains_c), (table_a, table_b, table_c)
    qkv, out, ffn_in, ffn_down, gains, table = (state[i : i + 3] for i in range(0, 18, 3))
    qkv_o, out_o, in_o, down_o = (matrices[i : i + 4] for i in range(0, 16, 4))
    tp = lax.axis_size("tp")
    squares = told[0, :, :BLK]
    for i in range(1, told.shape[0]):
        squares = squares + told[i, :, :BLK]
    model = gains_sum.shape[1]
    per_row = model // BLK
    per_line = BLK // BUCKETS
    first = lax.axis_index("tp") * table_grad.shape[0]
    for line in range(2 * per_row + HEADS // per_line):
        index, at = divmod(line, 2)
        cols = slice((at + 1) * BLK, (at + 2) * BLK)
        value = told[index * tp, :, cols]
        for i in range(1, tp):
            value = value + told[index * tp + i, :, cols]
        squares = squares + value * value
        row, at = divmod(line, per_row)
        if row < 2:
            gains_sum[row : row + 1, at * BLK : (at + 1) * BLK] = value
            continue
        for i in range(per_line):
            head = at * per_line + i
            cell = value[:, i * BUCKETS : (i + 1) * BUCKETS]
            for h in range(table_grad.shape[0]):

                @pl.when(first + h == head)
                def _():
                    table_grad[h : h + 1, :] = cell

    norm = jnp.sqrt(jnp.sum(squares, axis=1, keepdims=True))
    norm_ref[...] = norm
    factor = clip_norm / jnp.maximum(norm, clip_norm)

    def update(state_refs, gradient, to, rate, at=...):
        new = adamw(state_refs[0][at], gradient * factor, state_refs[1][at], state_refs[2][at], rate)
        for ref, value in zip(to, new):
            ref[at] = value
        if len(to) == 4:
            to[3][at] = new[0].astype(bf16)

    update(ffn_in, grad_in[...], in_o, rate_small)
    update(ffn_down, grad_down[...], down_o, rate_small)
    width = qkv[0].shape[2]
    for part in range(3):
        update(qkv, grad_qkvo[:, part * width : (part + 1) * width], qkv_o, rate_small, part)
    update(out, grad_qkvo[:, 3 * width :], out_o, rate_large)
    update(gains, gains_sum[...], gains_o, rate_large)
    gains_grad[...] = gains_sum[...] * factor
    update(table, table_grad[...], table_o, rate_large)


def on_device(
    dp,
    inputs,
    cotangent,
    seg_lengths,
    bucket_ids,
    qkv_weight,
    qkv_first,
    qkv_second,
    out_weight,
    out_first,
    out_second,
    ffn_in_weight,
    ffn_in_first,
    ffn_in_second,
    ffn_down_weight,
    ffn_down_first,
    ffn_down_second,
    norm_gains,
    gains_first,
    gains_second,
    bias_table,
    table_first,
    table_second,
):
    tokens, model = inputs.shape
    rows, local = out_weight.shape
    hidden = ffn_in_weight.shape[1]
    heads_here = local // HDIM
    tp = lax.axis_size("tp")
    packed_cols = 4 * local
    direct = dp == 8

    def swap_dp(value, distance):
        return lax.ppermute(value, "dp", [(i, i ^ distance) for i in range(dp)])

    def swap_tp(value, distance):
        return lax.ppermute(value, "tp", [(i, i ^ distance) for i in range(tp)])

    def add(one, two, behind=()):
        (out,) = call(add_kernel, [sds(one.shape, bf16)], (one, two), "add", limit=4, behind=behind)
        return out

    def pair_add(keep, got, behind):
        outs = [sds((2, *keep.shape[1:]), bf16)] * 2
        return call(pair_add_kernel, outs, (keep, got), "pair_add", limit=4, behind=behind)

    def next_add(keep, got, behind):
        outs = [sds(keep.shape[1:], bf16)] * 2
        return call(next_add_kernel, outs, (keep, got), "next_add", limit=4, behind=behind)

    half_shape = [sds((tokens // 2, model), bf16)] * 2
    matrices = (qkv_weight, out_weight, ffn_down_weight, ffn_in_weight)
    packed, packed_ffn = call(
        pack_kernel,
        [sds((rows, packed_cols), bf16), sds((rows, 2 * hidden), bf16)],
        matrices,
        "pack",
        hbm=(0, 1, 2, 3),
        scratch=[*(pltpu.VMEM(m.shape, f32) for m in matrices), pltpu.SemaphoreType.DMA((4,))],
    )
    ids = bucket_ids[None, :]
    act_one, act_one_t, bias, bucket_row, inputs, norm_gains_here, cotangent = call(
        prep_kernel,
        [
            sds((tokens, model), bf16),
            sds((model, tokens), bf16),
            sds((heads_here, LEN, LEN), f32),
            sds((1, 2 * LEN), jnp.int32),
            sds(inputs.shape, bf16),
            sds(norm_gains.shape, f32),
            sds(inputs.shape, bf16),
        ],
        (seg_lengths, bias_table.T, ids, inputs, norm_gains, cotangent),
        "prep",
        hbm=range(6),
        scratch=[
            pltpu.SMEM(seg_lengths.shape, jnp.int32),
            pltpu.SMEM((heads_here, BUCKETS), f32),
            pltpu.VMEM(ids.shape, jnp.int32),
            pltpu.SemaphoreType.DMA((6,)),
        ],
    )
    if direct:
        one, two = swap_dp(packed, 2), swap_dp(packed, 4)
        own, ffn_own = swap_dp(after(packed, act_one), 1), swap_dp(after(packed_ffn, act_one), 1)
        one_across = swap_dp(one, 1)
        three = swap_dp(two, 2)
        ffn_two = swap_dp(after(packed_ffn, two), 4)
        two_across = swap_dp(two, 1)
        ffn_one = swap_dp(after(packed_ffn, three, own, one_across), 2)
        three_across = swap_dp(three, 1)
        qkvo_blocks = [packed, own, one, one_across, two, two_across, three, three_across]
        ffn_three = swap_dp(after(ffn_two, ffn_one), 2)
        ffn_blocks = [packed_ffn, ffn_own, ffn_one, swap_dp(after(ffn_own, ffn_three), 2)]
        for block in (ffn_two, ffn_three):
            ffn_blocks += [block, swap_dp(block, 1)]
        bias = after(bias, ffn_own, ffn_two)
        ffn_early = (ffn_blocks[5], ffn_three)
    else:
        qkvo_blocks = [lax.all_gather(packed, "dp", axis=0, tiled=True)]
        ffn_blocks = ffn_early = [lax.all_gather(packed_ffn, "dp", axis=0, tiled=True)]
    n_blocks = len(qkvo_blocks)

    weights_one, qkv, prob, mixed, attn_keep, attn_send = call(
        functools.partial(attend_kernel, n_blocks),
        [
            sds((model, packed_cols), bf16),
            sds((tokens, 3 * local), bf16),
            sds((heads_here, LEN, LEN), bf16),
            sds((tokens, local), bf16),
            *half_shape,
        ],
        (act_one, bias, *qkvo_blocks),
        "attend",
    )
    half_blocks = [sds((BLK, model), bf16)] * 2
    attn_first = call(
        split_add_kernel, half_blocks, (attn_keep, swap_tp(attn_send, 1)), "split_add", limit=4
    )
    attn_own = [add(first, swap_tp(first, 2), ffn_early) for first in attn_first]
    attn_sums = (*attn_own, *(swap_tp(own, 1) for own in attn_own))
    resid, act_two, hidden_act, pre_grad, back_keep, back_send, down_full, in_full = call(
        functools.partial(ffn_kernel, n_blocks),
        [
            sds((tokens, model), f32),
            sds((tokens, model), bf16),
            sds((tokens, hidden), bf16),
            sds((tokens, hidden), bf16),
            *half_shape,
            *[sds((model, hidden), bf16)] * 2,
        ],
        (inputs, norm_gains_here, cotangent, *attn_sums, *ffn_blocks),
        "ffn",
        scratch=[pltpu.VMEM((tokens, hidden), f32)],
    )
    down_order, in_order = (2, 1, 4), (1, 2, 4)
    grad_scratch = [pltpu.VMEM((model, hidden), f32)]
    down_parts = call(
        functools.partial(down_grad_kernel, down_order),
        spread_shapes(dp, model, hidden, (4, 4)),
        (cotangent, hidden_act),
        "down_grad",
        scratch=grad_scratch,
    )
    back_first = add(back_keep, swap_tp(back_send, 1), down_parts[:1])
    back_got = swap_tp(back_first, 2)
    *in_parts, gain_two_part = call(
        functools.partial(in_grad_kernel, in_order),
        [*spread_shapes(dp, model, hidden, (4, 4)), sds((1, model), f32)],
        (act_two, after(pre_grad, back_first), in_full, norm_gains_here),
        "in_grad",
        scratch=grad_scratch,
    )
    share_shapes = [half_shape[0], *half_blocks]
    ffn_keep, *ffn_send = call(
        ffn_out_kernel, share_shapes, (hidden_act, down_full), "ffn_out", behind=(gain_two_part,)
    )
    ffn_got = [swap_tp(part, 1) for part in ffn_send]
    ffn_sums = call(core_add_kernel, half_blocks, (ffn_keep, *ffn_got), "ffn_add", limit=4)
    back_sum = add(back_first, back_got, ffn_sums[:1])
    attend_behind = ()
    if direct:
        down_keep, down_send = down_parts
        down_one = pair_add(down_keep, swap_dp(down_send, down_order[0]), (back_sum,))
        attend_behind = down_one
    everyone = dp * tp
    qkvo_shapes = spread_shapes(dp, model, packed_cols, (4, 2))
    small_shape = sds((2 * rows + SMALL, model), bf16) if direct else sds((SMALL, model), f32)
    *qkvo_parts, share_grad, small, proj_grad = call(
        functools.partial(attend_back_kernel, len(qkvo_shapes)),
        [*qkvo_shapes, sds((BLK, model), f32), small_shape, sds((tokens, 3 * local), bf16)],
        (
            resid,
            cotangent,
            norm_gains_here,
            back_sum,
            swap_tp(back_sum, 1),
            weights_one,
            qkv,
            prob,
            mixed,
            act_one_t,
            bucket_row,
            gain_two_part,
        ),
        "attend_back",
        scratch=[
            pltpu.VMEM((tokens, model), bf16),
            pltpu.VMEM((model, packed_cols), f32),
            pltpu.VMEM((8, 2 * LEN), f32),
        ],
        behind=attend_behind,
    )
    def summed(parts, behind):
        return call(
            functools.partial(sum_kernel, len(parts)),
            [sds((rows, parts[0].shape[1]), f32), sds((1, BLK), f32)],
            parts,
            "sum_parts",
            limit=4,
            behind=behind,
        )

    def act_shares(behind):
        keep, *send = call(
            act_grad_kernel, share_shapes, (proj_grad, weights_one), "act_grad", behind=behind
        )
        return (keep, *(swap_tp(part, 1) for part in send))

    def share_sums(shares, behind):
        outs = [sds((2 * BLK, model), bf16)] * 2
        return call(core_add_kernel, outs, (*ffn_sums, *shares), "core_add", limit=4, behind=behind)

    if direct:
        keep, send_low = qkvo_parts
        in_keep, in_send = in_parts
        in_one = pair_add(in_keep, swap_dp(in_send, in_order[0]), (proj_grad,))
        got_high = swap_dp(after(small, *in_one), 1)
        act_parts = act_shares(in_one)
        down_two = next_add(down_one[0], swap_dp(down_one[1], down_order[1]), act_parts[:1])
        (high,) = call(
            last_high_kernel, [small_shape], (keep, small, got_high), "last_high", limit=4, behind=down_two
        )
        got_low = swap_dp(after(send_low, high), 1)
        down_grad, down_squares = summed((down_two[0], swap_dp(down_two[1], down_order[2])), (high,))
        in_two = next_add(in_one[0], swap_dp(in_one[1], in_order[1]), (down_grad,))
        mine, theirs = share_sums(act_parts, in_two)
        in_grad, in_squares = summed((in_two[0], swap_dp(in_two[1], in_order[2])), (mine,))
        last, late = call(
            last_late_kernel,
            [sds((rows, packed_cols), f32), sds((rows + SMALL, packed_cols), bf16)],
            (keep, got_low, high, swap_dp(high, 2)),
            "last_late",
            limit=4,
            behind=(in_grad,),
        )
        last_parts = (last, late, swap_dp(late, 4))
        share_behind = (late,)
    else:
        qkvo_sums, down_sums, in_sums = (
            (lax.psum_scatter(p[0].astype(f32), "dp", scatter_dimension=0, tiled=True),)
            for p in (qkvo_parts, down_parts, in_parts)
        )
        last_parts = (*qkvo_sums, lax.psum(small, "dp"))
        down_grad, down_squares = summed(down_sums, ())
        in_grad, in_squares = summed(in_sums, ())
        mine, theirs = share_sums(act_shares(()), ())
        share_behind = ()
    block_out, input_grad = call(
        share_out_kernel,
        [sds((BLK, model), bf16), sds((BLK, model), f32)],
        (resid, inputs, norm_gains_here, share_grad, mine, swap_tp(theirs, 2)),
        "share_out",
        behind=share_behind,
    )
    matrices = (
        qkv_weight,
        qkv_first,
        qkv_second,
        out_weight,
        out_first,
        out_second,
        ffn_in_weight,
        ffn_in_first,
        ffn_in_second,
        ffn_down_weight,
        ffn_down_first,
        ffn_down_second,
    )
    vectors = (norm_gains, gains_first, gains_second, bias_table.T, table_first.T, table_second.T)
    state = matrices + vectors
    fetched = call(
        fetch_kernel,
        [sds(m.shape, f32) for m in state],
        state,
        "fetch",
        hbm=range(18),
        scratch=[pltpu.SemaphoreType.DMA((18,))],
        limit=4,
        behind=(block_out,),
    )
    qkvo_grad, payload = call(
        functools.partial(last_sum_kernel, direct),
        [sds((rows, packed_cols), f32), pltpu.HBM((everyone, 1, 3 * BLK), f32)],
        (down_squares, in_squares, *last_parts),
        "last_sum",
        scratch=[
            pltpu.VMEM((everyone, 1, 3 * BLK), f32),
            pltpu.VMEM((LINES + 8, BLK), f32),
            pltpu.SemaphoreType.DMA,
        ],
        behind=(fetched[0],),
    )
    told = lax.all_to_all(payload, ("dp", "tp"), 0, 0)
    shapes = [(m.shape, kind) for m in matrices[::3] for kind in (f32, f32, f32, bf16)]
    norm, *updated = call(
        adam_kernel,
        [
            sds((1, 1), f32),
            *(sds(shape, kind) for shape, kind in shapes),
            *[sds(norm_gains.shape, f32)] * 4,
            *[sds((heads_here, BUCKETS), f32)] * 3,
        ],
        (told, qkvo_grad, in_grad, down_grad, *fetched),
        "adam",
        scratch=[pltpu.VMEM(norm_gains.shape, f32), pltpu.VMEM((heads_here, BUCKETS), f32)],
    )
    return (block_out, input_grad, norm.reshape(()), *updated[:-3], *(t.T for t in updated[-3:]))


def solution(mesh):
    row = P("dp", None)
    matrix = P("dp", "tp")
    stack = P(None, "dp", "tp")
    table = P(None, "tp")
    share = P(("dp", "tp"), None)
    in_specs = (
        *(row,) * 3,
        P(),
        *(stack,) * 3,
        *(matrix,) * 9,
        *(P(),) * 3,
        *(table,) * 3,
    )
    out_specs = (
        *(share,) * 2,
        P(),
        *(stack,) * 4,
        *(matrix,) * 12,
        *(P(),) * 4,
        *(table,) * 3,
    )
    return jax.shard_map(
        functools.partial(on_device, mesh.shape["dp"]),
        mesh=mesh,
        in_specs=in_specs,
        out_specs=out_specs,
        check_vma=False,
    )
```

```python
import functools
import math

import jax
import jax.numpy as jnp
from jax import lax
from jax.experimental import pallas as pl
from jax.experimental.pallas import tpu as pltpu
from jax.sharding import PartitionSpec as P

HEADS = 12
HDIM = 64
BUCKETS = 32
LEN = 512
BLK = 128
WIN = LEN + BLK
SMALL = 8
LINES = 16


eps_norm = 1e-06
clip_norm = 1.0
beta_one = 0.9
beta_two = 0.999
adam_eps = 1e-08
decay_rate = 0.01
adam_step = 10.0
mask_fill = -1000000000.0
rate_small = 0.02
rate_large = 0.5
gelu_coef = 0.044715
root_coef = math.sqrt(2.0 / math.pi)

f32 = jnp.float32
bf16 = jnp.bfloat16
sds = jax.ShapeDtypeStruct


def dot_nn(a, b):
    return lax.dot_general(a, b, (((1,), (0,)), ((), ())), preferred_element_type=f32)


def dot_nt(a, b):
    return lax.dot_general(a, b, (((1,), (1,)), ((), ())), preferred_element_type=f32)


def dot_tn(a, b):
    return lax.dot_general(a, b, (((0,), (0,)), ((), ())), preferred_element_type=f32)


def after(value, *deps):
    return lax.optimization_barrier((value, *deps))[0]


def call(body, outs, args, name, hbm=(), scratch=(), limit=16, behind=()):
    spaces = [pl.ANY if i in hbm else pltpu.VMEM for i in range(len(args))]
    args = [after(args[0], *behind), *args[1:]] if behind else args
    args = [
        pltpu.with_memory_space_constraint(a, pltpu.HBM) if i in hbm else a for i, a in enumerate(args)
    ]
    return pl.pallas_call(
        body,
        out_shape=tuple(outs),
        in_specs=[pl.BlockSpec(memory_space=space) for space in spaces],
        out_specs=tuple(
            pl.BlockSpec(memory_space=pl.ANY if hasattr(o, "memory_space") else pltpu.VMEM) for o in outs
        ),
        scratch_shapes=list(scratch),
        compiler_params=pltpu.CompilerParams(vmem_limit_bytes=limit << 20),
        cost_estimate=pl.CostEstimate(flops=0, bytes_accessed=0, transcendentals=0),
        name=name,
    )(*args)


def to_hbm(staged, out, sem):
    copy = pltpu.make_async_copy(staged, out, sem)
    copy.start()
    copy.wait()


def assemble(into, blocks, start_col=0):
    cols = slice(start_col, start_col + into.shape[1])
    if len(blocks) == 1:
        into[...] = blocks[0][:, cols]
        return
    me = lax.axis_index("dp")
    rows = blocks[0].shape[0]
    for e, block in enumerate(blocks):
        start = pl.multiple_of((me ^ e) * rows, 32)
        into[pl.ds(start, rows), :] = block[:, cols]


def spread(grad, outs, order=(1, 2, 4)):
    if len(outs) == 1:
        outs[0][...] = grad[...].astype(bf16)
        return
    me = lax.axis_index("dp")
    rows = outs[0].shape[1]
    keep, *send = outs
    for b in range(2):
        for k in range(4):
            out, at = (keep, k) if b == 0 else (send[0], k) if len(send) == 1 else (send[1 - (k >> 1)], k & 1)
            apart = b * order[0] ^ (k >> 1) * order[1] ^ (k & 1) * order[2]
            start = pl.multiple_of((me ^ apart) * rows, 32)
            block = grad[pl.ds(start, rows), :].astype(bf16)
            if len(out.shape) == 2:
                out[at * rows : (at + 1) * rows, :] = block
            else:
                out[at] = block


def spread_shapes(dp, width, cols, lengths):
    if dp == 8:
        return [sds((n, width // dp, cols), bf16) for n in lengths]
    return [sds((width, cols), bf16)]


def half_rows():
    core = lax.axis_index("tp") & 1
    for half in range(2):
        for at in range(2):
            start = pl.multiple_of(((core ^ half) + 2 * at) * BLK, BLK)
            yield half, at, pl.ds(start, BLK)


def pack_kernel(qkv, out, down, ffn_in, packed, packed_ffn, *scratch):
    *landed, sems = scratch
    copies = [
        pltpu.make_async_copy(source, to, sems.at[i])
        for i, (source, to) in enumerate(zip((qkv, out, down, ffn_in), landed))
    ]
    for copy in copies:
        copy.start()
    local = out.shape[1]
    copies[0].wait()
    copies[1].wait()
    for part in range(3):
        packed[:, part * local : (part + 1) * local] = landed[0][part].astype(bf16)
    packed[:, 3 * local :] = landed[1][...].astype(bf16)
    width = down.shape[1]
    for i in (2, 3):
        copies[i].wait()
        packed_ffn[:, (i - 2) * width : (i - 1) * width] = landed[i][...].astype(bf16)


def prep_kernel(
    seg_in, table_in, bucket_in, x_in, gains_in, dy_in, act, act_t, bias, bucket, x, gains, dy, seg, table, ids, sems
):
    sources = (x_in, gains_in, bucket_in, seg_in, table_in, dy_in)
    copies = [
        pltpu.make_async_copy(source, to, sems.at[i])
        for i, (source, to) in enumerate(zip(sources, (x, gains, ids, seg, table, dy)))
    ]
    for copy in copies:
        copy.start()
    copies[0].wait()
    copies[1].wait()
    values = x[...].astype(f32)
    scale = lax.rsqrt(jnp.mean(values * values, axis=-1, keepdims=True) + eps_norm)
    low = (values * scale * gains[0:1, :]).astype(bf16)
    act[...] = low
    act_t[...] = low.T
    for copy in copies[2:]:
        copy.wait()
    ends = [seg[0, 0]]
    for k in (1, 2):
        ends.append(ends[-1] + seg[0, k])

    def segment_of(position):
        return sum((position >= end).astype(jnp.int32) for end in ends)

    seg_cols = segment_of(lax.broadcasted_iota(jnp.int32, (1, LEN), 1))
    heads = bias.shape[0]
    bucket[...] = jnp.zeros_like(bucket)
    bucket[:, : 2 * LEN - 1] = ids[...]
    lines = []
    for h in range(heads):
        line = jnp.zeros((1, 2 * LEN), f32)
        for b in range(BUCKETS):
            line = jnp.where(bucket[...] == b, table[h, b], line)
        lines.append(line)
    for r in range(LEN // BLK):
        seg_rows = segment_of(lax.broadcasted_iota(jnp.int32, (BLK, 1), 0) + r * BLK)
        visible = seg_rows == seg_cols
        low_at = LEN - BLK - r * BLK
        for h in range(heads):
            window = jnp.broadcast_to(lines[h][:, low_at : low_at + WIN], (BLK, WIN))
            turned = pltpu.roll(window, 1, 1, stride=1, stride_axis=0)
            bias[h, r * BLK : (r + 1) * BLK, :] = jnp.where(visible, turned[:, BLK:], mask_fill)


def attend_kernel(n_blocks, act, bias, *rest):
    blocks = rest[:n_blocks]
    weights, qkv, prob, mixed, keep, send = rest[n_blocks:]
    assemble(weights, blocks)
    width = qkv.shape[1] // 3
    qkv[...] = dot_nn(act[...], weights[:, : 3 * width]).astype(bf16)
    for h in range(bias.shape[0]):
        cols = slice(h * HDIM, (h + 1) * HDIM)
        query, key, value = (qkv[:, s * width + h * HDIM : s * width + (h + 1) * HDIM] for s in range(3))
        scores = dot_nt(query, key) + bias[h]
        top = jnp.max(scores, axis=-1, keepdims=True)
        exps = jnp.exp(scores - top)
        total = jnp.sum(exps, axis=-1, keepdims=True)
        low = (exps * (1.0 / total)).astype(bf16)
        prob[h] = low
        mixed[:, cols] = dot_nn(low, value).astype(bf16)
    out_cols = weights[:, 3 * width :]
    for half, at, rows in half_rows():
        to = send if half else keep
        to[at * BLK : (at + 1) * BLK, :] = dot_nt(mixed[rows, :], out_cols).astype(bf16)


def ffn_kernel(n_blocks, x, gains, dy, own_a, own_b, other_a, other_b, *rest):
    blocks = rest[:n_blocks]
    resid, act, hidden, pre_grad, keep, send, down, weights, hidden_grad = rest[n_blocks:]
    assemble(down, blocks)
    assemble(weights, blocks, down.shape[1])
    hidden_grad[...] = dot_nn(dy[...], down[...])
    for half, at, rows in half_rows():
        here = slice(at * BLK, (at + 1) * BLK)
        attn = ((own_a, own_b), (other_a, other_b))[half][at]
        values = x[rows, :].astype(f32) + attn[...].astype(f32)
        resid[rows, :] = values
        scale = lax.rsqrt(jnp.mean(values * values, axis=-1, keepdims=True) + eps_norm)
        low = (values * scale * gains[1:2, :]).astype(bf16)
        act[rows, :] = low
        u = dot_nn(low, weights[...])
        square = u * u
        tanh_part = jnp.tanh(root_coef * (u + gelu_coef * square * u))
        hidden[rows, :] = (0.5 * u * (1.0 + tanh_part)).astype(bf16)
        inner = root_coef * (1.0 + 3.0 * gelu_coef * square)
        slope = 0.5 * (1.0 + tanh_part) + 0.5 * u * (1.0 - tanh_part * tanh_part) * inner
        du = (hidden_grad[rows, :] * slope).astype(bf16)
        pre_grad[rows, :] = du
        (send if half else keep)[here, :] = dot_nt(du, weights[...]).astype(bf16)


def row_products(weights, grad):
    products = weights.astype(f32) * grad
    width = grad.shape[1]
    folded = sum(products[:, c : c + BLK] for c in range(0, width - BLK + 1, BLK))
    if width % BLK:
        rest = products[:, width - width % BLK :]
        wide = jnp.zeros((grad.shape[0], BLK - width % BLK), f32)
        folded = folded + jnp.concatenate([rest, wide], axis=1)
    return jnp.sum(folded.T, axis=0, keepdims=True)


def down_grad_kernel(order, left, right, *rest):
    outs, grad = rest[:-1], rest[-1]
    grad[...] = dot_tn(left[...], right[...])
    spread(grad, outs, order)


def in_grad_kernel(order, left, right, weights, gains, *rest):
    *outs, gain_part, grad = rest
    grad[...] = dot_tn(left[...], right[...])
    spread(grad, outs, order)
    gain_part[...] = row_products(weights[...], grad[...]) / gains[1:2, :]


def attend_back_kernel(
    n_outs, resid, dy, gains, own, other, weights, qkv, prob, mixed, act_t, bucket, gain_two, *rest
):
    outs = rest[:n_outs]
    share_grad, small, proj_grad, resid_low, grad, diag = rest[n_outs:]
    chip = lax.axis_index("tp") >> 1
    width = qkv.shape[1] // 3
    for half, at, rows in half_rows():
        here = slice(at * BLK, (at + 1) * BLK)
        act_grad = (other if half else own)[here, :].astype(f32)
        values = resid[rows, :]
        scale = lax.rsqrt(jnp.mean(values * values, axis=-1, keepdims=True) + eps_norm)
        normed = values * scale
        normal_grad = act_grad * gains[1:2, :]
        mean_part = jnp.mean(normal_grad * normed, axis=-1, keepdims=True)
        total = dy[rows, :].astype(f32) + scale * (normal_grad - normed * mean_part)
        resid_low[rows, :] = total.astype(bf16)
        if half == 0:

            @pl.when(chip == at)
            def _():
                share_grad[...] = total

    mix_grad = dot_nn(resid_low[...], weights[:, 3 * width :]).astype(bf16)
    heads = prob.shape[0]
    row = lax.broadcasted_iota(jnp.int32, (BLK, BLK), 0)
    col = lax.broadcasted_iota(jnp.int32, (BLK, BLK), 1)
    flip = (row + col == BLK - 1).astype(f32).astype(bf16)
    diag[...] = jnp.zeros_like(diag)
    for h in range(heads):
        query, key, value = (qkv[:, s * width + h * HDIM : s * width + (h + 1) * HDIM] for s in range(3))
        grad_rows = mix_grad[:, h * HDIM : (h + 1) * HDIM]
        prob_grad = dot_nt(grad_rows, value)
        prob_here = prob[h].astype(f32)
        row_dot = jnp.sum(prob_here * prob_grad, axis=-1, keepdims=True)
        low = (prob_here * (prob_grad - row_dot)).astype(bf16)
        for r in range(LEN // BLK):
            flipped = dot_nn(flip, low[r * BLK : (r + 1) * BLK, :])
            wide = jnp.concatenate([flipped, jnp.zeros((BLK, BLK), f32)], axis=1)
            turned = pltpu.roll(wide, 0, 1, stride=1, stride_axis=0)
            low_at = LEN - BLK - r * BLK
            diag[h : h + 1, low_at : low_at + WIN] += jnp.sum(turned, axis=0, keepdims=True)
        for s, part in enumerate((dot_nn(low, key), dot_tn(low, query), dot_tn(prob[h], grad_rows))):
            proj_grad[:, s * width + h * HDIM : s * width + (h + 1) * HDIM] = part.astype(bf16)
    grad[:, : 3 * width] = dot_nn(act_t[...], proj_grad[...])
    grad[:, 3 * width :] = dot_tn(resid_low[...], mixed[...])
    onehot = (lax.broadcasted_iota(jnp.int32, (BUCKETS, 2 * LEN), 0) == bucket[...]).astype(f32)
    by_bucket = lax.dot_general(
        diag[...],
        onehot,
        (((1,), (1,)), ((), ())),
        precision=lax.Precision.HIGHEST,
        preferred_element_type=f32,
    )
    first = lax.axis_index("tp") * heads
    cells = [
        sum(jnp.where(first + h == head, by_bucket[h : h + 1, :], 0.0) for h in range(heads))
        for head in range(HEADS)
    ]
    model = gains.shape[1]
    cells.append(jnp.zeros((1, model - HEADS * BUCKETS), f32))
    gain_one = row_products(weights[:, : 3 * width], grad[:, : 3 * width]) / gains[0:1, :]
    lines = (gain_one, gain_two[...], jnp.concatenate(cells, axis=1), jnp.zeros((SMALL - 3, model), f32))
    whole = jnp.concatenate(lines, axis=0)
    if n_outs == 1:
        spread(grad, outs)
        small[...] = whole
        return
    keep, low = outs
    rows = keep.shape[1]
    spread(grad, (keep, small, low))
    small[2 * rows :, :] = whole.astype(bf16)


def ffn_out_kernel(hidden, down, keep, *send):
    for half, at, rows in half_rows():
        block = dot_nt(hidden[rows, :], down[...]).astype(bf16)
        if half:
            send[at][...] = block
        else:
            keep[at * BLK : (at + 1) * BLK, :] = block


def act_grad_kernel(proj_grad, weights, keep, *send):
    width = proj_grad.shape[1]
    for half, at, rows in half_rows():
        block = dot_nt(proj_grad[rows, :], weights[:, :width]).astype(bf16)
        if half:
            send[at][...] = block
        else:
            keep[at * BLK : (at + 1) * BLK, :] = block


def core_add_kernel(*refs):
    *before, keep, got_a, got_b, mine, theirs = refs
    chip = lax.axis_index("tp") >> 1
    first = mine.shape[0] - BLK
    for to, block in zip((mine, theirs), before):
        to[:BLK, :] = block[...]
    for at, got in enumerate((got_a, got_b)):
        here = slice(at * BLK, (at + 1) * BLK)
        value = (keep[here, :].astype(f32) + got[...].astype(f32)).astype(bf16)

        @pl.when(chip == at)
        def _():
            mine[first:, :] = value

        @pl.when(chip != at)
        def _():
            theirs[first:, :] = value


def share_out_kernel(resid, x, gains, share_grad, mine, got, block_out, input_grad):
    share = pl.ds(pl.multiple_of(lax.axis_index("tp") * BLK, BLK), BLK)
    first, second = slice(0, BLK), slice(BLK, 2 * BLK)
    ffn = mine[first, :].astype(f32) + got[first, :].astype(f32)
    block_out[...] = (resid[share, :] + ffn).astype(bf16)
    values = x[share, :].astype(f32)
    scale = lax.rsqrt(jnp.mean(values * values, axis=-1, keepdims=True) + eps_norm)
    normed = values * scale
    normal_grad = (mine[second, :].astype(f32) + got[second, :].astype(f32)) * gains[0:1, :]
    mean_part = jnp.mean(normal_grad * normed, axis=-1, keepdims=True)
    input_grad[...] = share_grad[...] + scale * (normal_grad - normed * mean_part)


def add_kernel(one, two, out):
    out[...] = (one[...].astype(f32) + two[...].astype(f32)).astype(bf16)


def split_add_kernel(one, two, *outs):
    for i, out in enumerate(outs):
        rows = slice(i * BLK, (i + 1) * BLK)
        out[...] = (one[rows, :].astype(f32) + two[rows, :].astype(f32)).astype(bf16)


def pair_add_kernel(keep, got, mine, theirs):
    for k in range(4):
        to = theirs if k >= 2 else mine
        to[k % 2] = (keep[k].astype(f32) + got[k].astype(f32)).astype(bf16)


def high_add_kernel(keep, got, theirs):
    for k in range(2):
        theirs[k] = (keep[k + 2].astype(f32) + got[k].astype(f32)).astype(bf16)


def late_add_kernel(keep, got_low, got, mine, theirs):
    for k, to in enumerate((mine, theirs)):
        to[...] = (keep[k].astype(f32) + got_low[k].astype(f32) + got[k].astype(f32)).astype(bf16)


def next_add_kernel(keep, got, mine, theirs):
    for k, to in enumerate((mine, theirs)):
        to[...] = (keep[k].astype(f32) + got[k].astype(f32)).astype(bf16)


def last_high_kernel(keep, sent, got, out):
    rows = keep.shape[1]
    for k in range(2):
        here = slice(k * rows, (k + 1) * rows)
        out[here, :] = (keep[k + 2].astype(f32) + got[here, :].astype(f32)).astype(bf16)
    small = slice(2 * rows, None)
    out[small, :] = (sent[small, :].astype(f32) + got[small, :].astype(f32)).astype(bf16)


def last_late_kernel(keep, got_low, sent, got, mine, out):
    rows = keep.shape[1]
    first, second, small = slice(0, rows), slice(rows, 2 * rows), slice(2 * rows, None)
    mine[...] = keep[0].astype(f32) + got_low[0].astype(f32) + got[first, :].astype(f32)
    block = keep[1].astype(f32) + got_low[1].astype(f32) + got[second, :].astype(f32)
    out[:rows, :] = block.astype(bf16)
    out[rows:, :] = (sent[small, :].astype(f32) + got[small, :].astype(f32)).astype(bf16)


def fold(values):
    rows, cols = values.shape
    squares = values * values
    lanes = sum(squares[:, c : c + BLK] for c in range(0, cols, BLK))
    return jnp.sum(lanes, axis=0, keepdims=True)


def sum_kernel(n_parts, *rest):
    parts, (grad, squares) = rest[:n_parts], rest[n_parts:]
    total = sum(part[...].astype(f32) for part in parts)
    grad[...] = total
    squares[...] = fold(total)


def last_sum_kernel(direct, extra_a, extra_b, *rest):
    *parts, grad, out, payload, lines, sem = rest
    if direct:
        mine, sent, got = parts
        rows = mine.shape[0]
        total = mine[...] + got[:rows, :].astype(f32)
        small = sent[rows:, :].astype(f32) + got[rows:, :].astype(f32)
    else:
        total, small = (part[...] for part in parts)
    grad[...] = total
    per_row = total.shape[1] // BLK
    lines[...] = jnp.zeros_like(lines)
    for line in range(LINES):
        row, at = divmod(line, per_row)
        lines[line : line + 1, :] = small[row : row + 1, at * BLK : (at + 1) * BLK]
    me = lax.axis_index("dp")
    start = pl.multiple_of(jnp.minimum(2 * me, LINES), 2)
    squares = fold(total) + extra_a[...] + extra_b[...]
    two = lines[pl.ds(start, 2), :]
    told = jnp.concatenate((squares, two[0:1, :], two[1:2, :]), axis=1)
    payload[...] = jnp.broadcast_to(told[None], payload.shape)
    to_hbm(payload, out, sem)


def adamw(weight, gradient, moment_one, moment_two, rate):
    one_new = beta_one * moment_one + (1.0 - beta_one) * gradient
    two_new = beta_two * moment_two + (1.0 - beta_two) * gradient * gradient
    root = math.sqrt(1.0 - beta_two**adam_step)
    scale = rate * root / (1.0 - beta_one**adam_step)
    step = scale * one_new / (jnp.sqrt(two_new) + adam_eps * root)
    return (weight * (1.0 - rate * decay_rate) - step, one_new, two_new)


def fetch_kernel(*refs):
    count = len(refs) // 2
    copies = [pltpu.make_async_copy(refs[i], refs[count + i], refs[-1].at[i]) for i in range(count)]
    for copy in copies:
        copy.start()
    for copy in copies:
        copy.wait()


def adam_kernel(*refs):
    told, grad_qkvo, grad_in, grad_down, *state = refs[:22]
    norm_ref, *matrices, gains_a, gains_b, gains_c, gains_grad, table_a, table_b, table_c = refs[22:46]
    gains_sum, table_grad = refs[46:]
    gains_o, table_o = (gains_a, gains_b, gains_c), (table_a, table_b, table_c)
    qkv, out, ffn_in, ffn_down, gains, table = (state[i : i + 3] for i in range(0, 18, 3))
    qkv_o, out_o, in_o, down_o = (matrices[i : i + 4] for i in range(0, 16, 4))
    tp = lax.axis_size("tp")
    squares = told[0, :, :BLK]
    for i in range(1, told.shape[0]):
        squares = squares + told[i, :, :BLK]
    model = gains_sum.shape[1]
    per_row = model // BLK
    per_line = BLK // BUCKETS
    first = lax.axis_index("tp") * table_grad.shape[0]
    for line in range(2 * per_row + HEADS // per_line):
        index, at = divmod(line, 2)
        cols = slice((at + 1) * BLK, (at + 2) * BLK)
        value = told[index * tp, :, cols]
        for i in range(1, tp):
            value = value + told[index * tp + i, :, cols]
        squares = squares + value * value
        row, at = divmod(line, per_row)
        if row < 2:
            gains_sum[row : row + 1, at * BLK : (at + 1) * BLK] = value
            continue
        for i in range(per_line):
            head = at * per_line + i
            cell = value[:, i * BUCKETS : (i + 1) * BUCKETS]
            for h in range(table_grad.shape[0]):

                @pl.when(first + h == head)
                def _():
                    table_grad[h : h + 1, :] = cell

    norm = jnp.sqrt(jnp.sum(squares, axis=1, keepdims=True))
    norm_ref[...] = norm
    factor = clip_norm / jnp.maximum(norm, clip_norm)

    def update(state_refs, gradient, to, rate, at=...):
        new = adamw(state_refs[0][at], gradient * factor, state_refs[1][at], state_refs[2][at], rate)
        for ref, value in zip(to, new):
            ref[at] = value
        if len(to) == 4:
            to[3][at] = new[0].astype(bf16)

    update(ffn_in, grad_in[...], in_o, rate_small)
    update(ffn_down, grad_down[...], down_o, rate_small)
    width = qkv[0].shape[2]
    for part in range(3):
        update(qkv, grad_qkvo[:, part * width : (part + 1) * width], qkv_o, rate_small, part)
    update(out, grad_qkvo[:, 3 * width :], out_o, rate_large)
    update(gains, gains_sum[...], gains_o, rate_large)
    gains_grad[...] = gains_sum[...] * factor
    update(table, table_grad[...], table_o, rate_large)


def on_device(
    dp,
    inputs,
    cotangent,
    seg_lengths,
    bucket_ids,
    qkv_weight,
    qkv_first,
    qkv_second,
    out_weight,
    out_first,
    out_second,
    ffn_in_weight,
    ffn_in_first,
    ffn_in_second,
    ffn_down_weight,
    ffn_down_first,
    ffn_down_second,
    norm_gains,
    gains_first,
    gains_second,
    bias_table,
    table_first,
    table_second,
):
    tokens, model = inputs.shape
    rows, local = out_weight.shape
    hidden = ffn_in_weight.shape[1]
    heads_here = local // HDIM
    tp = lax.axis_size("tp")
    packed_cols = 4 * local
    direct = dp == 8

    def swap_dp(value, distance):
        return lax.ppermute(value, "dp", [(i, i ^ distance) for i in range(dp)])

    def swap_tp(value, distance):
        return lax.ppermute(value, "tp", [(i, i ^ distance) for i in range(tp)])

    def add(one, two, behind=()):
        (out,) = call(add_kernel, [sds(one.shape, bf16)], (one, two), "add", limit=4, behind=behind)
        return out

    def pair_add(keep, got, behind):
        outs = [sds((2, *keep.shape[1:]), bf16)] * 2
        return call(pair_add_kernel, outs, (keep, got), "pair_add", limit=4, behind=behind)

    def high_add(keep, got, behind):
        outs = [sds((2, *keep.shape[1:]), bf16)]
        (out,) = call(high_add_kernel, outs, (keep, got), "high_add", limit=4, behind=behind)
        return out

    def late_add(keep, got_low, got, behind):
        outs = [sds(keep.shape[1:], bf16)] * 2
        return call(late_add_kernel, outs, (keep, got_low, got), "late_add", limit=4, behind=behind)

    def next_add(keep, got, behind):
        outs = [sds(keep.shape[1:], bf16)] * 2
        return call(next_add_kernel, outs, (keep, got), "next_add", limit=4, behind=behind)

    half_shape = [sds((tokens // 2, model), bf16)] * 2
    matrices = (qkv_weight, out_weight, ffn_down_weight, ffn_in_weight)
    packed, packed_ffn = call(
        pack_kernel,
        [sds((rows, packed_cols), bf16), sds((rows, 2 * hidden), bf16)],
        matrices,
        "pack",
        hbm=(0, 1, 2, 3),
        scratch=[*(pltpu.VMEM(m.shape, f32) for m in matrices), pltpu.SemaphoreType.DMA((4,))],
    )
    ids = bucket_ids[None, :]
    act_one, act_one_t, bias, bucket_row, inputs, norm_gains_here, cotangent = call(
        prep_kernel,
        [
            sds((tokens, model), bf16),
            sds((model, tokens), bf16),
            sds((heads_here, LEN, LEN), f32),
            sds((1, 2 * LEN), jnp.int32),
            sds(inputs.shape, bf16),
            sds(norm_gains.shape, f32),
            sds(inputs.shape, bf16),
        ],
        (seg_lengths, bias_table.T, ids, inputs, norm_gains, cotangent),
        "prep",
        hbm=range(6),
        scratch=[
            pltpu.SMEM(seg_lengths.shape, jnp.int32),
            pltpu.SMEM((heads_here, BUCKETS), f32),
            pltpu.VMEM(ids.shape, jnp.int32),
            pltpu.SemaphoreType.DMA((6,)),
        ],
    )
    if direct:
        one, two = swap_dp(packed, 2), swap_dp(packed, 4)
        own, ffn_own = swap_dp(after(packed, act_one), 1), swap_dp(after(packed_ffn, act_one), 1)
        one_across = swap_dp(one, 1)
        three = swap_dp(two, 2)
        ffn_two = swap_dp(after(packed_ffn, two), 4)
        two_across = swap_dp(two, 1)
        ffn_one = swap_dp(after(packed_ffn, three, own, one_across), 2)
        three_across = swap_dp(three, 1)
        qkvo_blocks = [packed, own, one, one_across, two, two_across, three, three_across]
        ffn_three = swap_dp(after(ffn_two, ffn_one), 2)
        ffn_blocks = [packed_ffn, ffn_own, ffn_one, swap_dp(after(ffn_own, ffn_one), 2)]
        for block in (ffn_two, ffn_three):
            ffn_blocks += [block, swap_dp(block, 1)]
        bias = after(bias, ffn_own, ffn_two)
        ffn_early = (ffn_blocks[5], ffn_three)
    else:
        qkvo_blocks = [lax.all_gather(packed, "dp", axis=0, tiled=True)]
        ffn_blocks = ffn_early = [lax.all_gather(packed_ffn, "dp", axis=0, tiled=True)]
    n_blocks = len(qkvo_blocks)

    weights_one, qkv, prob, mixed, attn_keep, attn_send = call(
        functools.partial(attend_kernel, n_blocks),
        [
            sds((model, packed_cols), bf16),
            sds((tokens, 3 * local), bf16),
            sds((heads_here, LEN, LEN), bf16),
            sds((tokens, local), bf16),
            *half_shape,
        ],
        (act_one, bias, *qkvo_blocks),
        "attend",
    )
    half_blocks = [sds((BLK, model), bf16)] * 2
    attn_first = call(
        split_add_kernel, half_blocks, (attn_keep, swap_tp(attn_send, 1)), "split_add", limit=4
    )
    attn_own = [add(first, swap_tp(first, 2), ffn_early) for first in attn_first]
    attn_sums = (*attn_own, *(swap_tp(own, 1) for own in attn_own))
    resid, act_two, hidden_act, pre_grad, back_keep, back_send, down_full, in_full = call(
        functools.partial(ffn_kernel, n_blocks),
        [
            sds((tokens, model), f32),
            sds((tokens, model), bf16),
            sds((tokens, hidden), bf16),
            sds((tokens, hidden), bf16),
            *half_shape,
            *[sds((model, hidden), bf16)] * 2,
        ],
        (inputs, norm_gains_here, cotangent, *attn_sums, *ffn_blocks),
        "ffn",
        scratch=[pltpu.VMEM((tokens, hidden), f32)],
    )
    down_order, in_order = (2, 4, 1), (1, 2, 4)
    grad_scratch = [pltpu.VMEM((model, hidden), f32)]
    down_parts = call(
        functools.partial(down_grad_kernel, down_order),
        spread_shapes(dp, model, hidden, (4, 2, 2)),
        (cotangent, hidden_act),
        "down_grad",
        scratch=grad_scratch,
    )
    back_first = add(back_keep, swap_tp(back_send, 1), down_parts[:1])
    back_got = swap_tp(back_first, 2)
    *in_parts, gain_two_part = call(
        functools.partial(in_grad_kernel, in_order),
        [*spread_shapes(dp, model, hidden, (4, 4)), sds((1, model), f32)],
        (act_two, after(pre_grad, back_first), in_full, norm_gains_here),
        "in_grad",
        scratch=grad_scratch,
    )
    share_shapes = [half_shape[0], *half_blocks]
    ffn_keep, *ffn_send = call(
        ffn_out_kernel, share_shapes, (hidden_act, down_full), "ffn_out", behind=(gain_two_part,)
    )
    ffn_got = [swap_tp(part, 1) for part in ffn_send]
    ffn_sums = call(core_add_kernel, half_blocks, (ffn_keep, *ffn_got), "ffn_add", limit=4)
    attend_behind = ()
    back_behind = ffn_sums[:1]
    if direct:
        down_keep, down_high, down_low = down_parts
        down_got = swap_dp(down_high, down_order[0])
        back_behind = (*back_behind, down_got)
    back_sum = add(back_first, back_got, back_behind)
    if direct:
        down_one = high_add(down_keep, down_got, (back_sum,))
        attend_behind = (down_one,)
    everyone = dp * tp
    qkvo_shapes = spread_shapes(dp, model, packed_cols, (4, 2))
    small_shape = sds((2 * rows + SMALL, model), bf16) if direct else sds((SMALL, model), f32)
    *qkvo_parts, share_grad, small, proj_grad = call(
        functools.partial(attend_back_kernel, len(qkvo_shapes)),
        [*qkvo_shapes, sds((BLK, model), f32), small_shape, sds((tokens, 3 * local), bf16)],
        (
            resid,
            cotangent,
            norm_gains_here,
            back_sum,
            swap_tp(back_sum, 1),
            weights_one,
            qkv,
            prob,
            mixed,
            act_one_t,
            bucket_row,
            gain_two_part,
        ),
        "attend_back",
        scratch=[
            pltpu.VMEM((tokens, model), bf16),
            pltpu.VMEM((model, packed_cols), f32),
            pltpu.VMEM((8, 2 * LEN), f32),
        ],
        behind=attend_behind,
    )
    def summed(parts, behind):
        return call(
            functools.partial(sum_kernel, len(parts)),
            [sds((rows, parts[0].shape[1]), f32), sds((1, BLK), f32)],
            parts,
            "sum_parts",
            limit=4,
            behind=behind,
        )

    def act_shares(behind):
        keep, *send = call(
            act_grad_kernel, share_shapes, (proj_grad, weights_one), "act_grad", behind=behind
        )
        return (keep, *(swap_tp(part, 1) for part in send))

    def share_sums(shares, behind):
        outs = [sds((2 * BLK, model), bf16)] * 2
        return call(core_add_kernel, outs, (*ffn_sums, *shares), "core_add", limit=4, behind=behind)

    if direct:
        keep, send_low = qkvo_parts
        in_keep, in_send = in_parts
        in_one = pair_add(in_keep, swap_dp(in_send, in_order[0]), (proj_grad,))
        got_high = swap_dp(after(small, *in_one), 1)
        act_parts = act_shares(in_one)
        down_rest = (swap_dp(down_low, down_order[0]), swap_dp(down_one, down_order[1]))
        down_two = late_add(down_keep, *down_rest, act_parts[:1])
        (high,) = call(
            last_high_kernel, [small_shape], (keep, small, got_high), "last_high", limit=4, behind=down_two
        )
        got_low = swap_dp(after(send_low, high), 1)
        down_grad, down_squares = summed((down_two[0], swap_dp(down_two[1], down_order[2])), (high,))
        in_two = next_add(in_one[0], swap_dp(in_one[1], in_order[1]), (down_grad,))
        mine, theirs = share_sums(act_parts, in_two)
        in_grad, in_squares = summed((in_two[0], swap_dp(in_two[1], in_order[2])), (mine,))
        last, late = call(
            last_late_kernel,
            [sds((rows, packed_cols), f32), sds((rows + SMALL, packed_cols), bf16)],
            (keep, got_low, high, swap_dp(high, 2)),
            "last_late",
            limit=4,
            behind=(in_grad,),
        )
        last_parts = (last, late, swap_dp(late, 4))
        share_behind = (late,)
    else:
        qkvo_sums, down_sums, in_sums = (
            (lax.psum_scatter(p[0].astype(f32), "dp", scatter_dimension=0, tiled=True),)
            for p in (qkvo_parts, down_parts, in_parts)
        )
        last_parts = (*qkvo_sums, lax.psum(small, "dp"))
        down_grad, down_squares = summed(down_sums, ())
        in_grad, in_squares = summed(in_sums, ())
        mine, theirs = share_sums(act_shares(()), ())
        share_behind = ()
    block_out, input_grad = call(
        share_out_kernel,
        [sds((BLK, model), bf16), sds((BLK, model), f32)],
        (resid, inputs, norm_gains_here, share_grad, mine, swap_tp(theirs, 2)),
        "share_out",
        behind=share_behind,
    )
    matrices = (
        qkv_weight,
        qkv_first,
        qkv_second,
        out_weight,
        out_first,
        out_second,
        ffn_in_weight,
        ffn_in_first,
        ffn_in_second,
        ffn_down_weight,
        ffn_down_first,
        ffn_down_second,
    )
    vectors = (norm_gains, gains_first, gains_second, bias_table.T, table_first.T, table_second.T)
    state = matrices + vectors
    fetched = call(
        fetch_kernel,
        [sds(m.shape, f32) for m in state],
        state,
        "fetch",
        hbm=range(18),
        scratch=[pltpu.SemaphoreType.DMA((18,))],
        limit=4,
        behind=(block_out,),
    )
    qkvo_grad, payload = call(
        functools.partial(last_sum_kernel, direct),
        [sds((rows, packed_cols), f32), pltpu.HBM((everyone, 1, 3 * BLK), f32)],
        (down_squares, in_squares, *last_parts),
        "last_sum",
        scratch=[
            pltpu.VMEM((everyone, 1, 3 * BLK), f32),
            pltpu.VMEM((LINES + 8, BLK), f32),
            pltpu.SemaphoreType.DMA,
        ],
        behind=(fetched[0],),
    )
    told = lax.all_to_all(payload, ("dp", "tp"), 0, 0)
    shapes = [(m.shape, kind) for m in matrices[::3] for kind in (f32, f32, f32, bf16)]
    norm, *updated = call(
        adam_kernel,
        [
            sds((1, 1), f32),
            *(sds(shape, kind) for shape, kind in shapes),
            *[sds(norm_gains.shape, f32)] * 4,
            *[sds((heads_here, BUCKETS), f32)] * 3,
        ],
        (told, qkvo_grad, in_grad, down_grad, *fetched),
        "adam",
        scratch=[pltpu.VMEM(norm_gains.shape, f32), pltpu.VMEM((heads_here, BUCKETS), f32)],
    )
    return (block_out, input_grad, norm.reshape(()), *updated[:-3], *(t.T for t in updated[-3:]))


def solution(mesh):
    row = P("dp", None)
    matrix = P("dp", "tp")
    stack = P(None, "dp", "tp")
    table = P(None, "tp")
    share = P(("dp", "tp"), None)
    in_specs = (
        *(row,) * 3,
        P(),
        *(stack,) * 3,
        *(matrix,) * 9,
        *(P(),) * 3,
        *(table,) * 3,
    )
    out_specs = (
        *(share,) * 2,
        P(),
        *(stack,) * 4,
        *(matrix,) * 12,
        *(P(),) * 4,
        *(table,) * 3,
    )
    return jax.shard_map(
        functools.partial(on_device, mesh.shape["dp"]),
        mesh=mesh,
        in_specs=in_specs,
        out_specs=out_specs,
        check_vma=False,
    )
```

```python
import functools
import math

import jax
import jax.numpy as jnp
from jax import lax
from jax.experimental import pallas as pl
from jax.experimental.pallas import tpu as pltpu
from jax.sharding import PartitionSpec as P

HEADS = 12
HDIM = 64
BUCKETS = 32
LEN = 512
BLK = 128
WIN = LEN + BLK
SMALL = 8
LINES = 16


eps_norm = 1e-06
clip_norm = 1.0
beta_one = 0.9
beta_two = 0.999
adam_eps = 1e-08
decay_rate = 0.01
adam_step = 10.0
mask_fill = -1000000000.0
rate_small = 0.02
rate_large = 0.5
gelu_coef = 0.044715
root_coef = math.sqrt(2.0 / math.pi)

f32 = jnp.float32
bf16 = jnp.bfloat16
sds = jax.ShapeDtypeStruct


def dot_nn(a, b):
    return lax.dot_general(a, b, (((1,), (0,)), ((), ())), preferred_element_type=f32)


def dot_nt(a, b):
    return lax.dot_general(a, b, (((1,), (1,)), ((), ())), preferred_element_type=f32)


def dot_tn(a, b):
    return lax.dot_general(a, b, (((0,), (0,)), ((), ())), preferred_element_type=f32)


def after(value, *deps):
    return lax.optimization_barrier((value, *deps))[0]


def call(body, outs, args, name, hbm=(), scratch=(), limit=16, behind=()):
    spaces = [pl.ANY if i in hbm else pltpu.VMEM for i in range(len(args))]
    args = [after(args[0], *behind), *args[1:]] if behind else args
    args = [
        pltpu.with_memory_space_constraint(a, pltpu.HBM) if i in hbm else a for i, a in enumerate(args)
    ]
    return pl.pallas_call(
        body,
        out_shape=tuple(outs),
        in_specs=[pl.BlockSpec(memory_space=space) for space in spaces],
        out_specs=tuple(
            pl.BlockSpec(memory_space=pl.ANY if hasattr(o, "memory_space") else pltpu.VMEM) for o in outs
        ),
        scratch_shapes=list(scratch),
        compiler_params=pltpu.CompilerParams(vmem_limit_bytes=limit << 20),
        cost_estimate=pl.CostEstimate(flops=0, bytes_accessed=0, transcendentals=0),
        name=name,
    )(*args)


def to_hbm(staged, out, sem):
    copy = pltpu.make_async_copy(staged, out, sem)
    copy.start()
    copy.wait()


def assemble(into, blocks, start_col=0):
    cols = slice(start_col, start_col + into.shape[1])
    if len(blocks) == 1:
        into[...] = blocks[0][:, cols]
        return
    me = lax.axis_index("dp")
    rows = blocks[0].shape[0]
    for e, block in enumerate(blocks):
        start = pl.multiple_of((me ^ e) * rows, 32)
        into[pl.ds(start, rows), :] = block[:, cols]


def spread(grad, outs, order=(1, 2, 4)):
    if len(outs) == 1:
        outs[0][...] = grad[...].astype(bf16)
        return
    me = lax.axis_index("dp")
    rows = outs[0].shape[1]
    keep, *send = outs
    for b in range(2):
        for k in range(4):
            out, at = (keep, k) if b == 0 else (send[0], k) if len(send) == 1 else (send[1 - (k >> 1)], k & 1)
            apart = b * order[0] ^ (k >> 1) * order[1] ^ (k & 1) * order[2]
            start = pl.multiple_of((me ^ apart) * rows, 32)
            block = grad[pl.ds(start, rows), :].astype(bf16)
            if len(out.shape) == 2:
                out[at * rows : (at + 1) * rows, :] = block
            else:
                out[at] = block


def spread_shapes(dp, width, cols, lengths):
    if dp == 8:
        return [sds((n, width // dp, cols), bf16) for n in lengths]
    return [sds((width, cols), bf16)]


def half_rows():
    core = lax.axis_index("tp") & 1
    for half in range(2):
        for at in range(2):
            start = pl.multiple_of(((core ^ half) + 2 * at) * BLK, BLK)
            yield half, at, pl.ds(start, BLK)


def pack_kernel(qkv, out, down, ffn_in, packed, packed_ffn, *scratch):
    *landed, sems = scratch
    copies = [
        pltpu.make_async_copy(source, to, sems.at[i])
        for i, (source, to) in enumerate(zip((qkv, out, down, ffn_in), landed))
    ]
    for copy in copies:
        copy.start()
    local = out.shape[1]
    copies[0].wait()
    copies[1].wait()
    for part in range(3):
        packed[:, part * local : (part + 1) * local] = landed[0][part].astype(bf16)
    packed[:, 3 * local :] = landed[1][...].astype(bf16)
    width = down.shape[1]
    for i in (2, 3):
        copies[i].wait()
        packed_ffn[:, (i - 2) * width : (i - 1) * width] = landed[i][...].astype(bf16)


def prep_kernel(
    seg_in, table_in, bucket_in, x_in, gains_in, dy_in, act, act_t, bias, bucket, x, gains, dy, seg, table, ids, sems
):
    sources = (x_in, gains_in, bucket_in, seg_in, table_in, dy_in)
    copies = [
        pltpu.make_async_copy(source, to, sems.at[i])
        for i, (source, to) in enumerate(zip(sources, (x, gains, ids, seg, table, dy)))
    ]
    for copy in copies:
        copy.start()
    copies[0].wait()
    copies[1].wait()
    values = x[...].astype(f32)
    scale = lax.rsqrt(jnp.mean(values * values, axis=-1, keepdims=True) + eps_norm)
    low = (values * scale * gains[0:1, :]).astype(bf16)
    act[...] = low
    act_t[...] = low.T
    for copy in copies[2:]:
        copy.wait()
    ends = [seg[0, 0]]
    for k in (1, 2):
        ends.append(ends[-1] + seg[0, k])

    def segment_of(position):
        return sum((position >= end).astype(jnp.int32) for end in ends)

    seg_cols = segment_of(lax.broadcasted_iota(jnp.int32, (1, LEN), 1))
    heads = bias.shape[0]
    bucket[...] = jnp.zeros_like(bucket)
    bucket[:, : 2 * LEN - 1] = ids[...]
    lines = []
    for h in range(heads):
        line = jnp.zeros((1, 2 * LEN), f32)
        for b in range(BUCKETS):
            line = jnp.where(bucket[...] == b, table[h, b], line)
        lines.append(line)
    for r in range(LEN // BLK):
        seg_rows = segment_of(lax.broadcasted_iota(jnp.int32, (BLK, 1), 0) + r * BLK)
        visible = seg_rows == seg_cols
        low_at = LEN - BLK - r * BLK
        for h in range(heads):
            window = jnp.broadcast_to(lines[h][:, low_at : low_at + WIN], (BLK, WIN))
            turned = pltpu.roll(window, 1, 1, stride=1, stride_axis=0)
            bias[h, r * BLK : (r + 1) * BLK, :] = jnp.where(visible, turned[:, BLK:], mask_fill)


def attend_kernel(n_blocks, act, bias, *rest):
    blocks = rest[:n_blocks]
    weights, qkv, prob, mixed, keep, send = rest[n_blocks:]
    assemble(weights, blocks)
    width = qkv.shape[1] // 3
    qkv[...] = dot_nn(act[...], weights[:, : 3 * width]).astype(bf16)
    for h in range(bias.shape[0]):
        cols = slice(h * HDIM, (h + 1) * HDIM)
        query, key, value = (qkv[:, s * width + h * HDIM : s * width + (h + 1) * HDIM] for s in range(3))
        scores = dot_nt(query, key) + bias[h]
        top = jnp.max(scores, axis=-1, keepdims=True)
        exps = jnp.exp(scores - top)
        total = jnp.sum(exps, axis=-1, keepdims=True)
        low = (exps * (1.0 / total)).astype(bf16)
        prob[h] = low
        mixed[:, cols] = dot_nn(low, value).astype(bf16)
    out_cols = weights[:, 3 * width :]
    for half, at, rows in half_rows():
        to = send if half else keep
        to[at * BLK : (at + 1) * BLK, :] = dot_nt(mixed[rows, :], out_cols).astype(bf16)


def ffn_kernel(n_blocks, x, gains, dy, own_a, own_b, other_a, other_b, *rest):
    blocks = rest[:n_blocks]
    resid, act, hidden, pre_grad, keep, send, down, weights, hidden_grad = rest[n_blocks:]
    assemble(down, blocks)
    assemble(weights, blocks, down.shape[1])
    hidden_grad[...] = dot_nn(dy[...], down[...])
    for half, at, rows in half_rows():
        here = slice(at * BLK, (at + 1) * BLK)
        attn = ((own_a, own_b), (other_a, other_b))[half][at]
        values = x[rows, :].astype(f32) + attn[...].astype(f32)
        resid[rows, :] = values
        scale = lax.rsqrt(jnp.mean(values * values, axis=-1, keepdims=True) + eps_norm)
        low = (values * scale * gains[1:2, :]).astype(bf16)
        act[rows, :] = low
        u = dot_nn(low, weights[...])
        square = u * u
        tanh_part = jnp.tanh(root_coef * (u + gelu_coef * square * u))
        hidden[rows, :] = (0.5 * u * (1.0 + tanh_part)).astype(bf16)
        inner = root_coef * (1.0 + 3.0 * gelu_coef * square)
        slope = 0.5 * (1.0 + tanh_part) + 0.5 * u * (1.0 - tanh_part * tanh_part) * inner
        du = (hidden_grad[rows, :] * slope).astype(bf16)
        pre_grad[rows, :] = du
        (send if half else keep)[here, :] = dot_nt(du, weights[...]).astype(bf16)


def row_products(weights, grad):
    products = weights.astype(f32) * grad
    width = grad.shape[1]
    folded = sum(products[:, c : c + BLK] for c in range(0, width - BLK + 1, BLK))
    if width % BLK:
        rest = products[:, width - width % BLK :]
        wide = jnp.zeros((grad.shape[0], BLK - width % BLK), f32)
        folded = folded + jnp.concatenate([rest, wide], axis=1)
    return jnp.sum(folded.T, axis=0, keepdims=True)


def down_grad_kernel(order, left, right, *rest):
    outs, grad = rest[:-1], rest[-1]
    grad[...] = dot_tn(left[...], right[...])
    spread(grad, outs, order)


def in_grad_kernel(order, left, right, weights, gains, *rest):
    *outs, gain_part, grad = rest
    grad[...] = dot_tn(left[...], right[...])
    spread(grad, outs, order)
    gain_part[...] = row_products(weights[...], grad[...]) / gains[1:2, :]


def turn_kernel(prob, out):
    for h in range(prob.shape[0]):
        out[h] = prob[h].T


def attend_back_kernel(
    n_outs, resid, dy, gains, own, other, weights, qkv, prob, prob_t, mixed, act_t, bucket, gain_two, *rest
):
    outs = rest[:n_outs]
    share_grad, small, proj_grad, resid_low, grad, diag = rest[n_outs:]
    chip = lax.axis_index("tp") >> 1
    width = qkv.shape[1] // 3
    for half, at, rows in half_rows():
        here = slice(at * BLK, (at + 1) * BLK)
        act_grad = (other if half else own)[here, :].astype(f32)
        values = resid[rows, :]
        scale = lax.rsqrt(jnp.mean(values * values, axis=-1, keepdims=True) + eps_norm)
        normed = values * scale
        normal_grad = act_grad * gains[1:2, :]
        mean_part = jnp.mean(normal_grad * normed, axis=-1, keepdims=True)
        total = dy[rows, :].astype(f32) + scale * (normal_grad - normed * mean_part)
        resid_low[rows, :] = total.astype(bf16)
        if half == 0:

            @pl.when(chip == at)
            def _():
                share_grad[...] = total

    mix_grad = dot_nn(resid_low[...], weights[:, 3 * width :]).astype(bf16)
    heads = prob.shape[0]
    row = lax.broadcasted_iota(jnp.int32, (BLK, BLK), 0)
    col = lax.broadcasted_iota(jnp.int32, (BLK, BLK), 1)
    flip = (row + col == BLK - 1).astype(f32).astype(bf16)
    diag[...] = jnp.zeros_like(diag)
    for h in range(heads):
        query, key, value = (qkv[:, s * width + h * HDIM : s * width + (h + 1) * HDIM] for s in range(3))
        grad_rows = mix_grad[:, h * HDIM : (h + 1) * HDIM]
        prob_grad = dot_nt(grad_rows, value)
        prob_here = prob[h].astype(f32)
        row_dot = jnp.sum(prob_here * prob_grad, axis=-1, keepdims=True)
        low = (prob_here * (prob_grad - row_dot)).astype(bf16)
        for r in range(LEN // BLK):
            flipped = dot_nn(flip, low[r * BLK : (r + 1) * BLK, :])
            wide = jnp.concatenate([flipped, jnp.zeros((BLK, BLK), f32)], axis=1)
            turned = pltpu.roll(wide, 0, 1, stride=1, stride_axis=0)
            low_at = LEN - BLK - r * BLK
            diag[h : h + 1, low_at : low_at + WIN] += jnp.sum(turned, axis=0, keepdims=True)
        for s, part in enumerate((dot_nn(low, key), dot_tn(low, query), dot_nn(prob_t[h], grad_rows))):
            proj_grad[:, s * width + h * HDIM : s * width + (h + 1) * HDIM] = part.astype(bf16)
    grad[:, : 3 * width] = dot_nn(act_t[...], proj_grad[...])
    grad[:, 3 * width :] = dot_tn(resid_low[...], mixed[...])
    onehot = (lax.broadcasted_iota(jnp.int32, (BUCKETS, 2 * LEN), 0) == bucket[...]).astype(f32)
    by_bucket = lax.dot_general(
        diag[...],
        onehot,
        (((1,), (1,)), ((), ())),
        precision=lax.Precision.HIGHEST,
        preferred_element_type=f32,
    )
    first = lax.axis_index("tp") * heads
    cells = [
        sum(jnp.where(first + h == head, by_bucket[h : h + 1, :], 0.0) for h in range(heads))
        for head in range(HEADS)
    ]
    model = gains.shape[1]
    cells.append(jnp.zeros((1, model - HEADS * BUCKETS), f32))
    gain_one = row_products(weights[:, : 3 * width], grad[:, : 3 * width]) / gains[0:1, :]
    lines = (gain_one, gain_two[...], jnp.concatenate(cells, axis=1), jnp.zeros((SMALL - 3, model), f32))
    whole = jnp.concatenate(lines, axis=0)
    if n_outs == 1:
        spread(grad, outs)
        small[...] = whole
        return
    keep, low = outs
    rows = keep.shape[1]
    spread(grad, (keep, small, low))
    small[2 * rows :, :] = whole.astype(bf16)


def ffn_out_kernel(hidden, down, keep, *send):
    for half, at, rows in half_rows():
        block = dot_nt(hidden[rows, :], down[...]).astype(bf16)
        if half:
            send[at][...] = block
        else:
            keep[at * BLK : (at + 1) * BLK, :] = block


def act_grad_kernel(proj_grad, weights, keep, *send):
    width = proj_grad.shape[1]
    for half, at, rows in half_rows():
        block = dot_nt(proj_grad[rows, :], weights[:, :width]).astype(bf16)
        if half:
            send[at][...] = block
        else:
            keep[at * BLK : (at + 1) * BLK, :] = block


def core_add_kernel(*refs):
    *before, keep, got_a, got_b, mine, theirs = refs
    chip = lax.axis_index("tp") >> 1
    first = mine.shape[0] - BLK
    for to, block in zip((mine, theirs), before):
        to[:BLK, :] = block[...]
    for at, got in enumerate((got_a, got_b)):
        here = slice(at * BLK, (at + 1) * BLK)
        value = (keep[here, :].astype(f32) + got[...].astype(f32)).astype(bf16)

        @pl.when(chip == at)
        def _():
            mine[first:, :] = value

        @pl.when(chip != at)
        def _():
            theirs[first:, :] = value


def share_out_kernel(resid, x, gains, share_grad, mine, got, block_out, input_grad):
    share = pl.ds(pl.multiple_of(lax.axis_index("tp") * BLK, BLK), BLK)
    first, second = slice(0, BLK), slice(BLK, 2 * BLK)
    ffn = mine[first, :].astype(f32) + got[first, :].astype(f32)
    block_out[...] = (resid[share, :] + ffn).astype(bf16)
    values = x[share, :].astype(f32)
    scale = lax.rsqrt(jnp.mean(values * values, axis=-1, keepdims=True) + eps_norm)
    normed = values * scale
    normal_grad = (mine[second, :].astype(f32) + got[second, :].astype(f32)) * gains[0:1, :]
    mean_part = jnp.mean(normal_grad * normed, axis=-1, keepdims=True)
    input_grad[...] = share_grad[...] + scale * (normal_grad - normed * mean_part)


def add_kernel(one, two, out):
    out[...] = (one[...].astype(f32) + two[...].astype(f32)).astype(bf16)


def split_add_kernel(one, two, *outs):
    for i, out in enumerate(outs):
        rows = slice(i * BLK, (i + 1) * BLK)
        out[...] = (one[rows, :].astype(f32) + two[rows, :].astype(f32)).astype(bf16)


def pair_add_kernel(keep, got, mine, theirs):
    for k in range(4):
        to = theirs if k >= 2 else mine
        to[k % 2] = (keep[k].astype(f32) + got[k].astype(f32)).astype(bf16)


def high_add_kernel(keep, got, theirs):
    for k in range(2):
        theirs[k] = (keep[k + 2].astype(f32) + got[k].astype(f32)).astype(bf16)


def late_add_kernel(keep, got_low, got, mine, theirs):
    for k, to in enumerate((mine, theirs)):
        to[...] = (keep[k].astype(f32) + got_low[k].astype(f32) + got[k].astype(f32)).astype(bf16)


def next_add_kernel(keep, got, mine, theirs):
    for k, to in enumerate((mine, theirs)):
        to[...] = (keep[k].astype(f32) + got[k].astype(f32)).astype(bf16)


def last_high_kernel(keep, sent, got, out):
    rows = keep.shape[1]
    for k in range(2):
        here = slice(k * rows, (k + 1) * rows)
        out[here, :] = (keep[k + 2].astype(f32) + got[here, :].astype(f32)).astype(bf16)
    small = slice(2 * rows, None)
    out[small, :] = (sent[small, :].astype(f32) + got[small, :].astype(f32)).astype(bf16)


def last_late_kernel(keep, got_low, sent, got, mine, out):
    rows = keep.shape[1]
    first, second, small = slice(0, rows), slice(rows, 2 * rows), slice(2 * rows, None)
    mine[...] = keep[0].astype(f32) + got_low[0].astype(f32) + got[first, :].astype(f32)
    block = keep[1].astype(f32) + got_low[1].astype(f32) + got[second, :].astype(f32)
    out[:rows, :] = block.astype(bf16)
    out[rows:, :] = (sent[small, :].astype(f32) + got[small, :].astype(f32)).astype(bf16)


def fold(values):
    rows, cols = values.shape
    squares = values * values
    lanes = sum(squares[:, c : c + BLK] for c in range(0, cols, BLK))
    return jnp.sum(lanes, axis=0, keepdims=True)


def sum_kernel(n_parts, *rest):
    parts, (grad, squares) = rest[:n_parts], rest[n_parts:]
    total = sum(part[...].astype(f32) for part in parts)
    grad[...] = total
    squares[...] = fold(total)


def last_sum_kernel(direct, extra_a, extra_b, *rest):
    *parts, grad, out, payload, lines, sem = rest
    if direct:
        mine, sent, got = parts
        rows = mine.shape[0]
        total = mine[...] + got[:rows, :].astype(f32)
        small = sent[rows:, :].astype(f32) + got[rows:, :].astype(f32)
    else:
        total, small = (part[...] for part in parts)
    grad[...] = total
    per_row = total.shape[1] // BLK
    lines[...] = jnp.zeros_like(lines)
    for line in range(LINES):
        row, at = divmod(line, per_row)
        lines[line : line + 1, :] = small[row : row + 1, at * BLK : (at + 1) * BLK]
    me = lax.axis_index("dp")
    start = pl.multiple_of(jnp.minimum(2 * me, LINES), 2)
    squares = fold(total) + extra_a[...] + extra_b[...]
    two = lines[pl.ds(start, 2), :]
    told = jnp.concatenate((squares, two[0:1, :], two[1:2, :]), axis=1)
    payload[...] = jnp.broadcast_to(told[None], payload.shape)
    to_hbm(payload, out, sem)


def adamw(weight, gradient, moment_one, moment_two, rate):
    one_new = beta_one * moment_one + (1.0 - beta_one) * gradient
    two_new = beta_two * moment_two + (1.0 - beta_two) * gradient * gradient
    root = math.sqrt(1.0 - beta_two**adam_step)
    scale = rate * root / (1.0 - beta_one**adam_step)
    step = scale * one_new / (jnp.sqrt(two_new) + adam_eps * root)
    return (weight * (1.0 - rate * decay_rate) - step, one_new, two_new)


def fetch_kernel(*refs):
    count = len(refs) // 2
    copies = [pltpu.make_async_copy(refs[i], refs[count + i], refs[-1].at[i]) for i in range(count)]
    for copy in copies:
        copy.start()
    for copy in copies:
        copy.wait()


def adam_kernel(*refs):
    told, grad_qkvo, grad_in, grad_down, *state = refs[:22]
    norm_ref, *matrices, gains_a, gains_b, gains_c, gains_grad, table_a, table_b, table_c = refs[22:46]
    gains_sum, table_grad = refs[46:]
    gains_o, table_o = (gains_a, gains_b, gains_c), (table_a, table_b, table_c)
    qkv, out, ffn_in, ffn_down, gains, table = (state[i : i + 3] for i in range(0, 18, 3))
    qkv_o, out_o, in_o, down_o = (matrices[i : i + 4] for i in range(0, 16, 4))
    tp = lax.axis_size("tp")
    squares = told[0, :, :BLK]
    for i in range(1, told.shape[0]):
        squares = squares + told[i, :, :BLK]
    model = gains_sum.shape[1]
    per_row = model // BLK
    per_line = BLK // BUCKETS
    first = lax.axis_index("tp") * table_grad.shape[0]
    for line in range(2 * per_row + HEADS // per_line):
        index, at = divmod(line, 2)
        cols = slice((at + 1) * BLK, (at + 2) * BLK)
        value = told[index * tp, :, cols]
        for i in range(1, tp):
            value = value + told[index * tp + i, :, cols]
        squares = squares + value * value
        row, at = divmod(line, per_row)
        if row < 2:
            gains_sum[row : row + 1, at * BLK : (at + 1) * BLK] = value
            continue
        for i in range(per_line):
            head = at * per_line + i
            cell = value[:, i * BUCKETS : (i + 1) * BUCKETS]
            for h in range(table_grad.shape[0]):

                @pl.when(first + h == head)
                def _():
                    table_grad[h : h + 1, :] = cell

    norm = jnp.sqrt(jnp.sum(squares, axis=1, keepdims=True))
    norm_ref[...] = norm
    factor = clip_norm / jnp.maximum(norm, clip_norm)

    def update(state_refs, gradient, to, rate, at=...):
        new = adamw(state_refs[0][at], gradient * factor, state_refs[1][at], state_refs[2][at], rate)
        for ref, value in zip(to, new):
            ref[at] = value
        if len(to) == 4:
            to[3][at] = new[0].astype(bf16)

    update(ffn_in, grad_in[...], in_o, rate_small)
    update(ffn_down, grad_down[...], down_o, rate_small)
    width = qkv[0].shape[2]
    for part in range(3):
        update(qkv, grad_qkvo[:, part * width : (part + 1) * width], qkv_o, rate_small, part)
    update(out, grad_qkvo[:, 3 * width :], out_o, rate_large)
    update(gains, gains_sum[...], gains_o, rate_large)
    gains_grad[...] = gains_sum[...] * factor
    update(table, table_grad[...], table_o, rate_large)


def on_device(
    dp,
    inputs,
    cotangent,
    seg_lengths,
    bucket_ids,
    qkv_weight,
    qkv_first,
    qkv_second,
    out_weight,
    out_first,
    out_second,
    ffn_in_weight,
    ffn_in_first,
    ffn_in_second,
    ffn_down_weight,
    ffn_down_first,
    ffn_down_second,
    norm_gains,
    gains_first,
    gains_second,
    bias_table,
    table_first,
    table_second,
):
    tokens, model = inputs.shape
    rows, local = out_weight.shape
    hidden = ffn_in_weight.shape[1]
    heads_here = local // HDIM
    tp = lax.axis_size("tp")
    packed_cols = 4 * local
    direct = dp == 8

    def swap_dp(value, distance):
        return lax.ppermute(value, "dp", [(i, i ^ distance) for i in range(dp)])

    def swap_tp(value, distance):
        return lax.ppermute(value, "tp", [(i, i ^ distance) for i in range(tp)])

    def add(one, two, behind=()):
        (out,) = call(add_kernel, [sds(one.shape, bf16)], (one, two), "add", limit=4, behind=behind)
        return out

    def pair_add(keep, got, behind):
        outs = [sds((2, *keep.shape[1:]), bf16)] * 2
        return call(pair_add_kernel, outs, (keep, got), "pair_add", limit=4, behind=behind)

    def high_add(keep, got, behind):
        outs = [sds((2, *keep.shape[1:]), bf16)]
        (out,) = call(high_add_kernel, outs, (keep, got), "high_add", limit=4, behind=behind)
        return out

    def late_add(keep, got_low, got, behind):
        outs = [sds(keep.shape[1:], bf16)] * 2
        return call(late_add_kernel, outs, (keep, got_low, got), "late_add", limit=4, behind=behind)

    def next_add(keep, got, behind):
        outs = [sds(keep.shape[1:], bf16)] * 2
        return call(next_add_kernel, outs, (keep, got), "next_add", limit=4, behind=behind)

    half_shape = [sds((tokens // 2, model), bf16)] * 2
    matrices = (qkv_weight, out_weight, ffn_down_weight, ffn_in_weight)
    packed, packed_ffn = call(
        pack_kernel,
        [sds((rows, packed_cols), bf16), sds((rows, 2 * hidden), bf16)],
        matrices,
        "pack",
        hbm=(0, 1, 2, 3),
        scratch=[*(pltpu.VMEM(m.shape, f32) for m in matrices), pltpu.SemaphoreType.DMA((4,))],
    )
    ids = bucket_ids[None, :]
    act_one, act_one_t, bias, bucket_row, inputs, norm_gains_here, cotangent = call(
        prep_kernel,
        [
            sds((tokens, model), bf16),
            sds((model, tokens), bf16),
            sds((heads_here, LEN, LEN), f32),
            sds((1, 2 * LEN), jnp.int32),
            sds(inputs.shape, bf16),
            sds(norm_gains.shape, f32),
            sds(inputs.shape, bf16),
        ],
        (seg_lengths, bias_table.T, ids, inputs, norm_gains, cotangent),
        "prep",
        hbm=range(6),
        scratch=[
            pltpu.SMEM(seg_lengths.shape, jnp.int32),
            pltpu.SMEM((heads_here, BUCKETS), f32),
            pltpu.VMEM(ids.shape, jnp.int32),
            pltpu.SemaphoreType.DMA((6,)),
        ],
    )
    if direct:
        one, two = swap_dp(packed, 2), swap_dp(packed, 4)
        own, ffn_own = swap_dp(after(packed, act_one), 1), swap_dp(after(packed_ffn, act_one), 1)
        one_across = swap_dp(one, 1)
        three = swap_dp(two, 2)
        ffn_two = swap_dp(after(packed_ffn, two), 4)
        two_across = swap_dp(two, 1)
        ffn_one = swap_dp(after(packed_ffn, three, own), 2)
        three_across = swap_dp(three, 1)
        qkvo_blocks = [packed, own, one, one_across, two, two_across, three, three_across]
        ffn_three = swap_dp(after(ffn_two, ffn_one), 2)
        ffn_blocks = [packed_ffn, ffn_own, ffn_one, swap_dp(after(ffn_own, ffn_one), 2)]
        for block in (ffn_two, ffn_three):
            ffn_blocks += [block, swap_dp(block, 1)]
        bias = after(bias, ffn_own, one_across)
        ffn_first, ffn_early = (ffn_two,), (ffn_blocks[5], ffn_three)
    else:
        qkvo_blocks = [lax.all_gather(packed, "dp", axis=0, tiled=True)]
        ffn_first = ffn_blocks = ffn_early = [lax.all_gather(packed_ffn, "dp", axis=0, tiled=True)]
    n_blocks = len(qkvo_blocks)

    weights_one, qkv, prob, mixed, attn_keep, attn_send = call(
        functools.partial(attend_kernel, n_blocks),
        [
            sds((model, packed_cols), bf16),
            sds((tokens, 3 * local), bf16),
            sds((heads_here, LEN, LEN), bf16),
            sds((tokens, local), bf16),
            *half_shape,
        ],
        (act_one, bias, *qkvo_blocks),
        "attend",
    )
    half_blocks = [sds((BLK, model), bf16)] * 2
    attn_first = call(
        split_add_kernel, half_blocks, (attn_keep, swap_tp(after(attn_send, *ffn_first), 1)), "split_add", limit=4
    )
    attn_own = [add(first, swap_tp(first, 2), ffn_early) for first in attn_first]
    attn_sums = (*attn_own, *(swap_tp(own, 1) for own in attn_own))
    resid, act_two, hidden_act, pre_grad, back_keep, back_send, down_full, in_full = call(
        functools.partial(ffn_kernel, n_blocks),
        [
            sds((tokens, model), f32),
            sds((tokens, model), bf16),
            sds((tokens, hidden), bf16),
            sds((tokens, hidden), bf16),
            *half_shape,
            *[sds((model, hidden), bf16)] * 2,
        ],
        (inputs, norm_gains_here, cotangent, *attn_sums, *ffn_blocks),
        "ffn",
        scratch=[pltpu.VMEM((tokens, hidden), f32)],
    )
    down_order, in_order = (2, 4, 1), (1, 2, 4)
    grad_scratch = [pltpu.VMEM((model, hidden), f32)]
    down_parts = call(
        functools.partial(down_grad_kernel, down_order),
        spread_shapes(dp, model, hidden, (4, 2, 2)),
        (cotangent, hidden_act),
        "down_grad",
        scratch=grad_scratch,
    )
    back_first = add(back_keep, swap_tp(back_send, 1), down_parts[:1])
    back_got = swap_tp(back_first, 2)
    *in_parts, gain_two_part = call(
        functools.partial(in_grad_kernel, in_order),
        [*spread_shapes(dp, model, hidden, (4, 4)), sds((1, model), f32)],
        (act_two, after(pre_grad, back_first), in_full, norm_gains_here),
        "in_grad",
        scratch=grad_scratch,
    )
    share_shapes = [half_shape[0], *half_blocks]
    ffn_keep, *ffn_send = call(
        ffn_out_kernel, share_shapes, (hidden_act, down_full), "ffn_out", behind=(gain_two_part,)
    )
    ffn_got = [swap_tp(part, 1) for part in ffn_send]
    ffn_sums = call(core_add_kernel, half_blocks, (ffn_keep, *ffn_got), "ffn_add", limit=4)
    attend_behind = ()
    back_behind = ffn_sums[:1]
    if direct:
        down_keep, down_high, down_low = down_parts
        down_got = swap_dp(down_high, down_order[0])
        back_behind = (*back_behind, down_got)
    (prob_t,) = call(turn_kernel, [sds(prob.shape, bf16)], (prob,), "turn", behind=ffn_sums[:1])
    back_sum = add(back_first, back_got, (*back_behind, prob_t))
    if direct:
        down_one = high_add(down_keep, down_got, (back_sum,))
        attend_behind = (down_one,)
    everyone = dp * tp
    qkvo_shapes = spread_shapes(dp, model, packed_cols, (4, 2))
    small_shape = sds((2 * rows + SMALL, model), bf16) if direct else sds((SMALL, model), f32)
    *qkvo_parts, share_grad, small, proj_grad = call(
        functools.partial(attend_back_kernel, len(qkvo_shapes)),
        [*qkvo_shapes, sds((BLK, model), f32), small_shape, sds((tokens, 3 * local), bf16)],
        (
            resid,
            cotangent,
            norm_gains_here,
            back_sum,
            swap_tp(back_sum, 1),
            weights_one,
            qkv,
            prob,
            prob_t,
            mixed,
            act_one_t,
            bucket_row,
            gain_two_part,
        ),
        "attend_back",
        scratch=[
            pltpu.VMEM((tokens, model), bf16),
            pltpu.VMEM((model, packed_cols), f32),
            pltpu.VMEM((8, 2 * LEN), f32),
        ],
        behind=attend_behind,
    )
    def summed(parts, behind):
        return call(
            functools.partial(sum_kernel, len(parts)),
            [sds((rows, parts[0].shape[1]), f32), sds((1, BLK), f32)],
            parts,
            "sum_parts",
            limit=4,
            behind=behind,
        )

    def act_shares(behind):
        keep, *send = call(
            act_grad_kernel, share_shapes, (proj_grad, weights_one), "act_grad", behind=behind
        )
        return (keep, *(swap_tp(part, 1) for part in send))

    def share_sums(shares, behind):
        outs = [sds((2 * BLK, model), bf16)] * 2
        return call(core_add_kernel, outs, (*ffn_sums, *shares), "core_add", limit=4, behind=behind)

    if direct:
        keep, send_low = qkvo_parts
        in_keep, in_send = in_parts
        in_one = pair_add(in_keep, swap_dp(in_send, in_order[0]), (proj_grad,))
        got_high = swap_dp(after(small, *in_one), 1)
        act_parts = act_shares(in_one)
        down_rest = (swap_dp(down_low, down_order[0]), swap_dp(down_one, down_order[1]))
        down_two = late_add(down_keep, *down_rest, act_parts[:1])
        (high,) = call(
            last_high_kernel, [small_shape], (keep, small, got_high), "last_high", limit=4, behind=down_two
        )
        got_low = swap_dp(after(send_low, high), 1)
        down_grad, down_squares = summed((down_two[0], swap_dp(down_two[1], down_order[2])), (high,))
        in_two = next_add(in_one[0], swap_dp(in_one[1], in_order[1]), (down_grad,))
        mine, theirs = share_sums(act_parts, in_two)
        in_grad, in_squares = summed((in_two[0], swap_dp(in_two[1], in_order[2])), (mine,))
        last, late = call(
            last_late_kernel,
            [sds((rows, packed_cols), f32), sds((rows + SMALL, packed_cols), bf16)],
            (keep, got_low, high, swap_dp(high, 2)),
            "last_late",
            limit=4,
            behind=(in_grad,),
        )
        last_parts = (last, late, swap_dp(late, 4))
        share_behind = (late,)
    else:
        qkvo_sums, down_sums, in_sums = (
            (lax.psum_scatter(p[0].astype(f32), "dp", scatter_dimension=0, tiled=True),)
            for p in (qkvo_parts, down_parts, in_parts)
        )
        last_parts = (*qkvo_sums, lax.psum(small, "dp"))
        down_grad, down_squares = summed(down_sums, ())
        in_grad, in_squares = summed(in_sums, ())
        mine, theirs = share_sums(act_shares(()), ())
        share_behind = ()
    block_out, input_grad = call(
        share_out_kernel,
        [sds((BLK, model), bf16), sds((BLK, model), f32)],
        (resid, inputs, norm_gains_here, share_grad, mine, swap_tp(theirs, 2)),
        "share_out",
        behind=share_behind,
    )
    matrices = (
        qkv_weight,
        qkv_first,
        qkv_second,
        out_weight,
        out_first,
        out_second,
        ffn_in_weight,
        ffn_in_first,
        ffn_in_second,
        ffn_down_weight,
        ffn_down_first,
        ffn_down_second,
    )
    vectors = (norm_gains, gains_first, gains_second, bias_table.T, table_first.T, table_second.T)
    state = matrices + vectors
    fetched = call(
        fetch_kernel,
        [sds(m.shape, f32) for m in state],
        state,
        "fetch",
        hbm=range(18),
        scratch=[pltpu.SemaphoreType.DMA((18,))],
        limit=4,
        behind=(block_out,),
    )
    qkvo_grad, payload = call(
        functools.partial(last_sum_kernel, direct),
        [sds((rows, packed_cols), f32), pltpu.HBM((everyone, 1, 3 * BLK), f32)],
        (down_squares, in_squares, *last_parts),
        "last_sum",
        scratch=[
            pltpu.VMEM((everyone, 1, 3 * BLK), f32),
            pltpu.VMEM((LINES + 8, BLK), f32),
            pltpu.SemaphoreType.DMA,
        ],
        behind=(fetched[0],),
    )
    told = lax.all_to_all(payload, ("dp", "tp"), 0, 0)
    shapes = [(m.shape, kind) for m in matrices[::3] for kind in (f32, f32, f32, bf16)]
    norm, *updated = call(
        adam_kernel,
        [
            sds((1, 1), f32),
            *(sds(shape, kind) for shape, kind in shapes),
            *[sds(norm_gains.shape, f32)] * 4,
            *[sds((heads_here, BUCKETS), f32)] * 3,
        ],
        (told, qkvo_grad, in_grad, down_grad, *fetched),
        "adam",
        scratch=[pltpu.VMEM(norm_gains.shape, f32), pltpu.VMEM((heads_here, BUCKETS), f32)],
    )
    return (block_out, input_grad, norm.reshape(()), *updated[:-3], *(t.T for t in updated[-3:]))


def solution(mesh):
    row = P("dp", None)
    matrix = P("dp", "tp")
    stack = P(None, "dp", "tp")
    table = P(None, "tp")
    share = P(("dp", "tp"), None)
    in_specs = (
        *(row,) * 3,
        P(),
        *(stack,) * 3,
        *(matrix,) * 9,
        *(P(),) * 3,
        *(table,) * 3,
    )
    out_specs = (
        *(share,) * 2,
        P(),
        *(stack,) * 4,
        *(matrix,) * 12,
        *(P(),) * 4,
        *(table,) * 3,
    )
    return jax.shard_map(
        functools.partial(on_device, mesh.shape["dp"]),
        mesh=mesh,
        in_specs=in_specs,
        out_specs=out_specs,
        check_vma=False,
    )
```

```python
import functools
import math

import jax
import jax.numpy as jnp
from jax import lax
from jax.experimental import pallas as pl
from jax.experimental.pallas import tpu as pltpu
from jax.sharding import PartitionSpec as P

HEADS = 12
HDIM = 64
BUCKETS = 32
LEN = 512
BLK = 128
WIN = LEN + BLK
SMALL = 8
LINES = 16


eps_norm = 1e-06
clip_norm = 1.0
beta_one = 0.9
beta_two = 0.999
adam_eps = 1e-08
decay_rate = 0.01
adam_step = 10.0
mask_fill = -1000000000.0
rate_small = 0.02
rate_large = 0.5
gelu_coef = 0.044715
root_coef = math.sqrt(2.0 / math.pi)

f32 = jnp.float32
bf16 = jnp.bfloat16
sds = jax.ShapeDtypeStruct


def dot_nn(a, b):
    return lax.dot_general(a, b, (((1,), (0,)), ((), ())), preferred_element_type=f32)


def dot_nt(a, b):
    return lax.dot_general(a, b, (((1,), (1,)), ((), ())), preferred_element_type=f32)


def dot_tn(a, b):
    return lax.dot_general(a, b, (((0,), (0,)), ((), ())), preferred_element_type=f32)


def after(value, *deps):
    return lax.optimization_barrier((value, *deps))[0]


def call(body, outs, args, name, hbm=(), scratch=(), limit=16, behind=()):
    spaces = [pl.ANY if i in hbm else pltpu.VMEM for i in range(len(args))]
    args = [after(args[0], *behind), *args[1:]] if behind else args
    args = [
        pltpu.with_memory_space_constraint(a, pltpu.HBM) if i in hbm else a for i, a in enumerate(args)
    ]
    return pl.pallas_call(
        body,
        out_shape=tuple(outs),
        in_specs=[pl.BlockSpec(memory_space=space) for space in spaces],
        out_specs=tuple(
            pl.BlockSpec(memory_space=pl.ANY if hasattr(o, "memory_space") else pltpu.VMEM) for o in outs
        ),
        scratch_shapes=list(scratch),
        compiler_params=pltpu.CompilerParams(vmem_limit_bytes=limit << 20),
        cost_estimate=pl.CostEstimate(flops=0, bytes_accessed=0, transcendentals=0),
        name=name,
    )(*args)


def to_hbm(staged, out, sem):
    copy = pltpu.make_async_copy(staged, out, sem)
    copy.start()
    copy.wait()


def assemble(into, blocks, start_col=0):
    cols = slice(start_col, start_col + into.shape[1])
    if len(blocks) == 1:
        into[...] = blocks[0][:, cols]
        return
    me = lax.axis_index("dp")
    rows = blocks[0].shape[0]
    for e, block in enumerate(blocks):
        start = pl.multiple_of((me ^ e) * rows, 32)
        into[pl.ds(start, rows), :] = block[:, cols]


def spread(grad, outs, order=(1, 2, 4)):
    if len(outs) == 1:
        outs[0][...] = grad[...].astype(bf16)
        return
    me = lax.axis_index("dp")
    rows = outs[0].shape[1]
    keep, *send = outs
    for b in range(2):
        for k in range(4):
            out, at = (keep, k) if b == 0 else (send[0], k) if len(send) == 1 else (send[1 - (k >> 1)], k & 1)
            apart = b * order[0] ^ (k >> 1) * order[1] ^ (k & 1) * order[2]
            start = pl.multiple_of((me ^ apart) * rows, 32)
            block = grad[pl.ds(start, rows), :].astype(bf16)
            if len(out.shape) == 2:
                out[at * rows : (at + 1) * rows, :] = block
            else:
                out[at] = block


def spread_shapes(dp, width, cols, lengths):
    if dp == 8:
        return [sds((n, width // dp, cols), bf16) for n in lengths]
    return [sds((width, cols), bf16)]


def half_rows():
    core = lax.axis_index("tp") & 1
    for half in range(2):
        for at in range(2):
            start = pl.multiple_of(((core ^ half) + 2 * at) * BLK, BLK)
            yield half, at, pl.ds(start, BLK)


def pack_kernel(qkv, out, down, ffn_in, packed, packed_ffn, *scratch):
    *landed, sems = scratch
    copies = [
        pltpu.make_async_copy(source, to, sems.at[i])
        for i, (source, to) in enumerate(zip((qkv, out, down, ffn_in), landed))
    ]
    for copy in copies:
        copy.start()
    local = out.shape[1]
    copies[0].wait()
    copies[1].wait()
    for part in range(3):
        packed[:, part * local : (part + 1) * local] = landed[0][part].astype(bf16)
    packed[:, 3 * local :] = landed[1][...].astype(bf16)
    width = down.shape[1]
    for i in (2, 3):
        copies[i].wait()
        packed_ffn[:, (i - 2) * width : (i - 1) * width] = landed[i][...].astype(bf16)


def prep_kernel(
    seg_in, table_in, bucket_in, x_in, gains_in, dy_in, act, act_t, bias, bucket, x, gains, dy, seg, table, ids, sems
):
    sources = (x_in, gains_in, bucket_in, seg_in, table_in, dy_in)
    copies = [
        pltpu.make_async_copy(source, to, sems.at[i])
        for i, (source, to) in enumerate(zip(sources, (x, gains, ids, seg, table, dy)))
    ]
    for copy in copies:
        copy.start()
    copies[0].wait()
    copies[1].wait()
    values = x[...].astype(f32)
    scale = lax.rsqrt(jnp.mean(values * values, axis=-1, keepdims=True) + eps_norm)
    low = (values * scale * gains[0:1, :]).astype(bf16)
    act[...] = low
    act_t[...] = low.T
    for copy in copies[2:]:
        copy.wait()
    ends = [seg[0, 0]]
    for k in (1, 2):
        ends.append(ends[-1] + seg[0, k])

    def segment_of(position):
        return sum((position >= end).astype(jnp.int32) for end in ends)

    seg_cols = segment_of(lax.broadcasted_iota(jnp.int32, (1, LEN), 1))
    heads = bias.shape[0]
    bucket[...] = jnp.zeros_like(bucket)
    bucket[:, : 2 * LEN - 1] = ids[...]
    lines = []
    for h in range(heads):
        line = jnp.zeros((1, 2 * LEN), f32)
        for b in range(BUCKETS):
            line = jnp.where(bucket[...] == b, table[h, b], line)
        lines.append(line)
    for r in range(LEN // BLK):
        seg_rows = segment_of(lax.broadcasted_iota(jnp.int32, (BLK, 1), 0) + r * BLK)
        visible = seg_rows == seg_cols
        low_at = LEN - BLK - r * BLK
        for h in range(heads):
            window = jnp.broadcast_to(lines[h][:, low_at : low_at + WIN], (BLK, WIN))
            turned = pltpu.roll(window, 1, 1, stride=1, stride_axis=0)
            bias[h, r * BLK : (r + 1) * BLK, :] = jnp.where(visible, turned[:, BLK:], mask_fill)


def attend_kernel(n_blocks, act, bias, *rest):
    blocks = rest[:n_blocks]
    weights, qkv, prob, mixed, *halves = rest[n_blocks:]
    assemble(weights, blocks)
    width = qkv.shape[1] // 3
    qkv[...] = dot_nn(act[...], weights[:, : 3 * width]).astype(bf16)
    for h in range(bias.shape[0]):
        cols = slice(h * HDIM, (h + 1) * HDIM)
        query, key, value = (qkv[:, s * width + h * HDIM : s * width + (h + 1) * HDIM] for s in range(3))
        scores = dot_nt(query, key) + bias[h]
        top = jnp.max(scores, axis=-1, keepdims=True)
        exps = jnp.exp(scores - top)
        total = jnp.sum(exps, axis=-1, keepdims=True)
        low = (exps * (1.0 / total)).astype(bf16)
        prob[h] = low
        mixed[:, cols] = dot_nn(low, value).astype(bf16)
    out_cols = weights[:, 3 * width :]
    for half, at, rows in half_rows():
        halves[2 * half + at][...] = dot_nt(mixed[rows, :], out_cols).astype(bf16)


def ffn_kernel(n_blocks, x, gains, dy, own_a, own_b, other_a, other_b, *rest):
    blocks = rest[:n_blocks]
    resid, act, hidden, pre_grad, keep, send, down, weights, hidden_grad = rest[n_blocks:]
    assemble(down, blocks)
    assemble(weights, blocks, down.shape[1])
    hidden_grad[...] = dot_nn(dy[...], down[...])
    for half, at, rows in half_rows():
        here = slice(at * BLK, (at + 1) * BLK)
        attn = ((own_a, own_b), (other_a, other_b))[half][at]
        values = x[rows, :].astype(f32) + attn[...].astype(f32)
        resid[rows, :] = values
        scale = lax.rsqrt(jnp.mean(values * values, axis=-1, keepdims=True) + eps_norm)
        low = (values * scale * gains[1:2, :]).astype(bf16)
        act[rows, :] = low
        u = dot_nn(low, weights[...])
        square = u * u
        tanh_part = jnp.tanh(root_coef * (u + gelu_coef * square * u))
        hidden[rows, :] = (0.5 * u * (1.0 + tanh_part)).astype(bf16)
        inner = root_coef * (1.0 + 3.0 * gelu_coef * square)
        slope = 0.5 * (1.0 + tanh_part) + 0.5 * u * (1.0 - tanh_part * tanh_part) * inner
        du = (hidden_grad[rows, :] * slope).astype(bf16)
        pre_grad[rows, :] = du
        (send if half else keep)[here, :] = dot_nt(du, weights[...]).astype(bf16)


def row_products(weights, grad):
    products = weights.astype(f32) * grad
    width = grad.shape[1]
    folded = sum(products[:, c : c + BLK] for c in range(0, width - BLK + 1, BLK))
    if width % BLK:
        rest = products[:, width - width % BLK :]
        wide = jnp.zeros((grad.shape[0], BLK - width % BLK), f32)
        folded = folded + jnp.concatenate([rest, wide], axis=1)
    return jnp.sum(folded.T, axis=0, keepdims=True)


def down_grad_kernel(order, left, right, *rest):
    outs, grad = rest[:-1], rest[-1]
    grad[...] = dot_tn(left[...], right[...])
    spread(grad, outs, order)


def in_grad_kernel(order, left, right, weights, gains, *rest):
    *outs, gain_part, grad = rest
    grad[...] = dot_tn(left[...], right[...])
    spread(grad, outs, order)
    gain_part[...] = row_products(weights[...], grad[...]) / gains[1:2, :]


def turn_kernel(prob, out):
    for h in range(prob.shape[0]):
        out[h] = prob[h].T


def attend_back_kernel(
    n_outs, resid, dy, gains, own, other, weights, qkv, prob, prob_t, mixed, act_t, bucket, gain_two, *rest
):
    outs = rest[:n_outs]
    share_grad, small, proj_grad, resid_low, grad, diag = rest[n_outs:]
    chip = lax.axis_index("tp") >> 1
    width = qkv.shape[1] // 3
    for half, at, rows in half_rows():
        here = slice(at * BLK, (at + 1) * BLK)
        act_grad = (other if half else own)[here, :].astype(f32)
        values = resid[rows, :]
        scale = lax.rsqrt(jnp.mean(values * values, axis=-1, keepdims=True) + eps_norm)
        normed = values * scale
        normal_grad = act_grad * gains[1:2, :]
        mean_part = jnp.mean(normal_grad * normed, axis=-1, keepdims=True)
        total = dy[rows, :].astype(f32) + scale * (normal_grad - normed * mean_part)
        resid_low[rows, :] = total.astype(bf16)
        if half == 0:

            @pl.when(chip == at)
            def _():
                share_grad[...] = total

    mix_grad = dot_nn(resid_low[...], weights[:, 3 * width :]).astype(bf16)
    heads = prob.shape[0]
    row = lax.broadcasted_iota(jnp.int32, (BLK, BLK), 0)
    col = lax.broadcasted_iota(jnp.int32, (BLK, BLK), 1)
    flip = (row + col == BLK - 1).astype(f32).astype(bf16)
    diag[...] = jnp.zeros_like(diag)
    for h in range(heads):
        query, key, value = (qkv[:, s * width + h * HDIM : s * width + (h + 1) * HDIM] for s in range(3))
        grad_rows = mix_grad[:, h * HDIM : (h + 1) * HDIM]
        prob_grad = dot_nt(grad_rows, value)
        prob_here = prob[h].astype(f32)
        row_dot = jnp.sum(prob_here * prob_grad, axis=-1, keepdims=True)
        low = (prob_here * (prob_grad - row_dot)).astype(bf16)
        for r in range(LEN // BLK):
            flipped = dot_nn(flip, low[r * BLK : (r + 1) * BLK, :])
            wide = jnp.concatenate([flipped, jnp.zeros((BLK, BLK), f32)], axis=1)
            turned = pltpu.roll(wide, 0, 1, stride=1, stride_axis=0)
            low_at = LEN - BLK - r * BLK
            diag[h : h + 1, low_at : low_at + WIN] += jnp.sum(turned, axis=0, keepdims=True)
        for s, part in enumerate((dot_nn(low, key), dot_tn(low, query), dot_nn(prob_t[h], grad_rows))):
            proj_grad[:, s * width + h * HDIM : s * width + (h + 1) * HDIM] = part.astype(bf16)
    grad[:, : 3 * width] = dot_nn(act_t[...], proj_grad[...])
    grad[:, 3 * width :] = dot_tn(resid_low[...], mixed[...])
    onehot = (lax.broadcasted_iota(jnp.int32, (BUCKETS, 2 * LEN), 0) == bucket[...]).astype(f32)
    by_bucket = lax.dot_general(
        diag[...],
        onehot,
        (((1,), (1,)), ((), ())),
        precision=lax.Precision.HIGHEST,
        preferred_element_type=f32,
    )
    first = lax.axis_index("tp") * heads
    cells = [
        sum(jnp.where(first + h == head, by_bucket[h : h + 1, :], 0.0) for h in range(heads))
        for head in range(HEADS)
    ]
    model = gains.shape[1]
    cells.append(jnp.zeros((1, model - HEADS * BUCKETS), f32))
    gain_one = row_products(weights[:, : 3 * width], grad[:, : 3 * width]) / gains[0:1, :]
    lines = (gain_one, gain_two[...], jnp.concatenate(cells, axis=1), jnp.zeros((SMALL - 3, model), f32))
    whole = jnp.concatenate(lines, axis=0)
    if n_outs == 1:
        spread(grad, outs)
        small[...] = whole
        return
    keep, low = outs
    rows = keep.shape[1]
    spread(grad, (keep, small, low))
    small[2 * rows :, :] = whole.astype(bf16)


def ffn_out_kernel(hidden, down, keep, *send):
    for half, at, rows in half_rows():
        block = dot_nt(hidden[rows, :], down[...]).astype(bf16)
        if half:
            send[at][...] = block
        else:
            keep[at * BLK : (at + 1) * BLK, :] = block


def act_grad_kernel(proj_grad, weights, keep, *send):
    width = proj_grad.shape[1]
    for half, at, rows in half_rows():
        block = dot_nt(proj_grad[rows, :], weights[:, :width]).astype(bf16)
        if half:
            send[at][...] = block
        else:
            keep[at * BLK : (at + 1) * BLK, :] = block


def core_add_kernel(*refs):
    *before, keep, got_a, got_b, mine, theirs = refs
    chip = lax.axis_index("tp") >> 1
    first = mine.shape[0] - BLK
    for to, block in zip((mine, theirs), before):
        to[:BLK, :] = block[...]
    for at, got in enumerate((got_a, got_b)):
        here = slice(at * BLK, (at + 1) * BLK)
        value = (keep[here, :].astype(f32) + got[...].astype(f32)).astype(bf16)

        @pl.when(chip == at)
        def _():
            mine[first:, :] = value

        @pl.when(chip != at)
        def _():
            theirs[first:, :] = value


def share_out_kernel(resid, x, gains, share_grad, mine, got, block_out, input_grad):
    share = pl.ds(pl.multiple_of(lax.axis_index("tp") * BLK, BLK), BLK)
    first, second = slice(0, BLK), slice(BLK, 2 * BLK)
    ffn = mine[first, :].astype(f32) + got[first, :].astype(f32)
    block_out[...] = (resid[share, :] + ffn).astype(bf16)
    values = x[share, :].astype(f32)
    scale = lax.rsqrt(jnp.mean(values * values, axis=-1, keepdims=True) + eps_norm)
    normed = values * scale
    normal_grad = (mine[second, :].astype(f32) + got[second, :].astype(f32)) * gains[0:1, :]
    mean_part = jnp.mean(normal_grad * normed, axis=-1, keepdims=True)
    input_grad[...] = share_grad[...] + scale * (normal_grad - normed * mean_part)


def add_kernel(one, two, out):
    out[...] = (one[...].astype(f32) + two[...].astype(f32)).astype(bf16)


def pair_add_kernel(keep, got, mine, theirs):
    for k in range(4):
        to = theirs if k >= 2 else mine
        to[k % 2] = (keep[k].astype(f32) + got[k].astype(f32)).astype(bf16)


def high_add_kernel(keep, got, theirs):
    for k in range(2):
        theirs[k] = (keep[k + 2].astype(f32) + got[k].astype(f32)).astype(bf16)


def late_add_kernel(keep, got_low, got, mine, theirs):
    for k, to in enumerate((mine, theirs)):
        to[...] = (keep[k].astype(f32) + got_low[k].astype(f32) + got[k].astype(f32)).astype(bf16)


def next_add_kernel(keep, got, mine, theirs):
    for k, to in enumerate((mine, theirs)):
        to[...] = (keep[k].astype(f32) + got[k].astype(f32)).astype(bf16)


def last_high_kernel(keep, sent, got, out):
    rows = keep.shape[1]
    for k in range(2):
        here = slice(k * rows, (k + 1) * rows)
        out[here, :] = (keep[k + 2].astype(f32) + got[here, :].astype(f32)).astype(bf16)
    small = slice(2 * rows, None)
    out[small, :] = (sent[small, :].astype(f32) + got[small, :].astype(f32)).astype(bf16)


def last_late_kernel(keep, got_low, sent, got, mine, out):
    rows = keep.shape[1]
    first, second, small = slice(0, rows), slice(rows, 2 * rows), slice(2 * rows, None)
    mine[...] = keep[0].astype(f32) + got_low[0].astype(f32) + got[first, :].astype(f32)
    block = keep[1].astype(f32) + got_low[1].astype(f32) + got[second, :].astype(f32)
    out[:rows, :] = block.astype(bf16)
    out[rows:, :] = (sent[small, :].astype(f32) + got[small, :].astype(f32)).astype(bf16)


def fold(values):
    rows, cols = values.shape
    squares = values * values
    lanes = sum(squares[:, c : c + BLK] for c in range(0, cols, BLK))
    return jnp.sum(lanes, axis=0, keepdims=True)


def sum_kernel(n_parts, *rest):
    parts, (grad, squares) = rest[:n_parts], rest[n_parts:]
    total = sum(part[...].astype(f32) for part in parts)
    grad[...] = total
    squares[...] = fold(total)


def last_sum_kernel(direct, extra_a, extra_b, *rest):
    *parts, grad, out, payload, lines, sem = rest
    if direct:
        mine, sent, got = parts
        rows = mine.shape[0]
        total = mine[...] + got[:rows, :].astype(f32)
        small = sent[rows:, :].astype(f32) + got[rows:, :].astype(f32)
    else:
        total, small = (part[...] for part in parts)
    grad[...] = total
    per_row = total.shape[1] // BLK
    lines[...] = jnp.zeros_like(lines)
    for line in range(LINES):
        row, at = divmod(line, per_row)
        lines[line : line + 1, :] = small[row : row + 1, at * BLK : (at + 1) * BLK]
    me = lax.axis_index("dp")
    start = pl.multiple_of(jnp.minimum(2 * me, LINES), 2)
    squares = fold(total) + extra_a[...] + extra_b[...]
    two = lines[pl.ds(start, 2), :]
    told = jnp.concatenate((squares, two[0:1, :], two[1:2, :]), axis=1)
    payload[...] = jnp.broadcast_to(told[None], payload.shape)
    to_hbm(payload, out, sem)


def adamw(weight, gradient, moment_one, moment_two, rate):
    one_new = beta_one * moment_one + (1.0 - beta_one) * gradient
    two_new = beta_two * moment_two + (1.0 - beta_two) * gradient * gradient
    root = math.sqrt(1.0 - beta_two**adam_step)
    scale = rate * root / (1.0 - beta_one**adam_step)
    step = scale * one_new / (jnp.sqrt(two_new) + adam_eps * root)
    return (weight * (1.0 - rate * decay_rate) - step, one_new, two_new)


def fetch_kernel(*refs):
    count = len(refs) // 2
    copies = [pltpu.make_async_copy(refs[i], refs[count + i], refs[-1].at[i]) for i in range(count)]
    for copy in copies:
        copy.start()
    for copy in copies:
        copy.wait()


def adam_kernel(*refs):
    told, grad_qkvo, grad_in, grad_down, *state = refs[:22]
    norm_ref, *matrices, gains_a, gains_b, gains_c, gains_grad, table_a, table_b, table_c = refs[22:46]
    gains_sum, table_grad = refs[46:]
    gains_o, table_o = (gains_a, gains_b, gains_c), (table_a, table_b, table_c)
    qkv, out, ffn_in, ffn_down, gains, table = (state[i : i + 3] for i in range(0, 18, 3))
    qkv_o, out_o, in_o, down_o = (matrices[i : i + 4] for i in range(0, 16, 4))
    tp = lax.axis_size("tp")
    squares = told[0, :, :BLK]
    for i in range(1, told.shape[0]):
        squares = squares + told[i, :, :BLK]
    model = gains_sum.shape[1]
    per_row = model // BLK
    per_line = BLK // BUCKETS
    first = lax.axis_index("tp") * table_grad.shape[0]
    for line in range(2 * per_row + HEADS // per_line):
        index, at = divmod(line, 2)
        cols = slice((at + 1) * BLK, (at + 2) * BLK)
        value = told[index * tp, :, cols]
        for i in range(1, tp):
            value = value + told[index * tp + i, :, cols]
        squares = squares + value * value
        row, at = divmod(line, per_row)
        if row < 2:
            gains_sum[row : row + 1, at * BLK : (at + 1) * BLK] = value
            continue
        for i in range(per_line):
            head = at * per_line + i
            cell = value[:, i * BUCKETS : (i + 1) * BUCKETS]
            for h in range(table_grad.shape[0]):

                @pl.when(first + h == head)
                def _():
                    table_grad[h : h + 1, :] = cell

    norm = jnp.sqrt(jnp.sum(squares, axis=1, keepdims=True))
    norm_ref[...] = norm
    factor = clip_norm / jnp.maximum(norm, clip_norm)

    def update(state_refs, gradient, to, rate, at=...):
        new = adamw(state_refs[0][at], gradient * factor, state_refs[1][at], state_refs[2][at], rate)
        for ref, value in zip(to, new):
            ref[at] = value
        if len(to) == 4:
            to[3][at] = new[0].astype(bf16)

    update(ffn_in, grad_in[...], in_o, rate_small)
    update(ffn_down, grad_down[...], down_o, rate_small)
    width = qkv[0].shape[2]
    for part in range(3):
        update(qkv, grad_qkvo[:, part * width : (part + 1) * width], qkv_o, rate_small, part)
    update(out, grad_qkvo[:, 3 * width :], out_o, rate_large)
    update(gains, gains_sum[...], gains_o, rate_large)
    gains_grad[...] = gains_sum[...] * factor
    update(table, table_grad[...], table_o, rate_large)


def on_device(
    dp,
    inputs,
    cotangent,
    seg_lengths,
    bucket_ids,
    qkv_weight,
    qkv_first,
    qkv_second,
    out_weight,
    out_first,
    out_second,
    ffn_in_weight,
    ffn_in_first,
    ffn_in_second,
    ffn_down_weight,
    ffn_down_first,
    ffn_down_second,
    norm_gains,
    gains_first,
    gains_second,
    bias_table,
    table_first,
    table_second,
):
    tokens, model = inputs.shape
    rows, local = out_weight.shape
    hidden = ffn_in_weight.shape[1]
    heads_here = local // HDIM
    tp = lax.axis_size("tp")
    packed_cols = 4 * local
    direct = dp == 8

    def swap_dp(value, distance):
        return lax.ppermute(value, "dp", [(i, i ^ distance) for i in range(dp)])

    def swap_tp(value, distance):
        return lax.ppermute(value, "tp", [(i, i ^ distance) for i in range(tp)])

    def add(one, two, behind=()):
        (out,) = call(add_kernel, [sds(one.shape, bf16)], (one, two), "add", limit=4, behind=behind)
        return out

    def pair_add(keep, got, behind):
        outs = [sds((2, *keep.shape[1:]), bf16)] * 2
        return call(pair_add_kernel, outs, (keep, got), "pair_add", limit=4, behind=behind)

    def high_add(keep, got, behind):
        outs = [sds((2, *keep.shape[1:]), bf16)]
        (out,) = call(high_add_kernel, outs, (keep, got), "high_add", limit=4, behind=behind)
        return out

    def late_add(keep, got_low, got, behind):
        outs = [sds(keep.shape[1:], bf16)] * 2
        return call(late_add_kernel, outs, (keep, got_low, got), "late_add", limit=4, behind=behind)

    def next_add(keep, got, behind):
        outs = [sds(keep.shape[1:], bf16)] * 2
        return call(next_add_kernel, outs, (keep, got), "next_add", limit=4, behind=behind)

    half_shape = [sds((tokens // 2, model), bf16)] * 2
    matrices = (qkv_weight, out_weight, ffn_down_weight, ffn_in_weight)
    packed, packed_ffn = call(
        pack_kernel,
        [sds((rows, packed_cols), bf16), sds((rows, 2 * hidden), bf16)],
        matrices,
        "pack",
        hbm=(0, 1, 2, 3),
        scratch=[*(pltpu.VMEM(m.shape, f32) for m in matrices), pltpu.SemaphoreType.DMA((4,))],
    )
    ids = bucket_ids[None, :]
    act_one, act_one_t, bias, bucket_row, inputs, norm_gains_here, cotangent = call(
        prep_kernel,
        [
            sds((tokens, model), bf16),
            sds((model, tokens), bf16),
            sds((heads_here, LEN, LEN), f32),
            sds((1, 2 * LEN), jnp.int32),
            sds(inputs.shape, bf16),
            sds(norm_gains.shape, f32),
            sds(inputs.shape, bf16),
        ],
        (seg_lengths, bias_table.T, ids, inputs, norm_gains, cotangent),
        "prep",
        hbm=range(6),
        scratch=[
            pltpu.SMEM(seg_lengths.shape, jnp.int32),
            pltpu.SMEM((heads_here, BUCKETS), f32),
            pltpu.VMEM(ids.shape, jnp.int32),
            pltpu.SemaphoreType.DMA((6,)),
        ],
    )
    if direct:
        one, two = swap_dp(packed, 2), swap_dp(packed, 4)
        own, ffn_own = swap_dp(after(packed, act_one), 1), swap_dp(after(packed_ffn, act_one), 1)
        one_across = swap_dp(one, 1)
        three = swap_dp(two, 2)
        ffn_two = swap_dp(after(packed_ffn, two), 4)
        two_across = swap_dp(two, 1)
        ffn_one = swap_dp(after(packed_ffn, two, own), 2)
        three_across = swap_dp(three, 1)
        qkvo_blocks = [packed, own, one, one_across, two, two_across, three, three_across]
        ffn_three = swap_dp(after(ffn_two, ffn_one), 2)
        ffn_blocks = [packed_ffn, ffn_own, ffn_one, swap_dp(after(ffn_own, ffn_one), 2)]
        for block in (ffn_two, ffn_three):
            ffn_blocks += [block, swap_dp(block, 1)]
        bias = after(bias, ffn_own, one_across)
        ffn_first, ffn_early = (ffn_two,), (ffn_blocks[5], ffn_three)
    else:
        qkvo_blocks = [lax.all_gather(packed, "dp", axis=0, tiled=True)]
        ffn_first = ffn_blocks = ffn_early = [lax.all_gather(packed_ffn, "dp", axis=0, tiled=True)]
    n_blocks = len(qkvo_blocks)

    weights_one, qkv, prob, mixed, *attn_parts = call(
        functools.partial(attend_kernel, n_blocks),
        [
            sds((model, packed_cols), bf16),
            sds((tokens, 3 * local), bf16),
            sds((heads_here, LEN, LEN), bf16),
            sds((tokens, local), bf16),
            *[sds((BLK, model), bf16)] * 4,
        ],
        (act_one, bias, *qkvo_blocks),
        "attend",
    )
    half_blocks = [sds((BLK, model), bf16)] * 2
    attn_got = [swap_tp(after(part, *ffn_first), 1) for part in attn_parts[2:]]
    attn_first = [add(part, got) for part, got in zip(attn_parts, attn_got)]
    attn_own = [add(first, swap_tp(first, 2), ffn_early) for first in attn_first]
    attn_sums = (*attn_own, *(swap_tp(own, 1) for own in attn_own))
    resid, act_two, hidden_act, pre_grad, back_keep, back_send, down_full, in_full = call(
        functools.partial(ffn_kernel, n_blocks),
        [
            sds((tokens, model), f32),
            sds((tokens, model), bf16),
            sds((tokens, hidden), bf16),
            sds((tokens, hidden), bf16),
            *half_shape,
            *[sds((model, hidden), bf16)] * 2,
        ],
        (inputs, norm_gains_here, cotangent, *attn_sums, *ffn_blocks),
        "ffn",
        scratch=[pltpu.VMEM((tokens, hidden), f32)],
    )
    down_order, in_order = (2, 4, 1), (1, 2, 4)
    grad_scratch = [pltpu.VMEM((model, hidden), f32)]
    down_parts = call(
        functools.partial(down_grad_kernel, down_order),
        spread_shapes(dp, model, hidden, (4, 2, 2)),
        (cotangent, hidden_act),
        "down_grad",
        scratch=grad_scratch,
    )
    back_first = add(back_keep, swap_tp(back_send, 1), down_parts[:1])
    back_got = swap_tp(back_first, 2)
    *in_parts, gain_two_part = call(
        functools.partial(in_grad_kernel, in_order),
        [*spread_shapes(dp, model, hidden, (4, 4)), sds((1, model), f32)],
        (act_two, after(pre_grad, back_first), in_full, norm_gains_here),
        "in_grad",
        scratch=grad_scratch,
    )
    share_shapes = [half_shape[0], *half_blocks]
    ffn_keep, *ffn_send = call(
        ffn_out_kernel, share_shapes, (hidden_act, down_full), "ffn_out", behind=(gain_two_part,)
    )
    ffn_got = [swap_tp(part, 1) for part in ffn_send]
    ffn_sums = call(core_add_kernel, half_blocks, (ffn_keep, *ffn_got), "ffn_add", limit=4)
    attend_behind = ()
    back_behind = ffn_sums[:1]
    if direct:
        down_keep, down_high, down_low = down_parts
        down_got = swap_dp(down_high, down_order[0])
        back_behind = (*back_behind, down_got)
    (prob_t,) = call(turn_kernel, [sds(prob.shape, bf16)], (prob,), "turn", behind=ffn_sums[:1])
    back_sum = add(back_first, back_got, (*back_behind, prob_t))
    if direct:
        down_one = high_add(down_keep, down_got, (back_sum,))
        attend_behind = (down_one,)
    everyone = dp * tp
    qkvo_shapes = spread_shapes(dp, model, packed_cols, (4, 2))
    small_shape = sds((2 * rows + SMALL, model), bf16) if direct else sds((SMALL, model), f32)
    *qkvo_parts, share_grad, small, proj_grad = call(
        functools.partial(attend_back_kernel, len(qkvo_shapes)),
        [*qkvo_shapes, sds((BLK, model), f32), small_shape, sds((tokens, 3 * local), bf16)],
        (
            resid,
            cotangent,
            norm_gains_here,
            back_sum,
            swap_tp(back_sum, 1),
            weights_one,
            qkv,
            prob,
            prob_t,
            mixed,
            act_one_t,
            bucket_row,
            gain_two_part,
        ),
        "attend_back",
        scratch=[
            pltpu.VMEM((tokens, model), bf16),
            pltpu.VMEM((model, packed_cols), f32),
            pltpu.VMEM((8, 2 * LEN), f32),
        ],
        behind=attend_behind,
    )
    def summed(parts, behind):
        return call(
            functools.partial(sum_kernel, len(parts)),
            [sds((rows, parts[0].shape[1]), f32), sds((1, BLK), f32)],
            parts,
            "sum_parts",
            limit=4,
            behind=behind,
        )

    def act_shares(behind):
        keep, *send = call(
            act_grad_kernel, share_shapes, (proj_grad, weights_one), "act_grad", behind=behind
        )
        return (keep, *(swap_tp(part, 1) for part in send))

    def share_sums(shares, behind):
        outs = [sds((2 * BLK, model), bf16)] * 2
        return call(core_add_kernel, outs, (*ffn_sums, *shares), "core_add", limit=4, behind=behind)

    if direct:
        keep, send_low = qkvo_parts
        in_keep, in_send = in_parts
        in_one = pair_add(in_keep, swap_dp(in_send, in_order[0]), (proj_grad,))
        got_high = swap_dp(after(small, *in_one), 1)
        act_parts = act_shares(in_one)
        down_rest = (swap_dp(down_low, down_order[0]), swap_dp(down_one, down_order[1]))
        down_two = late_add(down_keep, *down_rest, act_parts[:1])
        (high,) = call(
            last_high_kernel, [small_shape], (keep, small, got_high), "last_high", limit=4, behind=down_two
        )
        got_low = swap_dp(after(send_low, high), 1)
        down_grad, down_squares = summed((down_two[0], swap_dp(down_two[1], down_order[2])), (high,))
        in_two = next_add(in_one[0], swap_dp(in_one[1], in_order[1]), (down_grad,))
        mine, theirs = share_sums(act_parts, in_two)
        in_grad, in_squares = summed((in_two[0], swap_dp(in_two[1], in_order[2])), (mine,))
        last, late = call(
            last_late_kernel,
            [sds((rows, packed_cols), f32), sds((rows + SMALL, packed_cols), bf16)],
            (keep, got_low, high, swap_dp(high, 2)),
            "last_late",
            limit=4,
            behind=(in_grad,),
        )
        last_parts = (last, late, swap_dp(late, 4))
        share_behind = (late,)
    else:
        qkvo_sums, down_sums, in_sums = (
            (lax.psum_scatter(p[0].astype(f32), "dp", scatter_dimension=0, tiled=True),)
            for p in (qkvo_parts, down_parts, in_parts)
        )
        last_parts = (*qkvo_sums, lax.psum(small, "dp"))
        down_grad, down_squares = summed(down_sums, ())
        in_grad, in_squares = summed(in_sums, ())
        mine, theirs = share_sums(act_shares(()), ())
        share_behind = ()
    block_out, input_grad = call(
        share_out_kernel,
        [sds((BLK, model), bf16), sds((BLK, model), f32)],
        (resid, inputs, norm_gains_here, share_grad, mine, swap_tp(theirs, 2)),
        "share_out",
        behind=share_behind,
    )
    matrices = (
        qkv_weight,
        qkv_first,
        qkv_second,
        out_weight,
        out_first,
        out_second,
        ffn_in_weight,
        ffn_in_first,
        ffn_in_second,
        ffn_down_weight,
        ffn_down_first,
        ffn_down_second,
    )
    vectors = (norm_gains, gains_first, gains_second, bias_table.T, table_first.T, table_second.T)
    state = matrices + vectors
    fetched = call(
        fetch_kernel,
        [sds(m.shape, f32) for m in state],
        state,
        "fetch",
        hbm=range(18),
        scratch=[pltpu.SemaphoreType.DMA((18,))],
        limit=4,
        behind=(block_out,),
    )
    qkvo_grad, payload = call(
        functools.partial(last_sum_kernel, direct),
        [sds((rows, packed_cols), f32), pltpu.HBM((everyone, 1, 3 * BLK), f32)],
        (down_squares, in_squares, *last_parts),
        "last_sum",
        scratch=[
            pltpu.VMEM((everyone, 1, 3 * BLK), f32),
            pltpu.VMEM((LINES + 8, BLK), f32),
            pltpu.SemaphoreType.DMA,
        ],
        behind=(fetched[0],),
    )
    told = lax.all_to_all(payload, ("dp", "tp"), 0, 0)
    shapes = [(m.shape, kind) for m in matrices[::3] for kind in (f32, f32, f32, bf16)]
    norm, *updated = call(
        adam_kernel,
        [
            sds((1, 1), f32),
            *(sds(shape, kind) for shape, kind in shapes),
            *[sds(norm_gains.shape, f32)] * 4,
            *[sds((heads_here, BUCKETS), f32)] * 3,
        ],
        (told, qkvo_grad, in_grad, down_grad, *fetched),
        "adam",
        scratch=[pltpu.VMEM(norm_gains.shape, f32), pltpu.VMEM((heads_here, BUCKETS), f32)],
    )
    return (block_out, input_grad, norm.reshape(()), *updated[:-3], *(t.T for t in updated[-3:]))


def solution(mesh):
    row = P("dp", None)
    matrix = P("dp", "tp")
    stack = P(None, "dp", "tp")
    table = P(None, "tp")
    share = P(("dp", "tp"), None)
    in_specs = (
        *(row,) * 3,
        P(),
        *(stack,) * 3,
        *(matrix,) * 9,
        *(P(),) * 3,
        *(table,) * 3,
    )
    out_specs = (
        *(share,) * 2,
        P(),
        *(stack,) * 4,
        *(matrix,) * 12,
        *(P(),) * 4,
        *(table,) * 3,
    )
    return jax.shard_map(
        functools.partial(on_device, mesh.shape["dp"]),
        mesh=mesh,
        in_specs=in_specs,
        out_specs=out_specs,
        check_vma=False,
    )
```

```python
import functools
import math

import jax
import jax.numpy as jnp
from jax import lax
from jax.experimental import pallas as pl
from jax.experimental.pallas import tpu as pltpu
from jax.sharding import PartitionSpec as P

HEADS = 12
HDIM = 64
BUCKETS = 32
LEN = 512
BLK = 128
WIN = LEN + BLK
SMALL = 8
LINES = 16


eps_norm = 1e-06
clip_norm = 1.0
beta_one = 0.9
beta_two = 0.999
adam_eps = 1e-08
decay_rate = 0.01
adam_step = 10.0
mask_fill = -1000000000.0
rate_small = 0.02
rate_large = 0.5
gelu_coef = 0.044715
root_coef = math.sqrt(2.0 / math.pi)

f32 = jnp.float32
bf16 = jnp.bfloat16
sds = jax.ShapeDtypeStruct


def dot_nn(a, b):
    return lax.dot_general(a, b, (((1,), (0,)), ((), ())), preferred_element_type=f32)


def dot_nt(a, b):
    return lax.dot_general(a, b, (((1,), (1,)), ((), ())), preferred_element_type=f32)


def dot_tn(a, b):
    return lax.dot_general(a, b, (((0,), (0,)), ((), ())), preferred_element_type=f32)


def after(value, *deps):
    return lax.optimization_barrier((value, *deps))[0]


def call(body, outs, args, name, hbm=(), scratch=(), limit=16, behind=()):
    spaces = [pl.ANY if i in hbm else pltpu.VMEM for i in range(len(args))]
    args = [after(args[0], *behind), *args[1:]] if behind else args
    args = [
        pltpu.with_memory_space_constraint(a, pltpu.HBM) if i in hbm else a for i, a in enumerate(args)
    ]
    return pl.pallas_call(
        body,
        out_shape=tuple(outs),
        in_specs=[pl.BlockSpec(memory_space=space) for space in spaces],
        out_specs=tuple(
            pl.BlockSpec(memory_space=pl.ANY if hasattr(o, "memory_space") else pltpu.VMEM) for o in outs
        ),
        scratch_shapes=list(scratch),
        compiler_params=pltpu.CompilerParams(vmem_limit_bytes=limit << 20),
        cost_estimate=pl.CostEstimate(flops=0, bytes_accessed=0, transcendentals=0),
        name=name,
    )(*args)


def to_hbm(staged, out, sem):
    copy = pltpu.make_async_copy(staged, out, sem)
    copy.start()
    copy.wait()


def assemble(into, blocks, start_col=0):
    cols = slice(start_col, start_col + into.shape[1])
    if len(blocks) == 1:
        into[...] = blocks[0][:, cols]
        return
    me = lax.axis_index("dp")
    rows = blocks[0].shape[0]
    for e, block in enumerate(blocks):
        start = pl.multiple_of((me ^ e) * rows, 32)
        into[pl.ds(start, rows), :] = block[:, cols]


def spread(grad, outs, order=(1, 2, 4)):
    if len(outs) == 1:
        outs[0][...] = grad[...].astype(bf16)
        return
    me = lax.axis_index("dp")
    rows = outs[0].shape[1]
    keep, *send = outs
    for b in range(2):
        for k in range(4):
            out, at = (keep, k) if b == 0 else (send[0], k) if len(send) == 1 else (send[1 - (k >> 1)], k & 1)
            apart = b * order[0] ^ (k >> 1) * order[1] ^ (k & 1) * order[2]
            start = pl.multiple_of((me ^ apart) * rows, 32)
            block = grad[pl.ds(start, rows), :].astype(bf16)
            if len(out.shape) == 2:
                out[at * rows : (at + 1) * rows, :] = block
            else:
                out[at] = block


def spread_shapes(dp, width, cols, lengths):
    if dp == 8:
        return [sds((n, width // dp, cols), bf16) for n in lengths]
    return [sds((width, cols), bf16)]


def half_rows():
    core = lax.axis_index("tp") & 1
    for half in range(2):
        for at in range(2):
            start = pl.multiple_of(((core ^ half) + 2 * at) * BLK, BLK)
            yield half, at, pl.ds(start, BLK)


def pack_kernel(qkv, out, down, ffn_in, packed, packed_ffn, *scratch):
    *landed, sems = scratch
    copies = [
        pltpu.make_async_copy(source, to, sems.at[i])
        for i, (source, to) in enumerate(zip((qkv, out, down, ffn_in), landed))
    ]
    for copy in copies:
        copy.start()
    local = out.shape[1]
    copies[0].wait()
    copies[1].wait()
    for part in range(3):
        packed[:, part * local : (part + 1) * local] = landed[0][part].astype(bf16)
    packed[:, 3 * local :] = landed[1][...].astype(bf16)
    width = down.shape[1]
    for i in (2, 3):
        copies[i].wait()
        packed_ffn[:, (i - 2) * width : (i - 1) * width] = landed[i][...].astype(bf16)


def prep_kernel(
    seg_in, table_in, bucket_in, x_in, gains_in, dy_in, act, act_t, bias, bucket, x, gains, dy, seg, table, ids, sems
):
    sources = (x_in, gains_in, bucket_in, seg_in, table_in, dy_in)
    copies = [
        pltpu.make_async_copy(source, to, sems.at[i])
        for i, (source, to) in enumerate(zip(sources, (x, gains, ids, seg, table, dy)))
    ]
    for copy in copies:
        copy.start()
    copies[0].wait()
    copies[1].wait()
    values = x[...].astype(f32)
    scale = lax.rsqrt(jnp.mean(values * values, axis=-1, keepdims=True) + eps_norm)
    low = (values * scale * gains[0:1, :]).astype(bf16)
    act[...] = low
    act_t[...] = low.T
    for copy in copies[2:]:
        copy.wait()
    ends = [seg[0, 0]]
    for k in (1, 2):
        ends.append(ends[-1] + seg[0, k])

    def segment_of(position):
        return sum((position >= end).astype(jnp.int32) for end in ends)

    seg_cols = segment_of(lax.broadcasted_iota(jnp.int32, (1, LEN), 1))
    heads = bias.shape[0]
    bucket[...] = jnp.zeros_like(bucket)
    bucket[:, : 2 * LEN - 1] = ids[...]
    lines = []
    for h in range(heads):
        line = jnp.zeros((1, 2 * LEN), f32)
        for b in range(BUCKETS):
            line = jnp.where(bucket[...] == b, table[h, b], line)
        lines.append(line)
    for r in range(LEN // BLK):
        seg_rows = segment_of(lax.broadcasted_iota(jnp.int32, (BLK, 1), 0) + r * BLK)
        visible = seg_rows == seg_cols
        low_at = LEN - BLK - r * BLK
        for h in range(heads):
            window = jnp.broadcast_to(lines[h][:, low_at : low_at + WIN], (BLK, WIN))
            turned = pltpu.roll(window, 1, 1, stride=1, stride_axis=0)
            bias[h, r * BLK : (r + 1) * BLK, :] = jnp.where(visible, turned[:, BLK:], mask_fill)


def attend_kernel(n_blocks, act, bias, *rest):
    blocks = rest[:n_blocks]
    weights, qkv, prob, mixed, *halves = rest[n_blocks:]
    assemble(weights, blocks)
    width = qkv.shape[1] // 3
    qkv[...] = dot_nn(act[...], weights[:, : 3 * width]).astype(bf16)
    for h in range(bias.shape[0]):
        cols = slice(h * HDIM, (h + 1) * HDIM)
        query, key, value = (qkv[:, s * width + h * HDIM : s * width + (h + 1) * HDIM] for s in range(3))
        scores = dot_nt(query, key) + bias[h]
        top = jnp.max(scores, axis=-1, keepdims=True)
        exps = jnp.exp(scores - top)
        total = jnp.sum(exps, axis=-1, keepdims=True)
        low = (exps * (1.0 / total)).astype(bf16)
        prob[h] = low
        mixed[:, cols] = dot_nn(low, value).astype(bf16)
    out_cols = weights[:, 3 * width :]
    for half, at, rows in half_rows():
        halves[2 * half + at][...] = dot_nt(mixed[rows, :], out_cols).astype(bf16)


def ffn_kernel(n_blocks, x, gains, dy, own_a, own_b, other_a, other_b, *rest):
    blocks = rest[:n_blocks]
    resid, act, hidden, pre_grad, keep, send, down, weights, hidden_grad = rest[n_blocks:]
    assemble(down, blocks)
    assemble(weights, blocks, down.shape[1])
    hidden_grad[...] = dot_nn(dy[...], down[...])
    for half, at, rows in half_rows():
        here = slice(at * BLK, (at + 1) * BLK)
        attn = ((own_a, own_b), (other_a, other_b))[half][at]
        values = x[rows, :].astype(f32) + attn[...].astype(f32)
        resid[rows, :] = values
        scale = lax.rsqrt(jnp.mean(values * values, axis=-1, keepdims=True) + eps_norm)
        low = (values * scale * gains[1:2, :]).astype(bf16)
        act[rows, :] = low
        u = dot_nn(low, weights[...])
        square = u * u
        tanh_part = jnp.tanh(root_coef * (u + gelu_coef * square * u))
        hidden[rows, :] = (0.5 * u * (1.0 + tanh_part)).astype(bf16)
        inner = root_coef * (1.0 + 3.0 * gelu_coef * square)
        slope = 0.5 * (1.0 + tanh_part) + 0.5 * u * (1.0 - tanh_part * tanh_part) * inner
        du = (hidden_grad[rows, :] * slope).astype(bf16)
        pre_grad[rows, :] = du
        (send if half else keep)[here, :] = dot_nt(du, weights[...]).astype(bf16)


def row_products(weights, grad):
    products = weights.astype(f32) * grad
    width = grad.shape[1]
    folded = sum(products[:, c : c + BLK] for c in range(0, width - BLK + 1, BLK))
    if width % BLK:
        rest = products[:, width - width % BLK :]
        wide = jnp.zeros((grad.shape[0], BLK - width % BLK), f32)
        folded = folded + jnp.concatenate([rest, wide], axis=1)
    return jnp.sum(folded.T, axis=0, keepdims=True)


def down_grad_kernel(order, left, right, *rest):
    outs, grad = rest[:-1], rest[-1]
    grad[...] = dot_tn(left[...], right[...])
    spread(grad, outs, order)


def in_grad_kernel(order, left, right, weights, gains, *rest):
    *outs, gain_part, grad = rest
    grad[...] = dot_tn(left[...], right[...])
    spread(grad, outs, order)
    gain_part[...] = row_products(weights[...], grad[...]) / gains[1:2, :]


def turn_kernel(prob, out):
    for h in range(prob.shape[0]):
        out[h] = prob[h].T


def attend_back_kernel(
    n_outs, resid, dy, gains, own, other, weights, qkv, prob, prob_t, mixed, act_t, bucket, gain_two, *rest
):
    outs = rest[:n_outs]
    share_grad, small, proj_grad, resid_low, grad, diag = rest[n_outs:]
    chip = lax.axis_index("tp") >> 1
    width = qkv.shape[1] // 3
    for half, at, rows in half_rows():
        here = slice(at * BLK, (at + 1) * BLK)
        act_grad = (other if half else own)[here, :].astype(f32)
        values = resid[rows, :]
        scale = lax.rsqrt(jnp.mean(values * values, axis=-1, keepdims=True) + eps_norm)
        normed = values * scale
        normal_grad = act_grad * gains[1:2, :]
        mean_part = jnp.mean(normal_grad * normed, axis=-1, keepdims=True)
        total = dy[rows, :].astype(f32) + scale * (normal_grad - normed * mean_part)
        resid_low[rows, :] = total.astype(bf16)
        if half == 0:

            @pl.when(chip == at)
            def _():
                share_grad[...] = total

    mix_grad = dot_nn(resid_low[...], weights[:, 3 * width :]).astype(bf16)
    heads = prob.shape[0]
    row = lax.broadcasted_iota(jnp.int32, (BLK, BLK), 0)
    col = lax.broadcasted_iota(jnp.int32, (BLK, BLK), 1)
    flip = (row + col == BLK - 1).astype(f32).astype(bf16)
    diag[...] = jnp.zeros_like(diag)
    for h in range(heads):
        query, key, value = (qkv[:, s * width + h * HDIM : s * width + (h + 1) * HDIM] for s in range(3))
        grad_rows = mix_grad[:, h * HDIM : (h + 1) * HDIM]
        prob_grad = dot_nt(grad_rows, value)
        prob_here = prob[h].astype(f32)
        row_dot = jnp.sum(prob_here * prob_grad, axis=-1, keepdims=True)
        low = (prob_here * (prob_grad - row_dot)).astype(bf16)
        for r in range(LEN // BLK):
            flipped = dot_nn(flip, low[r * BLK : (r + 1) * BLK, :])
            wide = jnp.concatenate([flipped, jnp.zeros((BLK, BLK), f32)], axis=1)
            turned = pltpu.roll(wide, 0, 1, stride=1, stride_axis=0)
            low_at = LEN - BLK - r * BLK
            diag[h : h + 1, low_at : low_at + WIN] += jnp.sum(turned, axis=0, keepdims=True)
        for s, part in enumerate((dot_nn(low, key), dot_tn(low, query), dot_nn(prob_t[h], grad_rows))):
            proj_grad[:, s * width + h * HDIM : s * width + (h + 1) * HDIM] = part.astype(bf16)
    grad[:, : 3 * width] = dot_nn(act_t[...], proj_grad[...])
    grad[:, 3 * width :] = dot_tn(resid_low[...], mixed[...])
    onehot = (lax.broadcasted_iota(jnp.int32, (BUCKETS, 2 * LEN), 0) == bucket[...]).astype(f32)
    by_bucket = lax.dot_general(
        diag[...],
        onehot,
        (((1,), (1,)), ((), ())),
        precision=lax.Precision.HIGHEST,
        preferred_element_type=f32,
    )
    first = lax.axis_index("tp") * heads
    cells = [
        sum(jnp.where(first + h == head, by_bucket[h : h + 1, :], 0.0) for h in range(heads))
        for head in range(HEADS)
    ]
    model = gains.shape[1]
    cells.append(jnp.zeros((1, model - HEADS * BUCKETS), f32))
    gain_one = row_products(weights[:, : 3 * width], grad[:, : 3 * width]) / gains[0:1, :]
    lines = (gain_one, gain_two[...], jnp.concatenate(cells, axis=1), jnp.zeros((SMALL - 3, model), f32))
    whole = jnp.concatenate(lines, axis=0)
    if n_outs == 1:
        spread(grad, outs)
        small[...] = whole
        return
    keep, low = outs
    rows = keep.shape[1]
    spread(grad, (keep, small, low))
    small[2 * rows :, :] = whole.astype(bf16)


def ffn_out_kernel(hidden, down, keep, *send):
    for half, at, rows in half_rows():
        block = dot_nt(hidden[rows, :], down[...]).astype(bf16)
        if half:
            send[at][...] = block
        else:
            keep[at * BLK : (at + 1) * BLK, :] = block


def act_grad_kernel(proj_grad, weights, keep, *send):
    width = proj_grad.shape[1]
    for half, at, rows in half_rows():
        block = dot_nt(proj_grad[rows, :], weights[:, :width]).astype(bf16)
        if half:
            send[at][...] = block
        else:
            keep[at * BLK : (at + 1) * BLK, :] = block


def core_add_kernel(*refs):
    *before, keep, got_a, got_b, mine, theirs = refs
    chip = lax.axis_index("tp") >> 1
    first = mine.shape[0] - BLK
    for to, block in zip((mine, theirs), before):
        to[:BLK, :] = block[...]
    for at, got in enumerate((got_a, got_b)):
        here = slice(at * BLK, (at + 1) * BLK)
        value = (keep[here, :].astype(f32) + got[...].astype(f32)).astype(bf16)

        @pl.when(chip == at)
        def _():
            mine[first:, :] = value

        @pl.when(chip != at)
        def _():
            theirs[first:, :] = value


def share_out_kernel(resid, x, gains, share_grad, mine, got, block_out, input_grad):
    share = pl.ds(pl.multiple_of(lax.axis_index("tp") * BLK, BLK), BLK)
    first, second = slice(0, BLK), slice(BLK, 2 * BLK)
    ffn = mine[first, :].astype(f32) + got[first, :].astype(f32)
    block_out[...] = (resid[share, :] + ffn).astype(bf16)
    values = x[share, :].astype(f32)
    scale = lax.rsqrt(jnp.mean(values * values, axis=-1, keepdims=True) + eps_norm)
    normed = values * scale
    normal_grad = (mine[second, :].astype(f32) + got[second, :].astype(f32)) * gains[0:1, :]
    mean_part = jnp.mean(normal_grad * normed, axis=-1, keepdims=True)
    input_grad[...] = share_grad[...] + scale * (normal_grad - normed * mean_part)


def add_kernel(one, two, out):
    out[...] = (one[...].astype(f32) + two[...].astype(f32)).astype(bf16)


def pair_add_kernel(keep, got, mine, theirs):
    for k in range(4):
        to = theirs if k >= 2 else mine
        to[k % 2] = (keep[k].astype(f32) + got[k].astype(f32)).astype(bf16)


def high_add_kernel(keep, got, theirs):
    for k in range(2):
        theirs[k] = (keep[k + 2].astype(f32) + got[k].astype(f32)).astype(bf16)


def late_add_kernel(keep, got_low, got, mine, theirs):
    for k, to in enumerate((mine, theirs)):
        to[...] = (keep[k].astype(f32) + got_low[k].astype(f32) + got[k].astype(f32)).astype(bf16)


def next_add_kernel(keep, got, mine, theirs):
    for k, to in enumerate((mine, theirs)):
        to[...] = (keep[k].astype(f32) + got[k].astype(f32)).astype(bf16)


def last_high_kernel(keep, sent, got, out):
    rows = keep.shape[1]
    for k in range(2):
        here = slice(k * rows, (k + 1) * rows)
        out[here, :] = (keep[k + 2].astype(f32) + got[here, :].astype(f32)).astype(bf16)
    small = slice(2 * rows, None)
    out[small, :] = (sent[small, :].astype(f32) + got[small, :].astype(f32)).astype(bf16)


def last_late_kernel(keep, got_low, sent, got, mine, out):
    rows = keep.shape[1]
    first, second, small = slice(0, rows), slice(rows, 2 * rows), slice(2 * rows, None)
    mine[...] = keep[0].astype(f32) + got_low[0].astype(f32) + got[first, :].astype(f32)
    block = keep[1].astype(f32) + got_low[1].astype(f32) + got[second, :].astype(f32)
    out[:rows, :] = block.astype(bf16)
    out[rows:, :] = (sent[small, :].astype(f32) + got[small, :].astype(f32)).astype(bf16)


def fold(values):
    rows, cols = values.shape
    squares = values * values
    lanes = sum(squares[:, c : c + BLK] for c in range(0, cols, BLK))
    return jnp.sum(lanes, axis=0, keepdims=True)


def sum_kernel(n_parts, *rest):
    parts, (grad, squares) = rest[:n_parts], rest[n_parts:]
    total = sum(part[...].astype(f32) for part in parts)
    grad[...] = total
    squares[...] = fold(total)


def last_sum_kernel(direct, extra_a, extra_b, *rest):
    *parts, grad, out, payload, lines, sem = rest
    if direct:
        mine, sent, got = parts
        rows = mine.shape[0]
        total = mine[...] + got[:rows, :].astype(f32)
        small = sent[rows:, :].astype(f32) + got[rows:, :].astype(f32)
    else:
        total, small = (part[...] for part in parts)
    grad[...] = total
    per_row = total.shape[1] // BLK
    lines[...] = jnp.zeros_like(lines)
    for line in range(LINES):
        row, at = divmod(line, per_row)
        lines[line : line + 1, :] = small[row : row + 1, at * BLK : (at + 1) * BLK]
    me = lax.axis_index("dp")
    start = pl.multiple_of(jnp.minimum(2 * me, LINES), 2)
    squares = fold(total) + extra_a[...] + extra_b[...]
    two = lines[pl.ds(start, 2), :]
    told = jnp.concatenate((squares, two[0:1, :], two[1:2, :]), axis=1)
    payload[...] = jnp.broadcast_to(told[None], payload.shape)
    to_hbm(payload, out, sem)


def adamw(weight, gradient, moment_one, moment_two, rate):
    one_new = beta_one * moment_one + (1.0 - beta_one) * gradient
    two_new = beta_two * moment_two + (1.0 - beta_two) * gradient * gradient
    root = math.sqrt(1.0 - beta_two**adam_step)
    scale = rate * root / (1.0 - beta_one**adam_step)
    step = scale * one_new / (jnp.sqrt(two_new) + adam_eps * root)
    return (weight * (1.0 - rate * decay_rate) - step, one_new, two_new)


def fetch_kernel(*refs):
    count = len(refs) // 2
    copies = [pltpu.make_async_copy(refs[i], refs[count + i], refs[-1].at[i]) for i in range(count)]
    for copy in copies:
        copy.start()
    for copy in copies:
        copy.wait()


def adam_kernel(*refs):
    told, grad_qkvo, grad_in, grad_down, *state = refs[:22]
    norm_ref, *matrices, gains_a, gains_b, gains_c, gains_grad, table_a, table_b, table_c = refs[22:46]
    gains_sum, table_grad = refs[46:]
    gains_o, table_o = (gains_a, gains_b, gains_c), (table_a, table_b, table_c)
    qkv, out, ffn_in, ffn_down, gains, table = (state[i : i + 3] for i in range(0, 18, 3))
    qkv_o, out_o, in_o, down_o = (matrices[i : i + 4] for i in range(0, 16, 4))
    tp = lax.axis_size("tp")
    squares = told[0, :, :BLK]
    for i in range(1, told.shape[0]):
        squares = squares + told[i, :, :BLK]
    model = gains_sum.shape[1]
    per_row = model // BLK
    per_line = BLK // BUCKETS
    first = lax.axis_index("tp") * table_grad.shape[0]
    for line in range(2 * per_row + HEADS // per_line):
        index, at = divmod(line, 2)
        cols = slice((at + 1) * BLK, (at + 2) * BLK)
        value = told[index * tp, :, cols]
        for i in range(1, tp):
            value = value + told[index * tp + i, :, cols]
        squares = squares + value * value
        row, at = divmod(line, per_row)
        if row < 2:
            gains_sum[row : row + 1, at * BLK : (at + 1) * BLK] = value
            continue
        for i in range(per_line):
            head = at * per_line + i
            cell = value[:, i * BUCKETS : (i + 1) * BUCKETS]
            for h in range(table_grad.shape[0]):

                @pl.when(first + h == head)
                def _():
                    table_grad[h : h + 1, :] = cell

    norm = jnp.sqrt(jnp.sum(squares, axis=1, keepdims=True))
    norm_ref[...] = norm
    factor = clip_norm / jnp.maximum(norm, clip_norm)

    def update(state_refs, gradient, to, rate, at=...):
        new = adamw(state_refs[0][at], gradient * factor, state_refs[1][at], state_refs[2][at], rate)
        for ref, value in zip(to, new):
            ref[at] = value
        if len(to) == 4:
            to[3][at] = new[0].astype(bf16)

    update(ffn_in, grad_in[...], in_o, rate_small)
    update(ffn_down, grad_down[...], down_o, rate_small)
    width = qkv[0].shape[2]
    for part in range(3):
        update(qkv, grad_qkvo[:, part * width : (part + 1) * width], qkv_o, rate_small, part)
    update(out, grad_qkvo[:, 3 * width :], out_o, rate_large)
    update(gains, gains_sum[...], gains_o, rate_large)
    gains_grad[...] = gains_sum[...] * factor
    update(table, table_grad[...], table_o, rate_large)


def on_device(
    dp,
    inputs,
    cotangent,
    seg_lengths,
    bucket_ids,
    qkv_weight,
    qkv_first,
    qkv_second,
    out_weight,
    out_first,
    out_second,
    ffn_in_weight,
    ffn_in_first,
    ffn_in_second,
    ffn_down_weight,
    ffn_down_first,
    ffn_down_second,
    norm_gains,
    gains_first,
    gains_second,
    bias_table,
    table_first,
    table_second,
):
    tokens, model = inputs.shape
    rows, local = out_weight.shape
    hidden = ffn_in_weight.shape[1]
    heads_here = local // HDIM
    tp = lax.axis_size("tp")
    packed_cols = 4 * local
    direct = dp == 8

    def swap_dp(value, distance):
        return lax.ppermute(value, "dp", [(i, i ^ distance) for i in range(dp)])

    def swap_tp(value, distance):
        return lax.ppermute(value, "tp", [(i, i ^ distance) for i in range(tp)])

    def add(one, two, behind=()):
        (out,) = call(add_kernel, [sds(one.shape, bf16)], (one, two), "add", limit=4, behind=behind)
        return out

    def pair_add(keep, got, behind):
        outs = [sds((2, *keep.shape[1:]), bf16)] * 2
        return call(pair_add_kernel, outs, (keep, got), "pair_add", limit=4, behind=behind)

    def high_add(keep, got, behind):
        outs = [sds((2, *keep.shape[1:]), bf16)]
        (out,) = call(high_add_kernel, outs, (keep, got), "high_add", limit=4, behind=behind)
        return out

    def late_add(keep, got_low, got, behind):
        outs = [sds(keep.shape[1:], bf16)] * 2
        return call(late_add_kernel, outs, (keep, got_low, got), "late_add", limit=4, behind=behind)

    def next_add(keep, got, behind):
        outs = [sds(keep.shape[1:], bf16)] * 2
        return call(next_add_kernel, outs, (keep, got), "next_add", limit=4, behind=behind)

    half_shape = [sds((tokens // 2, model), bf16)] * 2
    matrices = (qkv_weight, out_weight, ffn_down_weight, ffn_in_weight)
    packed, packed_ffn = call(
        pack_kernel,
        [sds((rows, packed_cols), bf16), sds((rows, 2 * hidden), bf16)],
        matrices,
        "pack",
        hbm=(0, 1, 2, 3),
        scratch=[*(pltpu.VMEM(m.shape, f32) for m in matrices), pltpu.SemaphoreType.DMA((4,))],
    )
    ids = bucket_ids[None, :]
    act_one, act_one_t, bias, bucket_row, inputs, norm_gains_here, cotangent = call(
        prep_kernel,
        [
            sds((tokens, model), bf16),
            sds((model, tokens), bf16),
            sds((heads_here, LEN, LEN), f32),
            sds((1, 2 * LEN), jnp.int32),
            sds(inputs.shape, bf16),
            sds(norm_gains.shape, f32),
            sds(inputs.shape, bf16),
        ],
        (seg_lengths, bias_table.T, ids, inputs, norm_gains, cotangent),
        "prep",
        hbm=range(6),
        scratch=[
            pltpu.SMEM(seg_lengths.shape, jnp.int32),
            pltpu.SMEM((heads_here, BUCKETS), f32),
            pltpu.VMEM(ids.shape, jnp.int32),
            pltpu.SemaphoreType.DMA((6,)),
        ],
    )
    if direct:
        one, two = swap_dp(packed, 2), swap_dp(packed, 4)
        own, ffn_own = swap_dp(after(packed, act_one), 1), swap_dp(after(packed_ffn, act_one), 1)
        one_across = swap_dp(one, 1)
        three = swap_dp(two, 2)
        ffn_two = swap_dp(after(packed_ffn, two), 4)
        two_across = swap_dp(two, 1)
        ffn_one = swap_dp(after(packed_ffn, two, own), 2)
        three_across = swap_dp(three, 1)
        qkvo_blocks = [packed, own, one, one_across, two, two_across, three, three_across]
        ffn_three = swap_dp(after(ffn_two, ffn_one), 2)
        ffn_blocks = [packed_ffn, ffn_own, ffn_one, swap_dp(after(ffn_own, ffn_one), 2)]
        for block in (ffn_two, ffn_three):
            ffn_blocks += [block, swap_dp(block, 1)]
        bias = after(bias, ffn_own, one_across)
        ffn_first, ffn_early = (ffn_two,), (ffn_blocks[5], ffn_three)
    else:
        qkvo_blocks = [lax.all_gather(packed, "dp", axis=0, tiled=True)]
        ffn_first = ffn_blocks = ffn_early = [lax.all_gather(packed_ffn, "dp", axis=0, tiled=True)]
    n_blocks = len(qkvo_blocks)

    weights_one, qkv, prob, mixed, *attn_parts = call(
        functools.partial(attend_kernel, n_blocks),
        [
            sds((model, packed_cols), bf16),
            sds((tokens, 3 * local), bf16),
            sds((heads_here, LEN, LEN), bf16),
            sds((tokens, local), bf16),
            *[sds((BLK, model), bf16)] * 4,
        ],
        (act_one, bias, *qkvo_blocks),
        "attend",
    )
    half_blocks = [sds((BLK, model), bf16)] * 2
    attn_got = [swap_tp(after(part, *ffn_first), 1) for part in attn_parts[2:]]
    attn_first = [add(part, got) for part, got in zip(attn_parts, attn_got)]
    attn_own = [add(first, swap_tp(first, 2), ffn_early) for first in attn_first]
    attn_sums = (*attn_own, *(swap_tp(own, 1) for own in attn_own))
    resid, act_two, hidden_act, pre_grad, back_keep, back_send, down_full, in_full = call(
        functools.partial(ffn_kernel, n_blocks),
        [
            sds((tokens, model), f32),
            sds((tokens, model), bf16),
            sds((tokens, hidden), bf16),
            sds((tokens, hidden), bf16),
            *half_shape,
            *[sds((model, hidden), bf16)] * 2,
        ],
        (inputs, norm_gains_here, cotangent, *attn_sums, *ffn_blocks),
        "ffn",
        scratch=[pltpu.VMEM((tokens, hidden), f32)],
    )
    down_order, in_order = (2, 4, 1), (1, 2, 4)
    grad_scratch = [pltpu.VMEM((model, hidden), f32)]
    down_parts = call(
        functools.partial(down_grad_kernel, down_order),
        spread_shapes(dp, model, hidden, (4, 2, 2)),
        (cotangent, hidden_act),
        "down_grad",
        scratch=grad_scratch,
    )
    back_first = add(back_keep, swap_tp(back_send, 1), down_parts[:1])
    back_got = swap_tp(back_first, 2)
    *in_parts, gain_two_part = call(
        functools.partial(in_grad_kernel, in_order),
        [*spread_shapes(dp, model, hidden, (4, 4)), sds((1, model), f32)],
        (act_two, after(pre_grad, back_first), in_full, norm_gains_here),
        "in_grad",
        scratch=grad_scratch,
    )
    share_shapes = [half_shape[0], *half_blocks]
    ffn_keep, *ffn_send = call(
        ffn_out_kernel, share_shapes, (hidden_act, down_full), "ffn_out", behind=(gain_two_part,)
    )
    ffn_got = [swap_tp(part, 1) for part in ffn_send]
    ffn_sums = call(core_add_kernel, half_blocks, (ffn_keep, *ffn_got), "ffn_add", limit=4)
    attend_behind = ()
    back_behind = ffn_sums[:1]
    if direct:
        down_keep, down_high, down_low = down_parts
        down_got = swap_dp(down_high, down_order[0])
        back_behind = (*back_behind, down_got)
    (prob_t,) = call(turn_kernel, [sds(prob.shape, bf16)], (prob,), "turn", behind=ffn_sums[:1])
    back_sum = add(back_first, back_got, (*back_behind, prob_t))
    if direct:
        down_one = high_add(down_keep, down_got, (back_sum,))
        attend_behind = (down_one,)
    everyone = dp * tp
    qkvo_shapes = spread_shapes(dp, model, packed_cols, (4, 2))
    small_shape = sds((2 * rows + SMALL, model), bf16) if direct else sds((SMALL, model), f32)
    *qkvo_parts, share_grad, small, proj_grad = call(
        functools.partial(attend_back_kernel, len(qkvo_shapes)),
        [*qkvo_shapes, sds((BLK, model), f32), small_shape, sds((tokens, 3 * local), bf16)],
        (
            resid,
            cotangent,
            norm_gains_here,
            back_sum,
            swap_tp(back_sum, 1),
            weights_one,
            qkv,
            prob,
            prob_t,
            mixed,
            act_one_t,
            bucket_row,
            gain_two_part,
        ),
        "attend_back",
        scratch=[
            pltpu.VMEM((tokens, model), bf16),
            pltpu.VMEM((model, packed_cols), f32),
            pltpu.VMEM((8, 2 * LEN), f32),
        ],
        behind=attend_behind,
    )
    def summed(parts, behind):
        return call(
            functools.partial(sum_kernel, len(parts)),
            [sds((rows, parts[0].shape[1]), f32), sds((1, BLK), f32)],
            parts,
            "sum_parts",
            limit=4,
            behind=behind,
        )

    def act_shares(behind):
        keep, *send = call(
            act_grad_kernel, share_shapes, (proj_grad, weights_one), "act_grad", behind=behind
        )
        return (keep, *(swap_tp(part, 1) for part in send))

    def share_sums(shares, behind):
        outs = [sds((2 * BLK, model), bf16)] * 2
        return call(core_add_kernel, outs, (*ffn_sums, *shares), "core_add", limit=4, behind=behind)

    if direct:
        keep, send_low = qkvo_parts
        in_keep, in_send = in_parts
        in_one = pair_add(in_keep, swap_dp(in_send, in_order[0]), (proj_grad,))
        got_high = swap_dp(small, 1)
        act_parts = act_shares(in_one)
        down_rest = (swap_dp(down_low, down_order[0]), swap_dp(down_one, down_order[1]))
        down_two = late_add(down_keep, *down_rest, act_parts[:1])
        (high,) = call(
            last_high_kernel, [small_shape], (keep, small, got_high), "last_high", limit=4, behind=down_two
        )
        got_low = swap_dp(after(send_low, high), 1)
        down_grad, down_squares = summed((down_two[0], swap_dp(down_two[1], down_order[2])), (high,))
        in_two = next_add(in_one[0], swap_dp(in_one[1], in_order[1]), (down_grad,))
        mine, theirs = share_sums(act_parts, in_two)
        in_grad, in_squares = summed((in_two[0], swap_dp(in_two[1], in_order[2])), (mine,))
        last, late = call(
            last_late_kernel,
            [sds((rows, packed_cols), f32), sds((rows + SMALL, packed_cols), bf16)],
            (keep, got_low, high, swap_dp(high, 2)),
            "last_late",
            limit=4,
            behind=(in_grad,),
        )
        last_parts = (last, late, swap_dp(late, 4))
        share_behind = (late,)
    else:
        qkvo_sums, down_sums, in_sums = (
            (lax.psum_scatter(p[0].astype(f32), "dp", scatter_dimension=0, tiled=True),)
            for p in (qkvo_parts, down_parts, in_parts)
        )
        last_parts = (*qkvo_sums, lax.psum(small, "dp"))
        down_grad, down_squares = summed(down_sums, ())
        in_grad, in_squares = summed(in_sums, ())
        mine, theirs = share_sums(act_shares(()), ())
        share_behind = ()
    block_out, input_grad = call(
        share_out_kernel,
        [sds((BLK, model), bf16), sds((BLK, model), f32)],
        (resid, inputs, norm_gains_here, share_grad, mine, swap_tp(theirs, 2)),
        "share_out",
        behind=share_behind,
    )
    matrices = (
        qkv_weight,
        qkv_first,
        qkv_second,
        out_weight,
        out_first,
        out_second,
        ffn_in_weight,
        ffn_in_first,
        ffn_in_second,
        ffn_down_weight,
        ffn_down_first,
        ffn_down_second,
    )
    vectors = (norm_gains, gains_first, gains_second, bias_table.T, table_first.T, table_second.T)
    state = matrices + vectors
    fetched = call(
        fetch_kernel,
        [sds(m.shape, f32) for m in state],
        state,
        "fetch",
        hbm=range(18),
        scratch=[pltpu.SemaphoreType.DMA((18,))],
        limit=4,
        behind=(block_out,),
    )
    qkvo_grad, payload = call(
        functools.partial(last_sum_kernel, direct),
        [sds((rows, packed_cols), f32), pltpu.HBM((everyone, 1, 3 * BLK), f32)],
        (down_squares, in_squares, *last_parts),
        "last_sum",
        scratch=[
            pltpu.VMEM((everyone, 1, 3 * BLK), f32),
            pltpu.VMEM((LINES + 8, BLK), f32),
            pltpu.SemaphoreType.DMA,
        ],
        behind=(fetched[0],),
    )
    told = lax.all_to_all(payload, ("dp", "tp"), 0, 0)
    shapes = [(m.shape, kind) for m in matrices[::3] for kind in (f32, f32, f32, bf16)]
    norm, *updated = call(
        adam_kernel,
        [
            sds((1, 1), f32),
            *(sds(shape, kind) for shape, kind in shapes),
            *[sds(norm_gains.shape, f32)] * 4,
            *[sds((heads_here, BUCKETS), f32)] * 3,
        ],
        (told, qkvo_grad, in_grad, down_grad, *fetched),
        "adam",
        scratch=[pltpu.VMEM(norm_gains.shape, f32), pltpu.VMEM((heads_here, BUCKETS), f32)],
    )
    return (block_out, input_grad, norm.reshape(()), *updated[:-3], *(t.T for t in updated[-3:]))


def solution(mesh):
    row = P("dp", None)
    matrix = P("dp", "tp")
    stack = P(None, "dp", "tp")
    table = P(None, "tp")
    share = P(("dp", "tp"), None)
    in_specs = (
        *(row,) * 3,
        P(),
        *(stack,) * 3,
        *(matrix,) * 9,
        *(P(),) * 3,
        *(table,) * 3,
    )
    out_specs = (
        *(share,) * 2,
        P(),
        *(stack,) * 4,
        *(matrix,) * 12,
        *(P(),) * 4,
        *(table,) * 3,
    )
    return jax.shard_map(
        functools.partial(on_device, mesh.shape["dp"]),
        mesh=mesh,
        in_specs=in_specs,
        out_specs=out_specs,
        check_vma=False,
    )
```
